32 devices in a mesh: fsdp: 4 (over x, core), ctx: 2 (over y), tp: 4 (over z).
Axes of the slice: x: 2, y: 2, z: 4, core: 2. Of those that a mesh axis runs over, the one named last changes fastest.
Arguments:
- states: bfloat16 [4, 1024, 2048], P('fsdp', 'ctx'), may hold values from -6 to 6
- teacher: bfloat16 [4, 1024, 2048], P('fsdp', 'ctx'), may hold values from -6 to 6
- lengths: int32 [4], P('fsdp'), may hold values from 513 to 1024, as said below
- routes: int32 [4, 1024, 8], P('fsdp', 'ctx'), may hold values from 0 to 31, all different within a row; in each aligned block of 512 rows (0 to 511, 512 to 1023, ..., all dimensions but the last counted through in order) at most 160 rows name the same one
- gate_weights: float32 [4, 1024, 8], P('fsdp', 'ctx'), may hold values from 0.05 to 0.2
- w_qkv: bfloat16 [2048, 3, 2048], P(('fsdp', 'ctx'), None, 'tp'), may hold values from -0.125 to 0.125
- w_out: bfloat16 [2048, 2048], P('tp', ('fsdp', 'ctx')), may hold values from -3 to 3
- norm_gains: bfloat16 [2, 2048], P(None, ('fsdp', 'ctx')), may hold values from 0.5 to 1.5
- qk_gains: bfloat16 [2, 128], P(None, ('fsdp', 'ctx')), may hold values from 0.099609375 to 1.8984375
- w_gate_up: bfloat16 [32, 2048, 2, 1024], P(('fsdp', 'ctx'), None, None, 'tp'), may hold values from -0.125 to 0.125
- w_down: bfloat16 [32, 1024, 2048], P(('fsdp', 'ctx'), 'tp'), may hold values from -0.75 to 0.75
Outputs:
- activations: bfloat16 [4, 1024, 2048], P('fsdp', 'ctx')
- loss_value: float32 [], replicated
- valid_count: float32 [], replicated
- grad_states: float32 [4, 1024, 2048], P('fsdp', 'ctx')
- grad_qkv: float32 [2048, 3, 2048], P(('fsdp', 'ctx'), None, 'tp')
- grad_out: float32 [2048, 2048], P('tp', ('fsdp', 'ctx'))
- grad_norm_gains: float32 [2, 2048], P(None, ('fsdp', 'ctx'))
- grad_qk_gains: float32 [2, 128], P(None, ('fsdp', 'ctx'))
- grad_gate_up: float32 [32, 2048, 2, 1024], P(('fsdp', 'ctx'), None, None, 'tp')
- grad_down: float32 [32, 1024, 2048], P(('fsdp', 'ctx'), 'tp')
The draws below stay inside these ranges and needn't reach their ends.
Inputs may be any that keep to these rules, and one draw needn't show every extreme that they name: `lengths`: every sequence has at least 513 valid slots, and some sequence has exactly 1024. `routes`: each slot names 8 different experts; among the 512 slots of one sequence on one index of ctx (aligned blocks of the flattened slots) no expert is named more than 160 times, a bound that some block reaches.
All inputs are finite; a program needn't handle non-finite values.
Results may differ from the reference program's by a relative error of at most 0.015.
Values may be sent and summed in bfloat16 or wider, within the bound.
No kernel may reach another device: no remote copies, remote signals or barrier semaphores. Data moves between devices by JAX's collectives and lax.ppermute only.
A program may use at most 320 MiB of HBM per device.

```python
import math
import jax
import jax.numpy as jnp
import numpy as np
from jax import lax

D = 2048
H = 16
DH = 128
FF = 1024
TOP = 8
E = 32
LEN = 1024
HD = 2048
LC = 512
CAP = 160
SEQS = 4
N_CTX = 2


def draw_lengths(key, part):
    key_base, key_pick = jax.random.split(jax.random.fold_in(key, 17))
    values = jax.random.randint(key_base, (SEQS,), LEN - LC + 1, LEN + 1)
    chosen = jax.random.randint(key_pick, (), 0, SEQS)
    return jnp.where(jnp.arange(SEQS) == chosen, LEN, values).astype(jnp.int32)


def steps_of(key, dims, cuts, least, largest):
    gain = 1.0
    for dim, parts in cuts:
        steps = jax.random.uniform(jax.random.fold_in(jax.random.fold_in(key, 6), dim), (parts,), jnp.float32, least / len(cuts), largest / len(cuts))
        gain = gain * jnp.repeat(jnp.exp(steps), dims[dim] // parts).reshape((-1,) + (1,) * (len(dims) - 1 - dim))
    return gain


def assign_block(rng, own, number, rows, number_of, top, bound, lean):
    sequence = jax.random.permutation(rng, number_of)
    heavy_load, common = load_shares(number_of, rows * top, bound, lean, True), load_shares(number_of, rows * top, bound, lean, False)
    places = jnp.arange(number_of)

    def named(sizes, offset_by):
        used = int((sizes > 0).sum())
        fixed = max(1, used // 4)
        moved = fixed + (places - fixed + offset_by * (used - fixed)) % max(1, number_of - fixed)
        return jnp.zeros((number_of,), jnp.int32).at[sequence[jnp.where(places < fixed, places, moved)]].set(jnp.asarray(sizes, jnp.int32))

    sizes = jnp.where(number % 4 == 0, named(heavy_load, number // 4), named(common, number - number // 4 - 1))
    mixed = jax.random.permutation(jax.random.fold_in(own, 3), number_of)
    source_of, sink = mixed[0:number_of // 2 * 2:2], mixed[1:number_of // 2 * 2:2]
    slack = jnp.minimum(sizes[source_of] - 1, bound - sizes[sink]) // 2
    slack = jnp.where((source_of == sequence[0]) | (sink == sequence[0]) | (sizes[sink] == 0), 0, jnp.maximum(slack, 0))
    moved = jax.random.randint(jax.random.fold_in(own, 4), (number_of // 2,), 0, 1 << 20) % (slack + 1)
    sizes = sizes.at[source_of].add(-moved).at[sink].add(moved)
    labels = jnp.searchsorted(jnp.cumsum(sizes), jnp.arange(rows * top), side="right").astype(jnp.int32)
    table = labels.reshape(top, rows).T
    table = table[jax.random.permutation(jax.random.fold_in(own, 1), rows)]
    offset_by = jax.random.randint(jax.random.fold_in(own, 2), (rows, 1), 0, top)
    return jnp.take_along_axis(table, (jnp.arange(top)[None, :] + offset_by) % top, axis=1)


def load_shares(count, total, most, slope, full):
    portions = [(1 << 20) // math.isqrt(rank ** slope) + 1 for rank in range(1, count + 1)]
    largest = most if full else min(most, max(-(-total // count), total * portions[0] // sum(portions)))
    least = 1 if total - largest >= count - 1 else 0
    counts, surplus = [largest] + [least] * (count - 1), total - largest - least * (count - 1)
    while surplus > 0:
        movable = [i for i in range(1, count) if counts[i] < largest] or [i for i in range(1, count) if counts[i] < most]
        whole, left = sum([portions[i] for i in movable]), surplus
        for i in movable:
            more = min(most - counts[i], max(1, left * portions[i] // whole), surplus)
            counts[i] = counts[i] + more
            surplus = surplus - more
    return np.array(counts)


def centred(key, extent, spread, most, shards=(), kind=jnp.bfloat16):
    drawn = jax.random.normal(key, extent, jnp.float32) * spread
    if len(shards) > 0:
        drawn = steps_of(key, extent, shards, -0.22, 0.18) * drawn
    return jnp.clip(drawn, min=-most, max=most).astype(kind)


def setup_inputs(seed: int = 0) -> dict:
    keys = jax.random.split(jax.random.key(seed), 12)
    states = centred(keys[0], (SEQS, LEN, D), 1.0, 6.0, ((0, 4), (1, 2)))
    teacher = centred(keys[1], (SEQS, LEN, D), 1.0, 6.0, ((0, 4), (1, 2)))
    lengths = draw_lengths(jax.random.fold_in(keys[11], 71), 0)
    routes_keys = jax.random.split(jax.random.fold_in(keys[3], 1), SEQS * LEN // LC)
    routes_turns = jax.random.permutation(jax.random.fold_in(keys[3], 3), SEQS * LEN // LC)
    routes = jax.vmap(lambda own, number: assign_block(jax.random.fold_in(keys[3], 2), own, number, LC, E, TOP, CAP, 1))(routes_keys, routes_turns).reshape((SEQS, LEN, TOP))
    gate_weights = jnp.clip(0.05 + 0.15 * jax.random.uniform(keys[4], (SEQS, LEN, TOP), jnp.float32) ** steps_of(keys[4], (SEQS, LEN, TOP), ((0, 4), (1, 2)), -0.2, 0.2), 0.05, 0.2)
    w_qkv = centred(keys[5], (D, 3, HD), D ** -0.5, 0.125, ((0, 8), (2, 4)))
    w_out = centred(keys[6], (HD, D), (max(1, 2 * HD // LEN)) ** -0.5, 3.0, ((0, 4), (1, 8)))
    norm_gains = jnp.clip(1.0 + 0.1 * jax.random.normal(keys[7], (2, D), jnp.float32), 0.5, 1.5).astype(jnp.bfloat16)
    qk_gains = jnp.clip(1.0 + 0.18 * jax.random.normal(keys[8], (2, DH), jnp.float32), 0.099609375, 1.8984375).astype(jnp.bfloat16)
    w_gate_up = centred(keys[9], (E, D, 2, FF), D ** -0.5, 0.125, ((0, 8), (3, 4)))
    w_down = centred(keys[10], (E, FF, D), (FF // 16) ** -0.5, 0.75, ((0, 8), (1, 4)))
    return {"states": states, "teacher": teacher, "lengths": lengths, "routes": routes, "gate_weights": gate_weights, "w_qkv": w_qkv, "w_out": w_out, "norm_gains": norm_gains, "qk_gains": qk_gains, "w_gate_up": w_gate_up, "w_down": w_down}


norm_eps = 1e-05
rope_base = 10000.0
loss_scale = 4096.0
masked_score = -1e+30

@jax.custom_vjp
def low(v):
    return lax.optimization_barrier(v.astype(jnp.bfloat16)).astype(jnp.float32)

@jax.custom_vjp
def low_back(v):
    return v

def low_keep(v):
    return (low(v), None)

def low_pass(kept, grad):
    return (grad,)

def back_keep(v):
    return (v, None)

def back_low(kept, grad):
    return (low(grad),)
low.defvjp(low_keep, low_pass)
low_back.defvjp(back_keep, back_low)

def exact_product(form, left, right):
    return jnp.einsum(form, left, right, precision=lax.Precision.HIGHEST)

def rms_norm(values, gain_vec):
    return values * lax.rsqrt(lax.optimization_barrier(jnp.mean(values * values, axis=-1, keepdims=True)) + norm_eps) * gain_vec

def rotate(values, position):
    half_dim = values.shape[-1] // 2
    frequency = rope_base ** (-2.0 * jnp.arange(half_dim, dtype=jnp.float32) / values.shape[-1])
    angles = position.astype(jnp.float32)[:, None] * frequency[None, :]
    cosine = jnp.cos(angles)[:, None, :]
    sine_part = jnp.sin(angles)[:, None, :]
    first_half = values[..., :half_dim]
    second_half = values[..., half_dim:]
    return jnp.concatenate([first_half * cosine - second_half * sine_part, second_half * cosine + first_half * sine_part], axis=-1)

def dispatch(route_rows, gate_rows, capacity, experts):
    flat_routes = route_rows.reshape(-1)
    matches = (flat_routes[:, None] == jnp.arange(experts, dtype=jnp.int32)[None, :]).astype(jnp.int32)
    ranking = lax.optimization_barrier(jnp.sum((jnp.cumsum(matches, axis=0) - 1) * matches, axis=1))
    source = jnp.arange(flat_routes.shape[0], dtype=jnp.int32) // route_rows.shape[-1]
    slot_rows = jnp.zeros((experts, capacity), jnp.int32).at[flat_routes, ranking].set(source)
    slot_gate = jnp.zeros((experts, capacity), jnp.float32).at[flat_routes, ranking].set(gate_rows.reshape(-1))
    return (slot_rows, slot_gate)

def experts_apply(normed_rows, route_rows, gate_rows, w_gate_up, w_down):
    slot_rows, slot_gate = dispatch(route_rows, gate_rows, CAP, E)
    expert_in = normed_rows[slot_rows]
    gate_up = low_back(exact_product('ecd,edkf->eckf', expert_in, w_gate_up))
    hidden = low(jax.nn.silu(gate_up[:, :, 0]) * gate_up[:, :, 1])
    expert_out = low_back(exact_product('ecf,efd->ecd', hidden, w_down))
    weighted = (expert_out * slot_gate[:, :, None]).reshape(-1, normed_rows.shape[-1])
    return jnp.zeros_like(normed_rows).at[slot_rows.reshape(-1)].add(weighted)

def block_layer(states, teacher, length, route_rows, gate_rows, weights):
    w_qkv, w_out, norm_gains, qk_gains, w_gate_up, w_down = weights
    position = jnp.arange(LEN, dtype=jnp.int32)
    normed = low(rms_norm(states, norm_gains[0]))
    projected = low_back(exact_product('nd,dkh->nkh', normed, w_qkv)).reshape(LEN, 3, H, DH)
    queries = low(rotate(rms_norm(projected[:, 0], qk_gains[0]), position))
    key_states = low(rotate(rms_norm(projected[:, 1], qk_gains[1]), position))
    values = low(projected[:, 2])
    key_valid = position < length
    query_rows = min(512, LEN)

    def attend(query_block):
        scores = low_back(exact_product('qhd,khd->hqk', query_block, key_states) * DH ** (-0.5))
        scores = jnp.where(key_valid[None, None, :], scores, masked_score)
        peak_score = lax.optimization_barrier(jnp.max(scores, axis=-1, keepdims=True))
        exponent = jnp.exp(scores - peak_score)
        probability = low(exponent / lax.optimization_barrier(jnp.sum(exponent, axis=-1, keepdims=True)))
        return exact_product('hqk,khd->qhd', probability, values)
    attended = lax.map(jax.checkpoint(attend), queries.reshape(LEN // query_rows, query_rows, H, DH))
    attended = low(low_back(attended.reshape(LEN, H * DH)))
    branch = low_back(exact_product('nf,fd->nd', attended, w_out))
    middle = states + branch
    normed_ffn = low(rms_norm(middle, norm_gains[1]))
    pieces = []
    for part_index in range(N_CTX):
        rows_here = slice(part_index * LC, (part_index + 1) * LC)
        pieces.append(jax.checkpoint(experts_apply)(normed_ffn[rows_here], route_rows[rows_here], gate_rows[rows_here], w_gate_up, w_down))
    final_state = middle + jnp.concatenate(pieces, axis=0)
    difference = final_state - teacher
    squared = jnp.sum(jnp.where(key_valid[:, None], difference * difference, 0.0))
    return (final_state, squared)

def reference(states, teacher, lengths, routes, gate_weights, w_qkv, w_out, norm_gains, qk_gains, w_gate_up, w_down):
    params = tuple((weight.astype(jnp.float32) for weight in (w_qkv, w_out, norm_gains, qk_gains, w_gate_up, w_down)))
    state_float = states.astype(jnp.float32)
    teacher_float = teacher.astype(jnp.float32)
    valid_count = jnp.sum(lengths).astype(jnp.float32)

    def forward(state_in, *weights):

        def seq_step(running, packed):
            seq_state, seq_teacher, seq_length, seq_routes, seq_gates = packed
            final_state, squared = block_layer(seq_state, seq_teacher, seq_length, seq_routes, seq_gates, weights)
            return (running + squared, final_state)
        summed, finals = lax.scan(jax.checkpoint(seq_step), jnp.zeros((), jnp.float32), (state_in, teacher_float, lengths, routes, gate_weights))
        return (finals, summed * (loss_scale / valid_count))
    (finals, scaled), pullback = jax.vjp(forward, state_float, *params)
    gradients = pullback((jnp.zeros_like(finals), jnp.ones_like(scaled)))
    return (finals.astype(jnp.bfloat16), scaled / loss_scale, valid_count, gradients[0], gradients[1], gradients[2], gradients[3], gradients[4], gradients[5], gradients[6])
```

```python
import jax
import jax.numpy as jnp
from jax import lax
from jax.experimental import pallas as pl
from jax.experimental.pallas import tpu as pltpu
from jax.sharding import PartitionSpec as P

norm_eps = 1e-05
rope_base = 10000.0
loss_scale = 4096.0
masked_score = -1e30
plane = ("fsdp", "ctx")
everywhere = ("fsdp", "ctx", "tp")
low = jnp.bfloat16
wide = jnp.float32


def rms_norm(values, gain_vec):
    return (
        values * lax.rsqrt(jnp.mean(values * values, axis=-1, keepdims=True) + norm_eps) * gain_vec
    )


def norm_back(grad_normed, values, gain_vec):
    inverse = lax.rsqrt(jnp.mean(values * values, axis=-1, keepdims=True) + norm_eps)
    scaled = values * inverse
    grad_scaled = grad_normed * gain_vec
    grad_values = inverse * (
        grad_scaled - scaled * jnp.mean(grad_scaled * scaled, axis=-1, keepdims=True)
    )
    return (grad_values, jnp.sum(grad_normed * scaled, axis=0))


def rotate(values, position):
    half_dim = values.shape[-1] // 2
    frequency = rope_base ** (-2.0 * jnp.arange(half_dim, dtype=wide) / values.shape[-1])
    angles = position.astype(wide)[:, None] * frequency[None, :]
    cosine = jnp.cos(angles)[:, None, :]
    sine_part = jnp.sin(angles)[:, None, :]
    first_half = values[..., :half_dim]
    second_half = values[..., half_dim:]
    return jnp.concatenate(
        [
            first_half * cosine - second_half * sine_part,
            second_half * cosine + first_half * sine_part,
        ],
        axis=-1,
    )


def prepare(projected, qk_float, position):
    queries = rotate(rms_norm(projected[:, 0], qk_float[0]), position)
    key_states = rotate(rms_norm(projected[:, 1], qk_float[1]), position)
    return (queries, key_states, projected[:, 2])


def attend_sequence(query_seq, kv_seq, valid_seq, score_scale):
    scores = (
        jnp.einsum("qhd,khd->hqk", query_seq, kv_seq[:, 0], preferred_element_type=wide)
        * score_scale
    )
    scores = jnp.where(valid_seq[None, None, :], scores, masked_score)
    peak_score = jnp.max(scores, axis=-1, keepdims=True)
    exponent = jnp.exp(scores - peak_score)
    row_total = jnp.sum(exponent, axis=-1, keepdims=True)
    probability = (exponent / row_total).astype(low)
    output = jnp.einsum("hqk,khd->qhd", probability, kv_seq[:, 1], preferred_element_type=wide)
    return (output, (peak_score + jnp.log(row_total))[..., 0])


def back_sequence(query_seq, kv_seq, valid_seq, log_seq, grad_seq, score_scale):
    scores = (
        jnp.einsum("qhd,khd->hqk", query_seq, kv_seq[:, 0], preferred_element_type=wide)
        * score_scale
    )
    scores = jnp.where(valid_seq[None, None, :], scores, masked_score)
    probability = jnp.exp(scores - log_seq[..., None])
    grad_prob = jnp.einsum("qhd,khd->hqk", grad_seq, kv_seq[:, 1], preferred_element_type=wide)
    grad_scores = (
        probability * (grad_prob - jnp.sum(probability * grad_prob, axis=-1, keepdims=True))
    ).astype(low)
    grad_query = (
        jnp.einsum("hqk,khd->qhd", grad_scores, kv_seq[:, 0], preferred_element_type=wide)
        * score_scale
    )
    grad_key = (
        jnp.einsum("hqk,qhd->khd", grad_scores, query_seq, preferred_element_type=wide)
        * score_scale
    )
    grad_value = jnp.einsum(
        "hqk,qhd->khd", probability.astype(low), grad_seq, preferred_element_type=wide
    )
    return (grad_query, jnp.stack([grad_key, grad_value], axis=1))


def route_tables(route_rows, gate_rows, experts):
    slots = route_rows.shape[0]
    hit = route_rows[None, :, :] == jnp.arange(experts, dtype=jnp.int32)[:, None, None]
    named = jnp.sum(hit.astype(wide), axis=-1)
    gates = jnp.sum(jnp.where(hit, gate_rows[None, :, :], 0.0), axis=-1)
    order = jnp.arange(slots, dtype=jnp.int32)
    before = (order[:, None] < order[None, :]).astype(low)
    rank = jnp.dot(named.astype(low), before, preferred_element_type=wide)
    return jnp.stack([jnp.where(named > 0.0, rank, -1.0), gates], axis=1)


def pick_rows(table_ref, block, capacity, slots):
    rank = table_ref[block, 0, 0:1, :].astype(jnp.int32)
    gate = table_ref[block, 0, 1:2, :]
    match = lax.broadcasted_iota(jnp.int32, (capacity, slots), 0) == rank
    chosen = jnp.where(match, 1.0, 0.0).astype(low)
    weight = jnp.sum(jnp.where(match, gate, 0.0), axis=1, keepdims=True)
    return (chosen, weight)


def spread_rows(place_ref, block, experts, capacity, slots):
    column = lax.broadcasted_iota(jnp.int32, (slots, experts * capacity), 1)
    match = column == place_ref[block, :, 0:1]
    for expert in range(1, experts):
        match = match | (column == place_ref[block, :, expert : expert + 1])
    return jnp.where(match, 1.0, 0.0).astype(low)


def nt_dot(left, right):
    return lax.dot_general(left, right, (((1,), (1,)), ((), ())), preferred_element_type=wide)


def tiles_of(width, most=512):
    step = min(width, most)
    return [slice(begin, begin + step) for begin in range(0, width, step)]


def combine_blocks(place_ref, rows_ref, out_ref, blocks, experts, capacity, slots, width):
    for block in range(blocks):
        matrix = spread_rows(place_ref, block, experts, capacity, slots)
        for cut in tiles_of(width):
            out_ref[block * slots : (block + 1) * slots, cut] = jnp.dot(
                matrix, rows_ref[block, :, cut], preferred_element_type=wide
            ).astype(low)


def forward_body(
    x_ref, table_ref, place_ref, up_ref, down_ref, out_ref, rows_ref, gate_up_ref, hidden_ref, y_ref
):
    expert = pl.program_id(1)
    experts = pl.num_programs(1)
    blocks, capacity, width = rows_ref.shape[1:]
    slots = x_ref.shape[0] // blocks
    half = down_ref.shape[1]
    weights = []
    for block in range(blocks):
        chosen, weight = pick_rows(table_ref, block, capacity, slots)
        weights.append(weight)
        for cut in tiles_of(width):
            rows_ref[0, block, :, cut] = jnp.dot(
                chosen,
                x_ref[block * slots : (block + 1) * slots, cut],
                preferred_element_type=wide,
            ).astype(low)
    rows = rows_ref[0].reshape(blocks * capacity, width)
    gate_up = jnp.dot(rows, up_ref[0], preferred_element_type=wide)
    gate_up_ref[0] = gate_up.reshape(blocks, capacity, 2 * half)
    gate_part = gate_up[:, :half]
    up_part = gate_up[:, half:]
    weight = jnp.concatenate(weights, axis=0)
    hidden = (gate_part * jax.nn.sigmoid(gate_part) * up_part * weight).astype(low)
    hidden_ref[0] = hidden.reshape(blocks, capacity, half)
    begin = pl.multiple_of(expert * capacity, 16)
    for cut in tiles_of(width):
        y_ref[:, pl.ds(begin, capacity), cut] = (
            jnp.dot(hidden, down_ref[0, :, cut], preferred_element_type=wide)
            .astype(low)
            .reshape(blocks, capacity, -1)
        )
    total = y_ref.shape[1] // capacity

    @pl.when(expert == experts - 1)
    def _():
        combine_blocks(place_ref, y_ref, out_ref, blocks, total, capacity, slots, width)


def backward_body(
    x_ref, table_ref, place_ref, up_ref, down_ref, gate_up_ref, out_ref, rows_ref, grad_ref, y_ref
):
    expert = pl.program_id(1)
    experts = pl.num_programs(1)
    blocks, capacity, width = rows_ref.shape[1:]
    slots = x_ref.shape[0] // blocks
    half = down_ref.shape[1]
    weights = []
    for block in range(blocks):
        chosen, weight = pick_rows(table_ref, block, capacity, slots)
        weights.append(weight)
        for cut in tiles_of(width):
            rows_ref[0, block, :, cut] = jnp.dot(
                chosen,
                x_ref[block * slots : (block + 1) * slots, cut],
                preferred_element_type=wide,
            ).astype(low)
    rows = rows_ref[0].reshape(blocks * capacity, width)
    weight = jnp.concatenate(weights, axis=0)
    grad_hidden = nt_dot(rows, down_ref[0]) * weight
    gate_up = gate_up_ref[0].reshape(blocks * capacity, 2 * half)
    gate_part = gate_up[:, :half]
    up_part = gate_up[:, half:]
    sigmoid = jax.nn.sigmoid(gate_part)
    grad_gate = grad_hidden * up_part * sigmoid * (1.0 + gate_part * (1.0 - sigmoid))
    grad_up = grad_hidden * gate_part * sigmoid
    grad_rows = jnp.concatenate([grad_gate, grad_up], axis=1).astype(low)
    grad_ref[0] = grad_rows.reshape(blocks, capacity, 2 * half)
    begin = pl.multiple_of(expert * capacity, 16)
    for cut in tiles_of(width):
        y_ref[:, pl.ds(begin, capacity), cut] = (
            nt_dot(grad_rows, up_ref[0, cut, :]).astype(low).reshape(blocks, capacity, -1)
        )
    total = y_ref.shape[1] // capacity

    @pl.when(expert == experts - 1)
    def _():
        combine_blocks(place_ref, y_ref, out_ref, blocks, total, capacity, slots, width)


def expert_call(body, x, table, place, w_up, w_down, gate_up, capacity, group):
    blocks, experts, _, slots = table.shape
    width = x.shape[1]
    double, half = w_up.shape[2], w_down.shape[1]
    backward = gate_up is not None
    row_spec = lambda last: pl.BlockSpec((1, group, capacity, last), lambda c, e: (e, c, 0, 0))
    row_shape = lambda last, kind: jax.ShapeDtypeStruct((experts, blocks, capacity, last), kind)
    in_specs = [
        pl.BlockSpec((group * slots, width), lambda c, e: (c, 0)),
        pl.BlockSpec((group, 1, 2, slots), lambda c, e: (c, e, 0, 0)),
        pl.BlockSpec((group, slots, experts), lambda c, e: (c, 0, 0)),
        pl.BlockSpec((1, width, double), lambda c, e: (e, 0, 0)),
        pl.BlockSpec((1, half, width), lambda c, e: (e, 0, 0)),
    ]
    operands = [x, table, place, w_up, w_down]
    out_specs = [pl.BlockSpec((group * slots, width), lambda c, e: (c, 0)), row_spec(width)]
    out_shape = [jax.ShapeDtypeStruct(x.shape, low), row_shape(width, low)]
    if backward:
        in_specs.append(row_spec(double))
        operands.append(gate_up)
        out_specs.append(row_spec(double))
        out_shape.append(row_shape(double, low))
    else:
        out_specs += [row_spec(double), row_spec(half)]
        out_shape += [row_shape(double, wide), row_shape(half, low)]
    rows = experts * blocks * capacity
    return pl.pallas_call(
        body,
        grid=(blocks // group, experts),
        in_specs=in_specs,
        out_specs=out_specs,
        out_shape=out_shape,
        scratch_shapes=[pltpu.VMEM((group, experts * capacity, width), low)],
        compiler_params=pltpu.CompilerParams(
            dimension_semantics=("arbitrary", "arbitrary"), vmem_limit_bytes=60 << 20
        ),
        cost_estimate=pl.CostEstimate(
            flops=2 * rows * width * (2 * slots + double + half),
            bytes_accessed=2 * x.size * 2 + rows * (2 * width + 6 * double),
            transcendentals=rows * half,
        ),
    )(*operands)


def per_device(
    states,
    teacher,
    lengths,
    routes,
    gate_weights,
    w_qkv,
    w_out,
    norm_gains,
    qk_gains,
    w_gate_up,
    w_down,
):
    seq_count, slot_count, width = states.shape
    top_count = routes.shape[-1]
    ctx_size = lax.axis_size("ctx")
    tp_size = lax.axis_size("tp")
    shards = lax.axis_size(plane)
    ctx_index = lax.axis_index("ctx")
    tp_index = lax.axis_index("tp")
    plane_index = lax.axis_index(plane)
    tokens = seq_count * slot_count
    part = tokens // tp_size
    shard_experts = w_gate_up.shape[0]
    hidden_local = w_gate_up.shape[3]
    experts = shard_experts * shards
    capacity = 5 * tokens * top_count // (4 * experts)
    own_slots = jnp.arange(slot_count, dtype=jnp.int32)
    position = ctx_index * slot_count + own_slots
    tok_position = jnp.tile(position, seq_count)
    row_valid = (position[None, :] < lengths[:, None]).reshape(tokens).astype(wide)
    mirror = [(i, (i + 1) % ctx_size) for i in range(ctx_size)]

    gain_cols, head_cols = norm_gains.shape[1], qk_gains.shape[1]
    small = jnp.concatenate(
        [
            norm_gains.astype(wide).reshape(-1),
            qk_gains.astype(wide).reshape(-1),
            jnp.sum(lengths).astype(wide)[None],
        ]
    )
    small_all = lax.all_gather(small, plane, axis=0)
    gain_rows = small_all[:, : 2 * gain_cols].reshape(shards, 2, gain_cols)
    full_gains = jnp.swapaxes(gain_rows, 0, 1).reshape(2, shards * gain_cols)
    head_rows = small_all[:, 2 * gain_cols : 2 * (gain_cols + head_cols)]
    qk_float = jnp.swapaxes(head_rows.reshape(shards, 2, head_cols), 0, 1).reshape(
        2, shards * head_cols
    )
    valid_count = jnp.sum(small_all[:, -1]) / ctx_size
    gain_attn, gain_ffn = full_gains[0], full_gains[1]
    head_dim = qk_float.shape[1]
    heads_local = w_qkv.shape[2] // head_dim
    score_scale = head_dim ** (-0.5)

    tables = route_tables(
        routes.reshape(tokens, top_count), gate_weights.reshape(tokens, top_count), experts
    )
    table = lax.all_to_all(tables, plane, split_axis=0, concat_axis=0, tiled=True).reshape(
        shards, shard_experts, 2, tokens
    )
    rank = table[:, :, 0].astype(jnp.int32)
    offset = (jnp.arange(shard_experts, dtype=jnp.int32) * capacity)[None, :, None]
    place = jnp.swapaxes(jnp.where(rank >= 0, rank + offset, -1), 1, 2)
    w_up = w_gate_up.reshape(shard_experts, width, 2 * hidden_local)

    full_qkv = lax.all_gather(w_qkv, plane, axis=0, tiled=True)
    full_out = lax.all_gather(
        lax.all_gather(w_out, "tp", axis=0, tiled=True), plane, axis=1, tiled=True
    )
    flat_states = states.astype(wide).reshape(tokens, width)
    normed = rms_norm(flat_states, gain_attn).astype(low)
    projected = jnp.einsum(
        "nd,dkh->nkh", normed, full_qkv, preferred_element_type=wide
    ).reshape(tokens, 3, heads_local, head_dim)

    def prepare_local(projected_in, gains_in):
        return prepare(projected_in, gains_in, tok_position)

    (queries, key_states, values), prepare_back = jax.vjp(prepare_local, projected, qk_float)
    query_low = queries.astype(low).reshape(seq_count, slot_count, heads_local, head_dim)
    key_value = (
        jnp.stack([key_states, values], axis=1)
        .astype(low)
        .reshape(seq_count, slot_count, 2, heads_local, head_dim)
    )
    other_kv = lax.ppermute(key_value, "ctx", mirror)
    gathered = jnp.concatenate([key_value, other_kv], axis=1)
    other_position = (1 - ctx_index) * slot_count + own_slots
    key_position = jnp.concatenate([position, other_position])
    key_valid = key_position[None, :] < lengths[:, None]
    pieces = [
        attend_sequence(query_low[i], gathered[i], key_valid[i], score_scale)
        for i in range(seq_count)
    ]
    attended_low = (
        jnp.stack([p[0] for p in pieces]).astype(low).reshape(tokens, heads_local * head_dim)
    )
    attended_all = lax.all_gather(attended_low, "tp", axis=1, tiled=True)
    middle = flat_states + jnp.dot(attended_all, full_out, preferred_element_type=wide)
    normed_ffn = rms_norm(middle, gain_ffn).astype(low)

    x_all = lax.all_gather(normed_ffn, plane, axis=0, tiled=True)
    partial_out, rows_in, gate_up, hidden = expert_call(
        forward_body, x_all, table, place, w_up, w_down, None, capacity, 2
    )
    begin = tp_index * part
    own = lambda a: lax.dynamic_slice_in_dim(a, begin, part, 0)
    mixture = lax.psum_scatter(
        lax.psum_scatter(partial_out, plane, scatter_dimension=0, tiled=True),
        "tp",
        scatter_dimension=0,
        tiled=True,
    ).astype(wide)
    middle_own = own(middle)
    final_own = middle_own + mixture
    difference = final_own - own(teacher.reshape(tokens, width)).astype(wide)
    valid_own = own(row_valid)
    local_loss = jnp.sum(valid_own * jnp.sum(difference * difference, axis=-1))
    grad_final = 2.0 * loss_scale / valid_count * valid_own[:, None] * difference
    activations = lax.all_gather(final_own.astype(low), "tp", axis=0, tiled=True).reshape(
        seq_count, slot_count, width
    )

    grad_block = lax.all_gather(grad_final.astype(low), "tp", axis=0, tiled=True)
    grad_all = lax.all_gather(grad_block, plane, axis=0, tiled=True)
    partial_in, rows_out, grad_rows = expert_call(
        backward_body, grad_all, table, place, w_up, w_down, gate_up, capacity, 2
    )
    grad_ffn = lax.psum_scatter(
        lax.psum_scatter(partial_in, plane, scatter_dimension=0, tiled=True),
        "tp",
        scatter_dimension=0,
        tiled=True,
    ).astype(wide)
    grad_gate_up = jnp.einsum(
        "ebcd,ebcf->edf", rows_in, grad_rows, preferred_element_type=wide
    ).reshape(shard_experts, width, 2, hidden_local)
    grad_down = jnp.einsum("ebcf,ebcd->efd", hidden, rows_out, preferred_element_type=wide)

    grad_middle_norm, grad_gain_ffn = norm_back(grad_ffn, middle_own, gain_ffn)
    grad_middle = grad_final + grad_middle_norm
    grad_branch = grad_middle.astype(low)

    grad_attended = lax.all_to_all(
        nt_dot(grad_branch, full_out).astype(low), "tp", split_axis=1, concat_axis=0, tiled=True
    )
    branch_block = lax.all_gather(grad_branch, "tp", axis=0, tiled=True)
    grad_w_out = jnp.einsum("nf,nd->fd", attended_low, branch_block, preferred_element_type=wide)
    grad_heads = grad_attended.reshape(seq_count, slot_count, heads_local, head_dim)
    backs = [
        back_sequence(
            query_low[i], gathered[i], key_valid[i], pieces[i][1], grad_heads[i], score_scale
        )
        for i in range(seq_count)
    ]
    grad_query = jnp.stack([b[0] for b in backs])
    grad_kv = jnp.stack([b[1] for b in backs])
    sent_kv = grad_kv[:, slot_count:].astype(low)
    own_kv = grad_kv[:, :slot_count] + lax.ppermute(sent_kv, "ctx", mirror).astype(wide)
    grad_projected, grad_qk = prepare_back(
        (
            grad_query.reshape(tokens, heads_local, head_dim),
            own_kv[:, :, 0].reshape(tokens, heads_local, head_dim),
            own_kv[:, :, 1].reshape(tokens, heads_local, head_dim),
        )
    )
    grad_proj_low = grad_projected.astype(low).reshape(tokens, 3, heads_local * head_dim)
    grad_normed = lax.psum_scatter(
        jnp.einsum("nkh,dkh->nd", grad_proj_low, full_qkv, preferred_element_type=wide).astype(low),
        "tp",
        scatter_dimension=0,
        tiled=True,
    ).astype(wide)
    grad_w_qkv = jnp.einsum("nd,nkh->dkh", normed, grad_proj_low, preferred_element_type=wide)
    grad_states_norm, grad_gain_attn = norm_back(grad_normed, own(flat_states), gain_attn)
    grad_states = (
        lax.all_gather((grad_middle + grad_states_norm).astype(low), "tp", axis=0, tiled=True)
        .astype(wide)
        .reshape(seq_count, slot_count, width)
    )
    sums = lax.psum(
        jnp.concatenate(
            [grad_gain_attn, grad_gain_ffn, grad_qk.reshape(-1), local_loss[None]]
        ),
        everywhere,
    )
    out_gains = lax.dynamic_slice_in_dim(
        sums[: 2 * width].reshape(2, width), plane_index * gain_cols, gain_cols, 1
    )
    out_qk = lax.dynamic_slice_in_dim(
        sums[2 * width : 2 * (width + head_dim)].reshape(2, head_dim),
        plane_index * head_cols,
        head_cols,
        1,
    )
    loss_value = sums[-1] / valid_count
    out_qkv = lax.psum_scatter(
        grad_w_qkv.astype(low), plane, scatter_dimension=0, tiled=True
    ).astype(wide)
    out_w_out = lax.psum_scatter(
        grad_w_out.astype(low), plane, scatter_dimension=1, tiled=True
    ).astype(wide)
    return (
        activations,
        loss_value,
        valid_count,
        grad_states,
        out_qkv,
        out_w_out,
        out_gains,
        out_qk,
        grad_gate_up,
        grad_down,
    )


def solution(mesh):
    placed = (
        P("fsdp", "ctx", None),
        P("fsdp", "ctx", None),
        P("fsdp"),
        P("fsdp", "ctx", None),
        P("fsdp", "ctx", None),
        P(("fsdp", "ctx"), None, "tp"),
        P("tp", ("fsdp", "ctx")),
        P(None, ("fsdp", "ctx")),
        P(None, ("fsdp", "ctx")),
        P(("fsdp", "ctx"), None, None, "tp"),
        P(("fsdp", "ctx"), "tp", None),
    )
    return jax.shard_map(
        per_device,
        mesh=mesh,
        in_specs=placed,
        out_specs=(
            P("fsdp", "ctx", None),
            P(),
            P(),
            P("fsdp", "ctx", None),
            P(("fsdp", "ctx"), None, "tp"),
            P("tp", ("fsdp", "ctx")),
            P(None, ("fsdp", "ctx")),
            P(None, ("fsdp", "ctx")),
            P(("fsdp", "ctx"), None, None, "tp"),
            P(("fsdp", "ctx"), "tp", None),
        ),
        check_vma=False,
    )
```

```python
import functools

import jax
import jax.numpy as jnp
from jax import lax
from jax.experimental import pallas as pl
from jax.experimental.pallas import tpu as pltpu
from jax.sharding import PartitionSpec as P

norm_eps = 1e-05
rope_base = 10000.0
loss_scale = 4096.0
masked_score = -1e30
plane = ("fsdp", "ctx")
everywhere = ("fsdp", "ctx", "tp")
low = jnp.bfloat16
wide = jnp.float32


def rms_norm(values, gain_vec):
    return (
        values * lax.rsqrt(jnp.mean(values * values, axis=-1, keepdims=True) + norm_eps) * gain_vec
    )


def norm_back(grad_normed, values, gain_vec):
    inverse = lax.rsqrt(jnp.mean(values * values, axis=-1, keepdims=True) + norm_eps)
    scaled = values * inverse
    grad_scaled = grad_normed * gain_vec
    grad_values = inverse * (
        grad_scaled - scaled * jnp.mean(grad_scaled * scaled, axis=-1, keepdims=True)
    )
    return (grad_values, jnp.sum(grad_normed * scaled, axis=0))


def rotate(values, position):
    half_dim = values.shape[-1] // 2
    frequency = rope_base ** (-2.0 * jnp.arange(half_dim, dtype=wide) / values.shape[-1])
    angles = position.astype(wide)[:, None] * frequency[None, :]
    cosine = jnp.cos(angles)[:, None, :]
    sine_part = jnp.sin(angles)[:, None, :]
    first_half = values[..., :half_dim]
    second_half = values[..., half_dim:]
    return jnp.concatenate(
        [
            first_half * cosine - second_half * sine_part,
            second_half * cosine + first_half * sine_part,
        ],
        axis=-1,
    )


def prepare(projected, qk_float, position):
    queries = rotate(rms_norm(projected[:, 0], qk_float[0]), position)
    key_states = rotate(rms_norm(projected[:, 1], qk_float[1]), position)
    return (queries, key_states, projected[:, 2])


def attend_sequence(query_seq, kv_seq, valid_seq, score_scale):
    scores = (
        jnp.einsum("qhd,khd->hqk", query_seq, kv_seq[:, 0], preferred_element_type=wide)
        * score_scale
    )
    scores = jnp.where(valid_seq[None, None, :], scores, masked_score)
    peak_score = jnp.max(scores, axis=-1, keepdims=True)
    exponent = jnp.exp(scores - peak_score)
    row_total = jnp.sum(exponent, axis=-1, keepdims=True)
    probability = (exponent / row_total).astype(low)
    output = jnp.einsum("hqk,khd->qhd", probability, kv_seq[:, 1], preferred_element_type=wide)
    return (output, (peak_score + jnp.log(row_total))[..., 0])


def back_sequence(query_seq, kv_seq, valid_seq, log_seq, grad_seq, score_scale):
    scores = (
        jnp.einsum("qhd,khd->hqk", query_seq, kv_seq[:, 0], preferred_element_type=wide)
        * score_scale
    )
    scores = jnp.where(valid_seq[None, None, :], scores, masked_score)
    probability = jnp.exp(scores - log_seq[..., None])
    grad_prob = jnp.einsum("qhd,khd->hqk", grad_seq, kv_seq[:, 1], preferred_element_type=wide)
    grad_scores = (
        probability * (grad_prob - jnp.sum(probability * grad_prob, axis=-1, keepdims=True))
    ).astype(low)
    grad_query = (
        jnp.einsum("hqk,khd->qhd", grad_scores, kv_seq[:, 0], preferred_element_type=wide)
        * score_scale
    )
    grad_key = (
        jnp.einsum("hqk,qhd->khd", grad_scores, query_seq, preferred_element_type=wide)
        * score_scale
    )
    grad_value = jnp.einsum(
        "hqk,qhd->khd", probability.astype(low), grad_seq, preferred_element_type=wide
    )
    return (grad_query, jnp.stack([grad_key, grad_value], axis=1))


def route_tables(route_rows, gate_rows, experts):
    slots = route_rows.shape[0]
    hit = route_rows[None, :, :] == jnp.arange(experts, dtype=jnp.int32)[:, None, None]
    named = jnp.sum(hit.astype(wide), axis=-1)
    gates = jnp.sum(jnp.where(hit, gate_rows[None, :, :], 0.0), axis=-1)
    order = jnp.arange(slots, dtype=jnp.int32)
    before = (order[:, None] < order[None, :]).astype(low)
    rank = jnp.dot(named.astype(low), before, preferred_element_type=wide)
    return jnp.stack([jnp.where(named > 0.0, rank, -1.0), gates], axis=1)


def pick_rows(table_ref, block, capacity, slots):
    rank = table_ref[block, 0, 0:1, :].astype(jnp.int32)
    gate = table_ref[block, 0, 1:2, :]
    match = lax.broadcasted_iota(jnp.int32, (capacity, slots), 0) == rank
    chosen = jnp.where(match, 1.0, 0.0).astype(low)
    weight = jnp.sum(jnp.where(match, gate, 0.0), axis=1, keepdims=True)
    return (chosen, weight)


def spread_rows(place_ref, block, experts, capacity, slots):
    column = lax.broadcasted_iota(jnp.int32, (slots, experts * capacity), 1)
    match = column == place_ref[block, :, 0:1]
    for expert in range(1, experts):
        match = match | (column == place_ref[block, :, expert : expert + 1])
    return jnp.where(match, 1.0, 0.0).astype(low)


def nt_dot(left, right):
    return lax.dot_general(left, right, (((1,), (1,)), ((), ())), preferred_element_type=wide)


def tiles_of(width, most=512):
    step = min(width, most)
    return [slice(begin, begin + step) for begin in range(0, width, step)]


def take_rows(x_refs, table_ref, rows_ref):
    blocks, capacity, width = rows_ref.shape[1:]
    halves = len(x_refs) // blocks
    slots = halves * x_refs[0].shape[0]
    step = slots // halves
    weights = []
    for block in range(blocks):
        chosen, weight = pick_rows(table_ref, block, capacity, slots)
        weights.append(weight)
        for cut in tiles_of(width):
            found = jnp.dot(
                chosen[:, :step], x_refs[block * halves][:, cut], preferred_element_type=wide
            )
            for half in range(1, halves):
                found = found + jnp.dot(
                    chosen[:, half * step : (half + 1) * step],
                    x_refs[block * halves + half][:, cut],
                    preferred_element_type=wide,
                )
            rows_ref[0, block, :, cut] = found.astype(low)
    return (rows_ref[0].reshape(blocks * capacity, width), jnp.concatenate(weights, axis=0))


def combine_blocks(place_ref, y_ref, out_refs, capacity):
    blocks, total, width = y_ref.shape
    slots, step = out_refs[0].shape
    parts = width // step
    for block in range(blocks):
        matrix = spread_rows(place_ref, block, total // capacity, capacity, slots)
        for k in range(parts):
            out_refs[block * parts + k][...] = jnp.dot(
                matrix, y_ref[block, :, k * step : (k + 1) * step], preferred_element_type=wide
            ).astype(low)


def forward_body(n_x, n_out, n_keep, *refs):
    x_refs, refs = refs[:n_x], refs[n_x:]
    (table_ref, place_ref, up_ref, down_ref), refs = refs[:4], refs[4 + n_keep :]
    out_refs, (rows_ref, gate_up_ref, hidden_ref, y_ref) = refs[:n_out], refs[n_out:]
    expert = pl.program_id(0)
    blocks, capacity, width = rows_ref.shape[1:]
    half = down_ref.shape[1]
    rows, weight = take_rows(x_refs, table_ref, rows_ref)
    gate_up = jnp.dot(rows, up_ref[0], preferred_element_type=wide)
    gate_up_ref[0] = gate_up.reshape(blocks, capacity, 2 * half)
    gate_part = gate_up[:, :half]
    up_part = gate_up[:, half:]
    hidden = (gate_part * jax.nn.sigmoid(gate_part) * up_part * weight).astype(low)
    hidden_ref[0] = hidden.reshape(blocks, capacity, half)
    begin = pl.multiple_of(expert * capacity, 16)
    for cut in tiles_of(width):
        y_ref[:, pl.ds(begin, capacity), cut] = (
            jnp.dot(hidden, down_ref[0, :, cut], preferred_element_type=wide)
            .astype(low)
            .reshape(blocks, capacity, -1)
        )

    @pl.when(expert == pl.num_programs(0) - 1)
    def _():
        combine_blocks(place_ref, y_ref, out_refs, capacity)


def backward_body(n_x, n_out, n_keep, *refs):
    x_refs, refs = refs[:n_x], refs[n_x:]
    (table_ref, place_ref, up_ref, down_ref, gate_up_ref), refs = refs[:5], refs[5 + n_keep :]
    out_refs, (rows_ref, grad_ref, y_ref) = refs[:n_out], refs[n_out:]
    expert = pl.program_id(0)
    blocks, capacity, width = rows_ref.shape[1:]
    half = down_ref.shape[1]
    rows, weight = take_rows(x_refs, table_ref, rows_ref)
    grad_hidden = nt_dot(rows, down_ref[0]) * weight
    gate_up = gate_up_ref[0].reshape(blocks * capacity, 2 * half)
    gate_part = gate_up[:, :half]
    up_part = gate_up[:, half:]
    sigmoid = jax.nn.sigmoid(gate_part)
    grad_gate = grad_hidden * up_part * sigmoid * (1.0 + gate_part * (1.0 - sigmoid))
    grad_up = grad_hidden * gate_part * sigmoid
    grad_rows = jnp.concatenate([grad_gate, grad_up], axis=1).astype(low)
    grad_ref[0] = grad_rows.reshape(blocks, capacity, 2 * half)
    begin = pl.multiple_of(expert * capacity, 16)
    for cut in tiles_of(width):
        y_ref[:, pl.ds(begin, capacity), cut] = (
            nt_dot(grad_rows, up_ref[0, cut, :]).astype(low).reshape(blocks, capacity, -1)
        )

    @pl.when(expert == pl.num_programs(0) - 1)
    def _():
        combine_blocks(place_ref, y_ref, out_refs, capacity)


def expert_call(chunk, pieces, table, place, w_up, w_down, gate_up, kept, capacity, total, parts):
    blocks, experts, _, slots = table.shape
    width = pieces[0].shape[1]
    double, half = w_up.shape[2], w_down.shape[1]
    backward = gate_up is not None
    row_spec = lambda last: pl.BlockSpec(
        (1, blocks, capacity, last), lambda e: (e, chunk, 0, 0)
    )
    row_shape = lambda last, kind: jax.ShapeDtypeStruct((experts, total, capacity, last), kind)
    step = width // parts
    whole = lambda shape: pl.BlockSpec(shape, lambda e: (0,) * len(shape))
    in_specs = [whole(p.shape) for p in pieces] + [
        pl.BlockSpec((blocks, 1, 2, slots), lambda e: (0, e, 0, 0)),
        whole((blocks, slots, experts)),
        pl.BlockSpec((1, width, double), lambda e: (e, 0, 0)),
        pl.BlockSpec((1, half, width), lambda e: (e, 0, 0)),
    ]
    operands = [*pieces, table, place, w_up, w_down]
    n_out = blocks * parts
    out_specs = [whole((slots, step))] * n_out + [row_spec(width), row_spec(double)]
    out_shape = [jax.ShapeDtypeStruct((slots, step), low)] * n_out + [row_shape(width, low)]
    if backward:
        in_specs.append(row_spec(double))
        operands.append(gate_up)
        out_shape.append(row_shape(double, low))
    else:
        out_specs.append(row_spec(half))
        out_shape += [row_shape(double, wide), row_shape(half, low)]
    aliases = {len(operands) + i: n_out + i for i in range(len(kept))}
    rows = experts * blocks * capacity
    body = functools.partial(
        backward_body if backward else forward_body, len(pieces), n_out, len(kept)
    )
    made = pl.pallas_call(
        body,
        grid=(experts,),
        in_specs=in_specs + [pl.BlockSpec(memory_space=pl.ANY)] * len(kept),
        out_specs=out_specs,
        out_shape=out_shape,
        input_output_aliases=aliases,
        scratch_shapes=[pltpu.VMEM((blocks, experts * capacity, width), low)],
        compiler_params=pltpu.CompilerParams(
            dimension_semantics=("arbitrary",), vmem_limit_bytes=56 << 20
        ),
        cost_estimate=pl.CostEstimate(
            flops=2 * rows * width * (2 * slots + double + half),
            bytes_accessed=4 * blocks * slots * width + rows * (2 * width + 6 * double),
            transcendentals=rows * half,
        ),
    )(*operands, *kept)
    outs = [made[b * parts : (b + 1) * parts] for b in range(blocks)]
    return (outs, made[n_out:])


def added(left, right):
    return left.astype(wide) + right.astype(wide)


class Plane:
    def __init__(self):
        self.fsdp, self.ctx = lax.axis_size("fsdp"), lax.axis_size("ctx")
        self.tree = self.fsdp == 4 and self.ctx == 2
        self.shards = self.fsdp * self.ctx

    def core(self, a):
        return lax.ppermute(a, "fsdp", [(i, i ^ 1) for i in range(self.fsdp)])

    def along_x(self, a):
        return lax.ppermute(a, "fsdp", [(i, i ^ 2) for i in range(self.fsdp)])

    def along_y(self, a):
        return lax.ppermute(a, "ctx", [(i, i ^ 1) for i in range(self.ctx)])

    def order(self):
        if not self.tree:
            return list(range(self.shards))
        fsdp, ctx = lax.axis_index("fsdp"), lax.axis_index("ctx")
        chips = ((0, 0), (1, 0), (0, 1), (1, 1))
        return [(fsdp ^ (2 * x) ^ core) * 2 + (ctx ^ y) for x, y in chips for core in (0, 1)]

    def gather(self, first, second):
        if not self.tree:
            tops = jnp.split(lax.all_gather(first, plane, axis=0, tiled=True), self.shards)
            ends = jnp.split(lax.all_gather(second, plane, axis=0, tiled=True), self.shards)
            return [
                [tops[i], ends[i], tops[i + 1], ends[i + 1]] for i in range(0, self.shards, 2)
            ]
        x_first, y_second = self.along_x(first), self.along_y(second)
        x_second, y_first = self.along_x(second), self.along_y(first)
        far_first, far_second = self.along_y(x_first), self.along_x(y_second)
        pairs = [
            (first, second),
            (x_first, x_second),
            (y_first, y_second),
            (far_first, far_second),
        ]
        return [[a, b, self.core(a), self.core(b)] for a, b in pairs]

    def reduce(self, outs):
        if not self.tree:
            flat = [jnp.concatenate(block, axis=1) for pair in outs for block in pair]
            total = lax.psum_scatter(
                jnp.concatenate(flat, axis=0), plane, scatter_dimension=0, tiled=True
            )
            return jnp.split(total.astype(wide), len(outs[0][0]), axis=1)
        sums = []
        for k in range(len(outs[0][0])):
            own, near_x, near_y, far = [added(pair[0][k], self.core(pair[1][k])) for pair in outs]
            if k % 2 == 0:
                near_y = near_y + self.along_x(far.astype(low)).astype(wide)
            else:
                near_x = near_x + self.along_y(far.astype(low)).astype(wide)
            sums.append(
                own
                + self.along_x(near_x.astype(low)).astype(wide)
                + self.along_y(near_y.astype(low)).astype(wide)
            )
        return sums


def per_device(
    states,
    teacher,
    lengths,
    routes,
    gate_weights,
    w_qkv,
    w_out,
    norm_gains,
    qk_gains,
    w_gate_up,
    w_down,
):
    seq_count, slot_count, width = states.shape
    top_count = routes.shape[-1]
    ctx_size = lax.axis_size("ctx")
    tp_size = lax.axis_size("tp")
    shards = lax.axis_size(plane)
    ctx_index = lax.axis_index("ctx")
    tp_index = lax.axis_index("tp")
    plane_index = lax.axis_index(plane)
    tokens = seq_count * slot_count
    part = tokens // tp_size
    shard_experts = w_gate_up.shape[0]
    hidden_local = w_gate_up.shape[3]
    experts = shard_experts * shards
    capacity = 5 * tokens * top_count // (4 * experts)
    own_slots = jnp.arange(slot_count, dtype=jnp.int32)
    position = ctx_index * slot_count + own_slots
    tok_position = jnp.tile(position, seq_count)
    row_valid = (position[None, :] < lengths[:, None]).reshape(tokens).astype(wide)
    mirror = [(i, (i + 1) % ctx_size) for i in range(ctx_size)]

    gain_cols, head_cols = norm_gains.shape[1], qk_gains.shape[1]
    small = jnp.concatenate(
        [
            norm_gains.astype(wide).reshape(-1),
            qk_gains.astype(wide).reshape(-1),
            jnp.sum(lengths).astype(wide)[None],
        ]
    )
    small_all = lax.all_gather(small, plane, axis=0)
    gain_rows = small_all[:, : 2 * gain_cols].reshape(shards, 2, gain_cols)
    full_gains = jnp.swapaxes(gain_rows, 0, 1).reshape(2, shards * gain_cols)
    head_rows = small_all[:, 2 * gain_cols : 2 * (gain_cols + head_cols)]
    qk_float = jnp.swapaxes(head_rows.reshape(shards, 2, head_cols), 0, 1).reshape(
        2, shards * head_cols
    )
    valid_count = jnp.sum(small_all[:, -1]) / ctx_size
    gain_attn, gain_ffn = full_gains[0], full_gains[1]
    head_dim = qk_float.shape[1]
    heads_local = w_qkv.shape[2] // head_dim
    score_scale = head_dim ** (-0.5)

    tables = route_tables(
        routes.reshape(tokens, top_count), gate_weights.reshape(tokens, top_count), experts
    )
    table = lax.all_to_all(tables, plane, split_axis=0, concat_axis=0, tiled=True).reshape(
        shards, shard_experts, 2, tokens
    )
    rank = table[:, :, 0].astype(jnp.int32)
    offset = (jnp.arange(shard_experts, dtype=jnp.int32) * capacity)[None, :, None]
    place = jnp.swapaxes(jnp.where(rank >= 0, rank + offset, -1), 1, 2)
    w_up = w_gate_up.reshape(shard_experts, width, 2 * hidden_local)
    places = Plane()
    order = places.order()
    sort = lambda a: jnp.concatenate(
        [lax.dynamic_slice_in_dim(a, block, 1, 0) for block in order], axis=0
    )
    table, place = sort(table), sort(place)
    back_table = jnp.swapaxes(
        table.reshape(shards, shard_experts, 2, tp_size, 2, part // 2), 3, 4
    ).reshape(table.shape)
    chunks = shards // 2
    pair = lambda a, c: a[2 * c : 2 * c + 2]
    parts = 4

    full_qkv = lax.all_gather(w_qkv.reshape(w_qkv.shape[0], -1), plane, axis=0, tiled=True)
    full_out = lax.all_gather(
        lax.all_gather(w_out, "tp", axis=0, tiled=True), plane, axis=1, tiled=True
    )
    flat_states = states.astype(wide).reshape(tokens, width)
    normed = rms_norm(flat_states, gain_attn).astype(low)
    projected = jnp.dot(normed, full_qkv, preferred_element_type=wide).reshape(
        tokens, 3, heads_local, head_dim
    )

    def prepare_local(projected_in, gains_in):
        return prepare(projected_in, gains_in, tok_position)

    (queries, key_states, values), prepare_back = jax.vjp(prepare_local, projected, qk_float)
    query_low = queries.astype(low).reshape(seq_count, slot_count, heads_local, head_dim)
    key_value = (
        jnp.stack([key_states, values], axis=1)
        .astype(low)
        .reshape(seq_count, slot_count, 2, heads_local, head_dim)
    )
    other_kv = lax.ppermute(key_value, "ctx", mirror)
    gathered = jnp.concatenate([key_value, other_kv], axis=1)
    other_position = (1 - ctx_index) * slot_count + own_slots
    key_position = jnp.concatenate([position, other_position])
    key_valid = key_position[None, :] < lengths[:, None]
    pieces = [
        attend_sequence(query_low[i], gathered[i], key_valid[i], score_scale)
        for i in range(seq_count)
    ]
    attended_low = (
        jnp.stack([p[0] for p in pieces]).astype(low).reshape(tokens, heads_local * head_dim)
    )
    attended_all = lax.all_gather(attended_low, "tp", axis=1, tiled=True)
    middle = flat_states + jnp.dot(attended_all, full_out, preferred_element_type=wide)
    normed_ffn = rms_norm(middle, gain_ffn).astype(low)

    begin = tp_index * part
    own = lambda a: lax.dynamic_slice_in_dim(a, begin, part, 0)
    half_rows = tokens // 2
    x_chunks = places.gather(normed_ffn[:half_rows], normed_ffn[half_rows:])
    kept, outs = (), []
    for c in range(chunks):
        made, kept = expert_call(
            c, x_chunks[c], pair(table, c), pair(place, c), w_up, w_down, None, kept,
            capacity, shards, parts,
        )
        outs.append(made)
    rows_in, gate_up, hidden = kept

    def finish(outs):
        sums = places.reduce(outs)
        ready = [
            lax.psum_scatter(
                jnp.concatenate(sums[k : k + 2], axis=1).astype(low),
                "tp",
                scatter_dimension=0,
                tiled=True,
            )
            for k in range(0, parts, 2)
        ]
        return jnp.concatenate(ready, axis=1).astype(wide)

    mixture = finish(outs)
    middle_own = own(middle)
    final_own = middle_own + mixture
    difference = final_own - own(teacher.reshape(tokens, width)).astype(wide)
    valid_own = own(row_valid)
    local_loss = jnp.sum(valid_own * jnp.sum(difference * difference, axis=-1))
    grad_final = 2.0 * loss_scale / valid_count * valid_own[:, None] * difference
    activations = lax.all_gather(final_own.astype(low), "tp", axis=0, tiled=True).reshape(
        seq_count, slot_count, width
    )

    grad_low = grad_final.astype(low)
    grad_chunks = places.gather(
        lax.all_gather(grad_low[: part // 2], "tp", axis=0, tiled=True),
        lax.all_gather(grad_low[part // 2 :], "tp", axis=0, tiled=True),
    )
    kept, outs = (), []
    for c in range(chunks):
        made, kept = expert_call(
            c, grad_chunks[c], pair(back_table, c), pair(place, c), w_up, w_down, gate_up, kept,
            capacity, shards, parts,
        )
        outs.append(made)
    rows_out, grad_rows = kept
    grad_ffn = finish(outs)
    grad_gate_up = jnp.einsum(
        "ebcd,ebcf->edf", rows_in, grad_rows, preferred_element_type=wide
    ).reshape(shard_experts, width, 2, hidden_local)
    grad_down = jnp.einsum("ebcf,ebcd->efd", hidden, rows_out, preferred_element_type=wide)

    grad_middle_norm, grad_gain_ffn = norm_back(grad_ffn, middle_own, gain_ffn)
    grad_middle = grad_final + grad_middle_norm
    grad_branch = grad_middle.astype(low)

    grad_attended = lax.all_to_all(
        nt_dot(grad_branch, full_out).astype(low), "tp", split_axis=1, concat_axis=0, tiled=True
    )
    branch_block = lax.all_gather(grad_branch, "tp", axis=0, tiled=True)
    grad_w_out = jnp.einsum("nf,nd->fd", attended_low, branch_block, preferred_element_type=wide)
    grad_heads = grad_attended.reshape(seq_count, slot_count, heads_local, head_dim)
    backs = [
        back_sequence(
            query_low[i], gathered[i], key_valid[i], pieces[i][1], grad_heads[i], score_scale
        )
        for i in range(seq_count)
    ]
    grad_query = jnp.stack([b[0] for b in backs])
    grad_kv = jnp.stack([b[1] for b in backs])
    sent_kv = grad_kv[:, slot_count:].astype(low)
    own_kv = grad_kv[:, :slot_count] + lax.ppermute(sent_kv, "ctx", mirror).astype(wide)
    grad_projected, grad_qk = prepare_back(
        (
            grad_query.reshape(tokens, heads_local, head_dim),
            own_kv[:, :, 0].reshape(tokens, heads_local, head_dim),
            own_kv[:, :, 1].reshape(tokens, heads_local, head_dim),
        )
    )
    grad_proj_low = grad_projected.astype(low).reshape(tokens, -1)
    grad_normed = lax.psum_scatter(
        nt_dot(grad_proj_low, full_qkv).astype(low),
        "tp",
        scatter_dimension=0,
        tiled=True,
    ).astype(wide)
    grad_w_qkv = jnp.einsum("nd,nk->dk", normed, grad_proj_low, preferred_element_type=wide)
    grad_states_norm, grad_gain_attn = norm_back(grad_normed, own(flat_states), gain_attn)
    grad_states = (
        lax.all_gather((grad_middle + grad_states_norm).astype(low), "tp", axis=0, tiled=True)
        .astype(wide)
        .reshape(seq_count, slot_count, width)
    )
    sums = lax.psum(
        jnp.concatenate(
            [grad_gain_attn, grad_gain_ffn, grad_qk.reshape(-1), local_loss[None]]
        ),
        everywhere,
    )
    out_gains = lax.dynamic_slice_in_dim(
        sums[: 2 * width].reshape(2, width), plane_index * gain_cols, gain_cols, 1
    )
    out_qk = lax.dynamic_slice_in_dim(
        sums[2 * width : 2 * (width + head_dim)].reshape(2, head_dim),
        plane_index * head_cols,
        head_cols,
        1,
    )
    loss_value = sums[-1] / valid_count
    out_qkv = lax.psum_scatter(
        grad_w_qkv.astype(low), plane, scatter_dimension=0, tiled=True
    ).astype(wide).reshape(w_qkv.shape)
    out_w_out = lax.psum_scatter(
        grad_w_out.astype(low), plane, scatter_dimension=1, tiled=True
    ).astype(wide)
    return (
        activations,
        loss_value,
        valid_count,
        grad_states,
        out_qkv,
        out_w_out,
        out_gains,
        out_qk,
        grad_gate_up,
        grad_down,
    )


def solution(mesh):
    placed = (
        P("fsdp", "ctx", None),
        P("fsdp", "ctx", None),
        P("fsdp"),
        P("fsdp", "ctx", None),
        P("fsdp", "ctx", None),
        P(("fsdp", "ctx"), None, "tp"),
        P("tp", ("fsdp", "ctx")),
        P(None, ("fsdp", "ctx")),
        P(None, ("fsdp", "ctx")),
        P(("fsdp", "ctx"), None, None, "tp"),
        P(("fsdp", "ctx"), "tp", None),
    )
    return jax.shard_map(
        per_device,
        mesh=mesh,
        in_specs=placed,
        out_specs=(
            P("fsdp", "ctx", None),
            P(),
            P(),
            P("fsdp", "ctx", None),
            P(("fsdp", "ctx"), None, "tp"),
            P("tp", ("fsdp", "ctx")),
            P(None, ("fsdp", "ctx")),
            P(None, ("fsdp", "ctx")),
            P(("fsdp", "ctx"), None, None, "tp"),
            P(("fsdp", "ctx"), "tp", None),
        ),
        check_vma=False,
    )
```

```python
import functools

import jax
import jax.numpy as jnp
from jax import lax
from jax.experimental import pallas as pl
from jax.experimental.pallas import tpu as pltpu
from jax.sharding import PartitionSpec as P

norm_eps = 1e-05
rope_base = 10000.0
loss_scale = 4096.0
masked_score = -1e30
plane = ("fsdp", "ctx")
everywhere = ("fsdp", "ctx", "tp")
low = jnp.bfloat16
wide = jnp.float32


def rms_norm(values, gain_vec):
    return (
        values * lax.rsqrt(jnp.mean(values * values, axis=-1, keepdims=True) + norm_eps) * gain_vec
    )


def norm_back(grad_normed, values, gain_vec):
    inverse = lax.rsqrt(jnp.mean(values * values, axis=-1, keepdims=True) + norm_eps)
    scaled = values * inverse
    grad_scaled = grad_normed * gain_vec
    grad_values = inverse * (
        grad_scaled - scaled * jnp.mean(grad_scaled * scaled, axis=-1, keepdims=True)
    )
    return (grad_values, jnp.sum(grad_normed * scaled, axis=0))


def rotate(values, position):
    half_dim = values.shape[-1] // 2
    frequency = rope_base ** (-2.0 * jnp.arange(half_dim, dtype=wide) / values.shape[-1])
    angles = position.astype(wide)[:, None] * frequency[None, :]
    cosine = jnp.cos(angles)[:, None, :]
    sine_part = jnp.sin(angles)[:, None, :]
    first_half = values[..., :half_dim]
    second_half = values[..., half_dim:]
    return jnp.concatenate(
        [
            first_half * cosine - second_half * sine_part,
            second_half * cosine + first_half * sine_part,
        ],
        axis=-1,
    )


def prepare(projected, qk_float, position):
    queries = rotate(rms_norm(projected[:, 0], qk_float[0]), position)
    key_states = rotate(rms_norm(projected[:, 1], qk_float[1]), position)
    return (queries, key_states, projected[:, 2])


def attend_sequence(query_seq, kv_seq, valid_seq, score_scale):
    scores = (
        jnp.einsum("qhd,khd->hqk", query_seq, kv_seq[:, 0], preferred_element_type=wide)
        * score_scale
    )
    scores = jnp.where(valid_seq[None, None, :], scores, masked_score)
    peak_score = jnp.max(scores, axis=-1, keepdims=True)
    exponent = jnp.exp(scores - peak_score)
    row_total = jnp.sum(exponent, axis=-1, keepdims=True)
    probability = (exponent / row_total).astype(low)
    output = jnp.einsum("hqk,khd->qhd", probability, kv_seq[:, 1], preferred_element_type=wide)
    return (output, (peak_score + jnp.log(row_total))[..., 0])


def back_sequence(query_seq, kv_seq, valid_seq, log_seq, grad_seq, score_scale):
    scores = (
        jnp.einsum("qhd,khd->hqk", query_seq, kv_seq[:, 0], preferred_element_type=wide)
        * score_scale
    )
    scores = jnp.where(valid_seq[None, None, :], scores, masked_score)
    probability = jnp.exp(scores - log_seq[..., None])
    grad_prob = jnp.einsum("qhd,khd->hqk", grad_seq, kv_seq[:, 1], preferred_element_type=wide)
    grad_scores = (
        probability * (grad_prob - jnp.sum(probability * grad_prob, axis=-1, keepdims=True))
    ).astype(low)
    grad_query = (
        jnp.einsum("hqk,khd->qhd", grad_scores, kv_seq[:, 0], preferred_element_type=wide)
        * score_scale
    )
    grad_key = (
        jnp.einsum("hqk,qhd->khd", grad_scores, query_seq, preferred_element_type=wide)
        * score_scale
    )
    grad_value = jnp.einsum(
        "hqk,qhd->khd", probability.astype(low), grad_seq, preferred_element_type=wide
    )
    return (grad_query, jnp.stack([grad_key, grad_value], axis=1))


def route_tables(route_rows, gate_rows, experts):
    slots = route_rows.shape[0]
    hit = route_rows[None, :, :] == jnp.arange(experts, dtype=jnp.int32)[:, None, None]
    named = jnp.sum(hit.astype(wide), axis=-1)
    gates = jnp.sum(jnp.where(hit, gate_rows[None, :, :], 0.0), axis=-1)
    order = jnp.arange(slots, dtype=jnp.int32)
    before = (order[:, None] < order[None, :]).astype(low)
    rank = jnp.dot(named.astype(low), before, preferred_element_type=wide)
    return jnp.stack([jnp.where(named > 0.0, rank, -1.0), gates], axis=1)


def pick_rows(table_ref, block, capacity, slots):
    rank = table_ref[block, 0, 0:1, :].astype(jnp.int32)
    gate = table_ref[block, 0, 1:2, :]
    match = lax.broadcasted_iota(jnp.int32, (capacity, slots), 0) == rank
    chosen = jnp.where(match, 1.0, 0.0).astype(low)
    weight = jnp.sum(jnp.where(match, gate, 0.0), axis=1, keepdims=True)
    return (chosen, weight)


def spread_rows(place_ref, block, experts, capacity, slots):
    column = lax.broadcasted_iota(jnp.int32, (slots, experts * capacity), 1)
    match = column == place_ref[block, :, 0:1]
    for expert in range(1, experts):
        match = match | (column == place_ref[block, :, expert : expert + 1])
    return jnp.where(match, 1.0, 0.0).astype(low)


def nt_dot(left, right):
    return lax.dot_general(left, right, (((1,), (1,)), ((), ())), preferred_element_type=wide)


def tiles_of(width, most=512):
    step = min(width, most)
    return [slice(begin, begin + step) for begin in range(0, width, step)]


def take_rows(x_refs, table_ref, rows_ref):
    blocks, capacity, width = rows_ref.shape[1:]
    slots = table_ref.shape[3]
    step, span = x_refs[0].shape
    halves, splits = slots // step, width // span
    weights = []
    for block in range(blocks):
        chosen, weight = pick_rows(table_ref, block, capacity, slots)
        weights.append(weight)
        for cut in tiles_of(width):
            split, begin = divmod(cut.start, span)
            found = None
            for half in range(halves):
                x_ref = x_refs[(block * halves + half) * splits + split]
                term = jnp.dot(
                    chosen[:, half * step : (half + 1) * step],
                    x_ref[:, begin : begin + cut.stop - cut.start],
                    preferred_element_type=wide,
                )
                found = term if found is None else found + term
            rows_ref[0, block, :, cut] = found.astype(low)
    return (rows_ref[0].reshape(blocks * capacity, width), jnp.concatenate(weights, axis=0))


def fill_spread(place_ref, spread_ref, capacity):
    blocks, slots, total = spread_ref.shape
    for block in range(blocks):
        spread_ref[block] = spread_rows(place_ref, block, total // capacity, capacity, slots)


def combine_blocks(spread_ref, y_ref, out_refs):
    for block, out_ref in enumerate(out_refs):
        for cut in tiles_of(y_ref.shape[2]):
            out_ref[:, cut] = jnp.dot(
                spread_ref[block], y_ref[block, :, cut], preferred_element_type=wide
            ).astype(low)


def forward_body(n_x, n_out, n_keep, *refs):
    x_refs, refs = refs[:n_x], refs[n_x:]
    (table_ref, place_ref, up_ref, down_ref), refs = refs[:4], refs[4 + n_keep :]
    out_refs, (rows_ref, gate_up_ref, hidden_ref, y_ref, spread_ref) = refs[:n_out], refs[n_out:]
    expert = pl.program_id(0)
    blocks, capacity, width = rows_ref.shape[1:]
    experts = y_ref.shape[1] // capacity

    @pl.when(expert == 0)
    def _():
        fill_spread(place_ref, spread_ref, capacity)

    half = down_ref.shape[1]
    rows, weight = take_rows(x_refs, table_ref, rows_ref)
    gate_up = jnp.dot(rows, up_ref[0], preferred_element_type=wide)
    gate_up_ref[0] = gate_up.reshape(blocks, capacity, 2 * half)
    gate_part = gate_up[:, :half]
    up_part = gate_up[:, half:]
    hidden = (gate_part * jax.nn.sigmoid(gate_part) * up_part * weight).astype(low)
    hidden_ref[0] = hidden.reshape(blocks, capacity, half)
    begin = pl.multiple_of(expert * capacity, 16)
    for cut in tiles_of(width):
        y_ref[:, pl.ds(begin, capacity), cut] = (
            jnp.dot(hidden, down_ref[0, :, cut], preferred_element_type=wide)
            .astype(low)
            .reshape(blocks, capacity, -1)
        )

    @pl.when(expert == experts - 1)
    def _():
        combine_blocks(spread_ref, y_ref, out_refs)


def backward_body(n_x, n_out, n_keep, *refs):
    x_refs, refs = refs[:n_x], refs[n_x:]
    (table_ref, place_ref, up_ref, down_ref, gate_up_ref), refs = refs[:5], refs[5 + n_keep :]
    out_refs, (rows_ref, grad_ref, y_ref, spread_ref) = refs[:n_out], refs[n_out:]
    expert = pl.program_id(0)
    blocks, capacity, width = rows_ref.shape[1:]
    experts = y_ref.shape[1] // capacity

    @pl.when(expert == 0)
    def _():
        fill_spread(place_ref, spread_ref, capacity)

    half = down_ref.shape[1]
    rows, weight = take_rows(x_refs, table_ref, rows_ref)
    grad_hidden = nt_dot(rows, down_ref[0]) * weight
    gate_up = gate_up_ref[0].reshape(blocks * capacity, 2 * half)
    gate_part = gate_up[:, :half]
    up_part = gate_up[:, half:]
    sigmoid = jax.nn.sigmoid(gate_part)
    grad_gate = grad_hidden * up_part * sigmoid * (1.0 + gate_part * (1.0 - sigmoid))
    grad_up = grad_hidden * gate_part * sigmoid
    grad_rows = jnp.concatenate([grad_gate, grad_up], axis=1).astype(low)
    grad_ref[0] = grad_rows.reshape(blocks, capacity, 2 * half)
    begin = pl.multiple_of(expert * capacity, 16)
    for cut in tiles_of(width):
        y_ref[:, pl.ds(begin, capacity), cut] = (
            nt_dot(grad_rows, up_ref[0, cut, :]).astype(low).reshape(blocks, capacity, -1)
        )

    @pl.when(expert == experts - 1)
    def _():
        combine_blocks(spread_ref, y_ref, out_refs)


def expert_call(chunk, pieces, table, place, w_up, w_down, gate_up, kept, capacity, total):
    blocks, experts, _, slots = table.shape
    width = w_up.shape[1]
    double, half = w_up.shape[2], w_down.shape[1]
    backward = gate_up is not None
    once = pl.Buffered(1)
    row_spec = lambda last: pl.BlockSpec(
        (1, blocks, capacity, last), lambda e: (e, chunk, 0, 0)
    )
    row_shape = lambda last, kind: jax.ShapeDtypeStruct((experts, total, capacity, last), kind)
    whole = lambda shape: pl.BlockSpec(shape, lambda e: (0,) * len(shape), pipeline_mode=once)
    in_specs = [whole(p.shape) for p in pieces] + [
        pl.BlockSpec((blocks, 1, 2, slots), lambda e: (0, e, 0, 0)),
        whole((blocks, slots, experts)),
        pl.BlockSpec((1, width, double), lambda e: (e, 0, 0)),
        pl.BlockSpec((1, half, width), lambda e: (e, 0, 0)),
    ]
    operands = [*pieces, table, place, w_up, w_down]
    n_out = blocks
    out_specs = [whole((slots, width))] * n_out + [row_spec(width), row_spec(double)]
    out_shape = [jax.ShapeDtypeStruct((slots, width), low)] * n_out + [row_shape(width, low)]
    if backward:
        in_specs.append(row_spec(double))
        operands.append(gate_up)
        out_shape.append(row_shape(double, low))
    else:
        out_specs.append(row_spec(half))
        out_shape += [row_shape(double, wide), row_shape(half, low)]
    aliases = {len(operands) + i: n_out + i for i in range(len(kept))}
    rows = experts * blocks * capacity
    body = functools.partial(
        backward_body if backward else forward_body, len(pieces), n_out, len(kept)
    )
    made = pl.pallas_call(
        body,
        grid=(experts,),
        in_specs=in_specs + [pl.BlockSpec(memory_space=pl.ANY)] * len(kept),
        out_specs=out_specs,
        out_shape=out_shape,
        input_output_aliases=aliases,
        scratch_shapes=[
            pltpu.VMEM((blocks, experts * capacity, width), low),
            pltpu.VMEM((blocks, slots, experts * capacity), low),
        ],
        compiler_params=pltpu.CompilerParams(
            dimension_semantics=("arbitrary",), vmem_limit_bytes=48 << 20
        ),
        cost_estimate=pl.CostEstimate(
            flops=2 * rows * width * (2 * slots + double + half),
            bytes_accessed=4 * blocks * slots * width + rows * (2 * width + 6 * double),
            transcendentals=rows * half,
        ),
    )(*operands, *kept)
    return (made[:n_out], made[n_out:])


def added(left, right):
    return left.astype(wide) + right.astype(wide)


def tie(values, *anchors):
    return lax.optimization_barrier((values, anchors))[0]


def sum_everywhere(values):
    values = values[None]
    for axis in everywhere:
        size, step = lax.axis_size(axis), 1
        while step < size:
            pairs = [(i, i ^ step) for i in range(size)]
            values = values + lax.ppermute(values, axis, pairs)
            step *= 2
    return values[0]


def line_gather(shard):
    size = lax.axis_size("tp")
    if size > 4:
        return lax.all_gather(shard, "tp", axis=0, tiled=True)
    move = lambda d: lax.ppermute(
        shard, "tp", [(i, i + d) for i in range(size) if 0 <= i + d < size]
    )
    near = [move(d) for d in range(size - 1, 0, -1)] + [shard] + [move(-d) for d in range(1, size)]
    rows = shard.shape[0]
    begin = (size - 1 - lax.axis_index("tp")) * rows
    return lax.dynamic_slice_in_dim(jnp.concatenate(near, axis=0), begin, size * rows, 0)


class Plane:
    def __init__(self):
        self.fsdp, self.ctx = lax.axis_size("fsdp"), lax.axis_size("ctx")
        self.tree = self.fsdp == 4 and self.ctx == 2
        self.shards = self.fsdp * self.ctx

    def core(self, a):
        return lax.ppermute(a, "fsdp", [(i, i ^ 1) for i in range(self.fsdp)])

    def along_x(self, a):
        return lax.ppermute(a, "fsdp", [(i, i ^ 2) for i in range(self.fsdp)])

    def along_y(self, a):
        return lax.ppermute(a, "ctx", [(i, i ^ 1) for i in range(self.ctx)])

    def order(self):
        if not self.tree:
            return list(range(self.shards))
        fsdp, ctx = lax.axis_index("fsdp"), lax.axis_index("ctx")
        chips = ((0, 0), (1, 0), (0, 1), (1, 1))
        return [(fsdp ^ (2 * x) ^ core) * 2 + (ctx ^ y) for x, y in chips for core in (0, 1)]

    def gather_whole(self, shard):
        rows = shard.shape[0]
        if not self.tree:
            return lax.all_gather(shard, plane, axis=0, tiled=True)
        halves = (shard[: rows // 2], shard[rows // 2 :]) if rows > 1 else (shard,)
        x = [self.along_x(h) for h in halves]
        y = [self.along_y(h) for h in halves]
        far = [self.along_y(x[0])] + [self.along_x(h) for h in y[1:]]
        whole = jnp.zeros((self.shards * rows, *shard.shape[1:]), shard.dtype)
        order = self.order()
        for c, pieces in enumerate((halves, x, y, far)):
            for core in (0, 1):
                begin = order[2 * c + core] * rows
                for piece in pieces:
                    found = self.core(piece) if core else piece
                    whole = lax.dynamic_update_slice_in_dim(whole, found, begin, 0)
                    begin = begin + piece.shape[0]
        return whole

    def reduce_whole(self, partial):
        rows = partial.shape[0] // self.shards
        if not self.tree:
            return lax.psum_scatter(partial, plane, scatter_dimension=0, tiled=True).astype(wide)
        blocks = [lax.dynamic_slice_in_dim(partial, i * rows, rows, 0) for i in self.order()]
        pre = [added(blocks[2 * c], self.core(blocks[2 * c + 1])) for c in range(4)]
        cuts = tiles_of(partial.shape[1], partial.shape[1] // 2)
        return jnp.concatenate(
            [self.total(k, *[p[:, cut] for p in pre]) for k, cut in enumerate(cuts)], axis=1
        )

    def total(self, k, own, near_x, near_y, far):
        if k % 2 == 0:
            near_y = near_y + self.along_x(far.astype(low)).astype(wide)
        else:
            near_x = near_x + self.along_y(far.astype(low)).astype(wide)
        from_x, from_y = self.along_x(near_x.astype(low)), self.along_y(near_y.astype(low))
        return own + from_x.astype(wide) + from_y.astype(wide)

    def experts(self, first, second, call, parts, filler=list):
        if not self.tree:
            tops = jnp.split(lax.all_gather(first, plane, axis=0, tiled=True), self.shards)
            ends = jnp.split(lax.all_gather(second, plane, axis=0, tiled=True), self.shards)
            made = []
            for i in range(0, self.shards, 2):
                made += call(i // 2, [tops[i], ends[i], tops[i + 1], ends[i + 1]])
            total = lax.psum_scatter(
                jnp.concatenate(made, axis=0), plane, scatter_dimension=0, tiled=True
            )
            return jnp.split(total, parts // 2, axis=1)
        cuts = tiles_of(first.shape[1], first.shape[1] // parts)
        pre = lambda made, other: [added(made[0][:, cut], other[:, cut]) for cut in cuts]
        middle = first.shape[1] // 2

        def beyond(x_half, y_half):
            return self.along_y(x_half[:, :middle]), self.along_x(y_half[:, middle:])

        x_first, y_first = self.along_x(first), self.along_y(first)
        far_first = beyond(x_first, y_first)
        second = tie(second, x_first, y_first)
        x_second, y_second = self.along_x(second), self.along_y(second)
        own = call(0, [first, second, self.core(first), self.core(second)])
        x_second, y_second = tie((x_second, y_second), own[0])
        far_second = beyond(x_second, y_second)
        near_x = call(1, [x_first, x_second, self.core(x_first), self.core(x_second)])
        other_own, other_x = self.core(own[1]), self.core(near_x[1])
        pieces = [y_first, y_second, self.core(y_first), self.core(y_second)]
        near_y = call(2, tie(pieces, far_first, other_own))
        other_y = self.core(near_y[1])
        sum_x = pre(near_x, other_x)
        early_x = [sum_x[k].astype(low) for k in range(0, parts, 2)]
        pieces = [*far_first, *far_second]
        pieces = tie(pieces + [self.core(piece) for piece in pieces], early_x)
        sent_x = [self.along_x(a) for a in early_x]
        far = tie(call(3, pieces), sent_x, other_y)
        other_far = self.core(far[1])
        sum_y = pre(near_y, other_y)
        sent_y = [self.along_y(sum_y[k].astype(low)) for k in range(1, parts, 2)]
        sum_own = pre(own, other_own)
        sum_far = pre(far, other_far)
        totals, fill = [], filler()

        def send_far(k, before):
            via_x, via_y = tie([sum_far[j].astype(low) for j in (k, k + 1)], before)
            return self.along_x(via_x), self.along_y(via_y)

        coming = send_far(0, ())
        for k in range(0, parts, 2):
            far_y, far_x = tie(coming, sent_y[k // 2], totals[-1:])
            from_y = self.along_y((sum_y[k] + far_y.astype(wide)).astype(low))
            from_x = self.along_x((sum_x[k + 1] + far_x.astype(wide)).astype(low))
            if k + 2 < parts:
                coming = send_far(k + 2, coming)
                from_y, from_x = tie((from_y, from_x), coming)
            elif fill:
                from_y, from_x = tie((from_y, from_x), fill)
            both = [
                added(sum_own[k], sent_x[k // 2]) + from_y.astype(wide),
                added(sum_own[k + 1], sent_y[k // 2]) + from_x.astype(wide),
            ]
            totals.append(jnp.concatenate(both, axis=1).astype(low))
        return totals


def per_device(
    states,
    teacher,
    lengths,
    routes,
    gate_weights,
    w_qkv,
    w_out,
    norm_gains,
    qk_gains,
    w_gate_up,
    w_down,
):
    seq_count, slot_count, width = states.shape
    top_count = routes.shape[-1]
    ctx_size = lax.axis_size("ctx")
    tp_size = lax.axis_size("tp")
    shards = lax.axis_size(plane)
    ctx_index = lax.axis_index("ctx")
    tp_index = lax.axis_index("tp")
    plane_index = lax.axis_index(plane)
    tokens = seq_count * slot_count
    part = tokens // tp_size
    shard_experts = w_gate_up.shape[0]
    hidden_local = w_gate_up.shape[3]
    experts = shard_experts * shards
    capacity = 5 * tokens * top_count // (4 * experts)
    own_slots = jnp.arange(slot_count, dtype=jnp.int32)
    position = ctx_index * slot_count + own_slots
    tok_position = jnp.tile(position, seq_count)
    row_valid = (position[None, :] < lengths[:, None]).reshape(tokens).astype(wide)
    mirror = [(i, (i + 1) % ctx_size) for i in range(ctx_size)]

    gain_cols, head_cols = norm_gains.shape[1], qk_gains.shape[1]
    small = jnp.concatenate(
        [
            norm_gains.astype(wide).reshape(-1),
            qk_gains.astype(wide).reshape(-1),
            jnp.sum(lengths).astype(wide)[None],
        ]
    )
    places = Plane()
    small_all = places.gather_whole(small[None])
    gain_rows = small_all[:, : 2 * gain_cols].reshape(shards, 2, gain_cols)
    full_gains = jnp.swapaxes(gain_rows, 0, 1).reshape(2, shards * gain_cols)
    head_rows = small_all[:, 2 * gain_cols : 2 * (gain_cols + head_cols)]
    qk_float = jnp.swapaxes(head_rows.reshape(shards, 2, head_cols), 0, 1).reshape(
        2, shards * head_cols
    )
    valid_count = jnp.sum(small_all[:, -1]) / ctx_size
    gain_attn, gain_ffn = full_gains[0], full_gains[1]
    head_dim = qk_float.shape[1]
    heads_local = w_qkv.shape[2] // head_dim
    score_scale = head_dim ** (-0.5)

    tables = route_tables(
        routes.reshape(tokens, top_count), gate_weights.reshape(tokens, top_count), experts
    )
    table = lax.all_to_all(tables, plane, split_axis=0, concat_axis=0, tiled=True).reshape(
        shards, shard_experts, 2, tokens
    )
    rank = table[:, :, 0].astype(jnp.int32)
    offset = (jnp.arange(shard_experts, dtype=jnp.int32) * capacity)[None, :, None]
    place = jnp.swapaxes(jnp.where(rank >= 0, rank + offset, -1), 1, 2)
    w_up = w_gate_up.reshape(shard_experts, width, 2 * hidden_local)
    order = places.order()
    sort = lambda a: jnp.concatenate(
        [lax.dynamic_slice_in_dim(a, block, 1, 0) for block in order], axis=0
    )
    table, place = sort(table), sort(place)
    half_table = jnp.swapaxes(
        table.reshape(shards, shard_experts, 2, tp_size, 2, part // 2), 3, 4
    ).reshape(table.shape)
    pair = lambda a, c: a[2 * c : 2 * c + 2]
    parts = 4

    full_qkv = lax.all_gather(w_qkv.reshape(w_qkv.shape[0], -1), plane, axis=0, tiled=True)
    rows_out = tie(line_gather(w_out), full_qkv[:1])
    full_out = lax.all_gather(rows_out, plane, axis=1, tiled=True)
    flat_states = states.astype(wide).reshape(tokens, width)
    normed = rms_norm(flat_states, gain_attn).astype(low)
    projected = jnp.dot(normed, full_qkv, preferred_element_type=wide).reshape(
        tokens, 3, heads_local, head_dim
    )

    def prepare_local(projected_in, gains_in):
        return prepare(projected_in, gains_in, tok_position)

    (queries, key_states, values), prepare_back = jax.vjp(prepare_local, projected, qk_float)
    query_low = queries.astype(low).reshape(seq_count, slot_count, heads_local, head_dim)
    key_value = (
        jnp.stack([key_states, values], axis=1)
        .astype(low)
        .reshape(seq_count, slot_count, 2, heads_local, head_dim)
    )
    other_kv = lax.ppermute(key_value, "ctx", mirror)
    gathered = jnp.concatenate([key_value, other_kv], axis=1)
    other_position = (1 - ctx_index) * slot_count + own_slots
    key_position = jnp.concatenate([position, other_position])
    key_valid = key_position[None, :] < lengths[:, None]
    pieces = [
        attend_sequence(query_low[i], gathered[i], key_valid[i], score_scale)
        for i in range(seq_count)
    ]
    attended_low = (
        jnp.stack([p[0] for p in pieces]).astype(low).reshape(tokens, heads_local * head_dim)
    )
    begin = tp_index * part
    own = lambda a: lax.dynamic_slice_in_dim(a, begin, part, 0)
    attended_own = lax.all_to_all(
        attended_low, "tp", split_axis=0, concat_axis=1, tiled=True
    )
    states_own = own(flat_states)
    middle_own = states_own + jnp.dot(attended_own, full_out, preferred_element_type=wide)
    normed_own = rms_norm(middle_own, gain_ffn).astype(low)

    both_halves = lambda a: [
        lax.all_gather(half, "tp", axis=0, tiled=True) for half in (a[: part // 2], a[part // 2 :])
    ]
    saved = [()]

    def forward(chunk, pieces):
        made, saved[0] = expert_call(
            chunk, pieces, pair(half_table, chunk), pair(place, chunk), w_up, w_down, None, saved[0],
            capacity, shards,
        )
        return made

    def finish(sums):
        ready = [
            lax.psum_scatter(total, "tp", scatter_dimension=0, tiled=True) for total in sums
        ]
        return jnp.concatenate(ready, axis=1).astype(wide)

    mixture = finish(
        places.experts(*both_halves(normed_own), forward, parts)
    )
    rows_in, gate_up, hidden = saved[0]
    final_own = middle_own + mixture
    difference = final_own - own(teacher.reshape(tokens, width)).astype(wide)
    valid_own = own(row_valid)
    local_loss = jnp.sum(valid_own * jnp.sum(difference * difference, axis=-1))
    grad_final = 2.0 * loss_scale / valid_count * valid_own[:, None] * difference
    activations = lax.all_gather(final_own.astype(low), "tp", axis=0, tiled=True).reshape(
        seq_count, slot_count, width
    )

    grad_low = grad_final.astype(low)
    saved[0] = ()

    def backward(chunk, pieces):
        made, saved[0] = expert_call(
            chunk, pieces, pair(half_table, chunk), pair(place, chunk), w_up, w_down, gate_up,
            saved[0], capacity, shards,
        )
        if chunk == 1:
            made = tie(made, activations)
        return made

    def weight_grads():
        rows_back, grad_rows = saved[0]
        grad_up = jnp.einsum(
            "ebcd,ebcf->edf", rows_in, grad_rows, preferred_element_type=wide
        ).reshape(shard_experts, width, 2, hidden_local)
        made.append(grad_up)
        made.append(
            jnp.einsum("ebcf,ebcd->efd", hidden, rows_back, preferred_element_type=wide)
        )
        return [made[1]]

    made = []
    sums = places.experts(*both_halves(grad_low), backward, parts, weight_grads)
    if not made:
        weight_grads()
    grad_gate_up, grad_down = made
    grad_ffn = tie(finish(sums), grad_gate_up, grad_down)

    grad_middle_norm, grad_gain_ffn = norm_back(grad_ffn, middle_own, gain_ffn)
    grad_middle = grad_final + grad_middle_norm
    grad_branch = grad_middle.astype(low)

    grad_attended = lax.all_to_all(
        nt_dot(grad_branch, full_out).astype(low), "tp", split_axis=1, concat_axis=0, tiled=True
    )
    branch_block = lax.all_gather(grad_branch, "tp", axis=0, tiled=True)
    grad_w_out = jnp.einsum("nd,nf->df", branch_block, attended_low, preferred_element_type=wide)
    grad_heads = grad_attended.reshape(seq_count, slot_count, heads_local, head_dim)
    backs = [
        back_sequence(
            query_low[i], gathered[i], key_valid[i], pieces[i][1], grad_heads[i], score_scale
        )
        for i in range(seq_count)
    ]
    grad_query = jnp.stack([b[0] for b in backs])
    grad_kv = jnp.stack([b[1] for b in backs])
    sent_kv = grad_kv[:, slot_count:].astype(low)
    own_kv = grad_kv[:, :slot_count] + lax.ppermute(sent_kv, "ctx", mirror).astype(wide)
    grad_projected, grad_qk = prepare_back(
        (
            grad_query.reshape(tokens, heads_local, head_dim),
            own_kv[:, :, 0].reshape(tokens, heads_local, head_dim),
            own_kv[:, :, 1].reshape(tokens, heads_local, head_dim),
        )
    )
    grad_proj_low = grad_projected.astype(low).reshape(tokens, -1)
    grad_normed = lax.psum_scatter(
        nt_dot(grad_proj_low, full_qkv).astype(low),
        "tp",
        scatter_dimension=0,
        tiled=True,
    ).astype(wide)
    grad_w_qkv = jnp.einsum("nd,nk->dk", normed, grad_proj_low, preferred_element_type=wide)
    grad_states_norm, grad_gain_attn = norm_back(grad_normed, states_own, gain_attn)
    grad_states = (
        lax.all_gather((grad_middle + grad_states_norm).astype(low), "tp", axis=0, tiled=True)
        .astype(wide)
        .reshape(seq_count, slot_count, width)
    )
    sums = sum_everywhere(
        jnp.concatenate([grad_gain_attn, grad_gain_ffn, grad_qk.reshape(-1), local_loss[None]])
    )
    out_gains = lax.dynamic_slice_in_dim(
        sums[: 2 * width].reshape(2, width), plane_index * gain_cols, gain_cols, 1
    )
    out_qk = lax.dynamic_slice_in_dim(
        sums[2 * width : 2 * (width + head_dim)].reshape(2, head_dim),
        plane_index * head_cols,
        head_cols,
        1,
    )
    loss_value = sums[-1] / valid_count
    weights_own = places.reduce_whole(
        jnp.concatenate([grad_w_qkv.astype(low), grad_w_out.astype(low)], axis=1)
    )
    qkv_cols = grad_w_qkv.shape[1]
    out_qkv = weights_own[:, :qkv_cols].reshape(w_qkv.shape)
    out_w_out = weights_own[:, qkv_cols:].T
    return (
        activations,
        loss_value,
        valid_count,
        grad_states,
        out_qkv,
        out_w_out,
        out_gains,
        out_qk,
        grad_gate_up,
        grad_down,
    )


def solution(mesh):
    placed = (
        P("fsdp", "ctx", None),
        P("fsdp", "ctx", None),
        P("fsdp"),
        P("fsdp", "ctx", None),
        P("fsdp", "ctx", None),
        P(("fsdp", "ctx"), None, "tp"),
        P("tp", ("fsdp", "ctx")),
        P(None, ("fsdp", "ctx")),
        P(None, ("fsdp", "ctx")),
        P(("fsdp", "ctx"), None, None, "tp"),
        P(("fsdp", "ctx"), "tp", None),
    )
    return jax.shard_map(
        per_device,
        mesh=mesh,
        in_specs=placed,
        out_specs=(
            P("fsdp", "ctx", None),
            P(),
            P(),
            P("fsdp", "ctx", None),
            P(("fsdp", "ctx"), None, "tp"),
            P("tp", ("fsdp", "ctx")),
            P(None, ("fsdp", "ctx")),
            P(None, ("fsdp", "ctx")),
            P(("fsdp", "ctx"), None, None, "tp"),
            P(("fsdp", "ctx"), "tp", None),
        ),
        check_vma=False,
    )
```

```python
import functools

import jax
import jax.numpy as jnp
from jax import lax
from jax.experimental.layout import Layout, with_layout_constraint
from jax.experimental import pallas as pl
from jax.experimental.pallas import tpu as pltpu
from jax.sharding import PartitionSpec as P

norm_eps = 1e-05
rope_base = 10000.0
loss_scale = 4096.0
masked_score = -1e30
plane = ("fsdp", "ctx")
everywhere = ("fsdp", "ctx", "tp")
low = jnp.bfloat16
wide = jnp.float32


def rms_norm(values, gain_vec):
    return (
        values * lax.rsqrt(jnp.mean(values * values, axis=-1, keepdims=True) + norm_eps) * gain_vec
    )


def norm_back(grad_normed, values, gain_vec):
    inverse = lax.rsqrt(jnp.mean(values * values, axis=-1, keepdims=True) + norm_eps)
    scaled = values * inverse
    grad_scaled = grad_normed * gain_vec
    grad_values = inverse * (
        grad_scaled - scaled * jnp.mean(grad_scaled * scaled, axis=-1, keepdims=True)
    )
    return (grad_values, jnp.sum(grad_normed * scaled, axis=0))


def rotate(values, position):
    half_dim = values.shape[-1] // 2
    frequency = rope_base ** (-2.0 * jnp.arange(half_dim, dtype=wide) / values.shape[-1])
    angles = position.astype(wide)[:, None] * frequency[None, :]
    cosine = jnp.cos(angles)[:, None, :]
    sine_part = jnp.sin(angles)[:, None, :]
    first_half = values[..., :half_dim]
    second_half = values[..., half_dim:]
    return jnp.concatenate(
        [
            first_half * cosine - second_half * sine_part,
            second_half * cosine + first_half * sine_part,
        ],
        axis=-1,
    )


def prepare(projected, qk_float, position):
    queries = rotate(rms_norm(projected[:, 0], qk_float[0]), position)
    key_states = rotate(rms_norm(projected[:, 1], qk_float[1]), position)
    return (queries, key_states, projected[:, 2])


def attend_sequence(query_seq, kv_seq, valid_seq, score_scale):
    scores = (
        jnp.einsum("qhd,khd->hqk", query_seq, kv_seq[:, 0], preferred_element_type=wide)
        * score_scale
    )
    scores = jnp.where(valid_seq[None, None, :], scores, masked_score)
    peak_score = jnp.max(scores, axis=-1, keepdims=True)
    exponent = jnp.exp(scores - peak_score)
    row_total = jnp.sum(exponent, axis=-1, keepdims=True)
    probability = (exponent / row_total).astype(low)
    output = jnp.einsum("hqk,khd->qhd", probability, kv_seq[:, 1], preferred_element_type=wide)
    return (output, (peak_score + jnp.log(row_total))[..., 0])


def back_sequence(query_seq, kv_seq, valid_seq, log_seq, grad_seq, score_scale):
    scores = (
        jnp.einsum("qhd,khd->hqk", query_seq, kv_seq[:, 0], preferred_element_type=wide)
        * score_scale
    )
    scores = jnp.where(valid_seq[None, None, :], scores, masked_score)
    probability = jnp.exp(scores - log_seq[..., None])
    grad_prob = jnp.einsum("qhd,khd->hqk", grad_seq, kv_seq[:, 1], preferred_element_type=wide)
    grad_scores = (
        probability * (grad_prob - jnp.sum(probability * grad_prob, axis=-1, keepdims=True))
    ).astype(low)
    grad_query = (
        jnp.einsum("hqk,khd->qhd", grad_scores, kv_seq[:, 0], preferred_element_type=wide)
        * score_scale
    )
    grad_key = (
        jnp.einsum("hqk,qhd->khd", grad_scores, query_seq, preferred_element_type=wide)
        * score_scale
    )
    grad_value = jnp.einsum(
        "hqk,qhd->khd", probability.astype(low), grad_seq, preferred_element_type=wide
    )
    return (grad_query, jnp.stack([grad_key, grad_value], axis=1))


def route_tables(route_rows, gate_rows, experts):
    slots = route_rows.shape[0]
    hit = route_rows[None, :, :] == jnp.arange(experts, dtype=jnp.int32)[:, None, None]
    named = jnp.sum(hit.astype(wide), axis=-1)
    gates = jnp.sum(jnp.where(hit, gate_rows[None, :, :], 0.0), axis=-1)
    order = jnp.arange(slots, dtype=jnp.int32)
    before = (order[:, None] < order[None, :]).astype(low)
    rank = jnp.dot(named.astype(low), before, preferred_element_type=wide)
    return jnp.stack([jnp.where(named > 0.0, rank, -1.0), gates], axis=1)


def pick_rows(table_ref, block, capacity, slots):
    rank = table_ref[block, 0, 0:1, :].astype(jnp.int32)
    gate = table_ref[block, 0, 1:2, :]
    match = lax.broadcasted_iota(jnp.int32, (capacity, slots), 0) == rank
    chosen = jnp.where(match, 1.0, 0.0).astype(low)
    weight = jnp.sum(jnp.where(match, gate, 0.0), axis=1, keepdims=True)
    return (chosen, weight)


def spread_rows(place_ref, block, experts, capacity, slots):
    column = lax.broadcasted_iota(jnp.int32, (slots, experts * capacity), 1)
    match = column == place_ref[block, :, 0:1]
    for expert in range(1, experts):
        match = match | (column == place_ref[block, :, expert : expert + 1])
    return jnp.where(match, 1.0, 0.0).astype(low)


def nt_dot(left, right):
    return lax.dot_general(left, right, (((1,), (1,)), ((), ())), preferred_element_type=wide)


def tiles_of(width, most=512):
    step = min(width, most)
    return [slice(begin, begin + step) for begin in range(0, width, step)]


def take_rows(x_refs, table_ref, rows_ref):
    blocks, capacity, width = rows_ref.shape[1:]
    slots = table_ref.shape[3]
    weights, place = [], 0
    for block in range(blocks):
        chosen, weight = pick_rows(table_ref, block, capacity, slots)
        weights.append(weight)
        done = 0
        while done < width:
            x_ref = x_refs[place]
            for cut in tiles_of(x_ref.shape[1]):
                rows_ref[0, block, :, done + cut.start : done + cut.stop] = jnp.dot(
                    chosen, x_ref[:, cut], preferred_element_type=wide
                ).astype(low)
            done, place = done + x_ref.shape[1], place + 1
    return (rows_ref[0].reshape(blocks * capacity, width), jnp.concatenate(weights, axis=0))


def fill_spread(place_ref, spread_ref, capacity):
    blocks, slots, total = spread_ref.shape
    for block in range(blocks):
        spread_ref[block] = spread_rows(place_ref, block, total // capacity, capacity, slots)


def combine_blocks(spread_ref, y_ref, out_refs):
    for block, out_ref in enumerate(out_refs):
        for cut in tiles_of(y_ref.shape[2]):
            out_ref[:, cut] = jnp.dot(
                spread_ref[block], y_ref[block, :, cut], preferred_element_type=wide
            ).astype(low)


def forward_body(n_x, n_out, n_keep, *refs):
    x_refs, refs = refs[:n_x], refs[n_x:]
    (table_ref, place_ref, up_ref, down_ref), refs = refs[:4], refs[4 + n_keep :]
    out_refs, (rows_ref, gate_up_ref, hidden_ref, y_ref, spread_ref) = refs[:n_out], refs[n_out:]
    expert = pl.program_id(0)
    blocks, capacity, width = rows_ref.shape[1:]
    experts = y_ref.shape[1] // capacity

    @pl.when(expert == 0)
    def _():
        fill_spread(place_ref, spread_ref, capacity)

    half = down_ref.shape[1]
    rows, weight = take_rows(x_refs, table_ref, rows_ref)
    gate_up = jnp.dot(rows, up_ref[0], preferred_element_type=wide)
    gate_up_ref[0] = gate_up.reshape(blocks, capacity, 2 * half)
    gate_part = gate_up[:, :half]
    up_part = gate_up[:, half:]
    hidden = (gate_part * jax.nn.sigmoid(gate_part) * up_part * weight).astype(low)
    hidden_ref[0] = hidden.reshape(blocks, capacity, half)
    begin = pl.multiple_of(expert * capacity, 16)
    for cut in tiles_of(width):
        y_ref[:, pl.ds(begin, capacity), cut] = (
            jnp.dot(hidden, down_ref[0, :, cut], preferred_element_type=wide)
            .astype(low)
            .reshape(blocks, capacity, -1)
        )

    @pl.when(expert == experts - 1)
    def _():
        combine_blocks(spread_ref, y_ref, out_refs)


def backward_body(n_x, n_out, n_keep, *refs):
    x_refs, refs = refs[:n_x], refs[n_x:]
    (table_ref, place_ref, up_ref, down_ref, gate_up_ref), refs = refs[:5], refs[5 + n_keep :]
    out_refs, (rows_ref, grad_ref, y_ref, spread_ref) = refs[:n_out], refs[n_out:]
    expert = pl.program_id(0)
    blocks, capacity, width = rows_ref.shape[1:]
    experts = y_ref.shape[1] // capacity

    @pl.when(expert == 0)
    def _():
        fill_spread(place_ref, spread_ref, capacity)

    half = down_ref.shape[1]
    rows, weight = take_rows(x_refs, table_ref, rows_ref)
    grad_hidden = nt_dot(rows, down_ref[0]) * weight
    gate_up = gate_up_ref[0].reshape(blocks * capacity, 2 * half)
    gate_part = gate_up[:, :half]
    up_part = gate_up[:, half:]
    sigmoid = jax.nn.sigmoid(gate_part)
    grad_gate = grad_hidden * up_part * sigmoid * (1.0 + gate_part * (1.0 - sigmoid))
    grad_up = grad_hidden * gate_part * sigmoid
    grad_rows = jnp.concatenate([grad_gate, grad_up], axis=1).astype(low)
    grad_ref[0] = grad_rows.reshape(blocks, capacity, 2 * half)
    begin = pl.multiple_of(expert * capacity, 16)
    for cut in tiles_of(width):
        y_ref[:, pl.ds(begin, capacity), cut] = (
            nt_dot(grad_rows, up_ref[0, cut, :]).astype(low).reshape(blocks, capacity, -1)
        )

    @pl.when(expert == experts - 1)
    def _():
        combine_blocks(spread_ref, y_ref, out_refs)


def expert_call(begin, pieces, table, place, w_up, w_down, gate_up, kept, capacity, total):
    blocks, experts, _, slots = table.shape
    width = w_up.shape[1]
    double, half = w_up.shape[2], w_down.shape[1]
    backward = gate_up is not None
    once = pl.Buffered(1)
    row_spec = lambda last: pl.BlockSpec(
        (1, blocks, capacity, last), lambda e: (e, begin // blocks, 0, 0)
    )
    row_shape = lambda last, kind: jax.ShapeDtypeStruct((experts, total, capacity, last), kind)
    whole = lambda shape: pl.BlockSpec(shape, lambda e: (0,) * len(shape), pipeline_mode=once)
    in_specs = [whole(p.shape) for p in pieces] + [
        pl.BlockSpec((blocks, 1, 2, slots), lambda e: (0, e, 0, 0)),
        whole((blocks, slots, experts)),
        pl.BlockSpec((1, width, double), lambda e: (e, 0, 0)),
        pl.BlockSpec((1, half, width), lambda e: (e, 0, 0)),
    ]
    operands = [*pieces, table, place, w_up, w_down]
    n_out = blocks
    out_specs = [whole((slots, width))] * n_out + [row_spec(width), row_spec(double)]
    out_shape = [jax.ShapeDtypeStruct((slots, width), low)] * n_out + [row_shape(width, low)]
    if backward:
        in_specs.append(row_spec(double))
        operands.append(gate_up)
        out_shape.append(row_shape(double, low))
    else:
        out_specs.append(row_spec(half))
        out_shape += [row_shape(double, wide), row_shape(half, low)]
    aliases = {len(operands) + i: n_out + i for i in range(len(kept))}
    rows = experts * blocks * capacity
    body = functools.partial(
        backward_body if backward else forward_body, len(pieces), n_out, len(kept)
    )
    made = pl.pallas_call(
        body,
        grid=(experts,),
        in_specs=in_specs + [pl.BlockSpec(memory_space=pl.ANY)] * len(kept),
        out_specs=out_specs,
        out_shape=out_shape,
        input_output_aliases=aliases,
        scratch_shapes=[
            pltpu.VMEM((blocks, experts * capacity, width), low),
            pltpu.VMEM((blocks, slots, experts * capacity), low),
        ],
        compiler_params=pltpu.CompilerParams(
            dimension_semantics=("arbitrary",), vmem_limit_bytes=56 << 20
        ),
        cost_estimate=pl.CostEstimate(
            flops=2 * rows * width * (2 * slots + double + half),
            bytes_accessed=4 * blocks * slots * width + rows * (2 * width + 6 * double),
            transcendentals=rows * half,
        ),
    )(*operands, *kept)
    return (made[:n_out], made[n_out:])


def added(left, right):
    return left.astype(wide) + right.astype(wide)


def tie(values, *anchors):
    return lax.optimization_barrier((values, anchors))[0]


def sum_everywhere(values):
    values = values[None]
    for axis in everywhere:
        size, step = lax.axis_size(axis), 1
        while step < size:
            pairs = [(i, i ^ step) for i in range(size)]
            values = values + lax.ppermute(values, axis, pairs)
            step *= 2
    return values[0]


def line_gather(shard):
    size = lax.axis_size("tp")
    if size > 4:
        return lax.all_gather(shard, "tp", axis=0, tiled=True)
    move = lambda d: lax.ppermute(
        shard, "tp", [(i, i + d) for i in range(size) if 0 <= i + d < size]
    )
    near = [move(d) for d in range(size - 1, 0, -1)] + [shard] + [move(-d) for d in range(1, size)]
    rows = shard.shape[0]
    begin = (size - 1 - lax.axis_index("tp")) * rows
    return lax.dynamic_slice_in_dim(jnp.concatenate(near, axis=0), begin, size * rows, 0)


class Plane:
    def __init__(self):
        self.fsdp, self.ctx = lax.axis_size("fsdp"), lax.axis_size("ctx")
        self.tree = self.fsdp == 4 and self.ctx == 2
        self.shards = self.fsdp * self.ctx

    def core(self, a):
        return lax.ppermute(a, "fsdp", [(i, i ^ 1) for i in range(self.fsdp)])

    def along_x(self, a):
        return lax.ppermute(a, "fsdp", [(i, i ^ 2) for i in range(self.fsdp)])

    def along_y(self, a):
        return lax.ppermute(a, "ctx", [(i, i ^ 1) for i in range(self.ctx)])

    def order(self):
        if not self.tree:
            return list(range(self.shards))
        fsdp, ctx = lax.axis_index("fsdp"), lax.axis_index("ctx")
        chips = ((0, 0), (1, 0), (0, 1), (1, 1))
        return [(fsdp ^ (2 * x) ^ core) * 2 + (ctx ^ y) for x, y in chips for core in (0, 1)]

    def gather_whole(self, shard):
        rows = shard.shape[0]
        if not self.tree:
            return lax.all_gather(shard, plane, axis=0, tiled=True)
        halves = (shard[: rows // 2], shard[rows // 2 :]) if rows > 1 else (shard,)
        x = [self.along_x(h) for h in halves]
        y = [self.along_y(h) for h in halves]
        far = [self.along_y(x[0])] + [self.along_x(h) for h in y[1:]]
        whole = jnp.zeros((self.shards * rows, *shard.shape[1:]), shard.dtype)
        order = self.order()
        for c, pieces in enumerate((halves, x, y, far)):
            for core in (0, 1):
                begin = order[2 * c + core] * rows
                for piece in pieces:
                    found = self.core(piece) if core else piece
                    whole = lax.dynamic_update_slice_in_dim(whole, found, begin, 0)
                    begin = begin + piece.shape[0]
        return whole

    def reduce_whole(self, partial):
        rows = partial.shape[0] // self.shards
        if not self.tree:
            return lax.psum_scatter(partial, plane, scatter_dimension=0, tiled=True).astype(wide)
        blocks = [lax.dynamic_slice_in_dim(partial, i * rows, rows, 0) for i in self.order()]
        pre = [added(blocks[2 * c], self.core(blocks[2 * c + 1])) for c in range(4)]
        cuts = tiles_of(partial.shape[1], partial.shape[1] // 2)
        return jnp.concatenate(
            [self.total(k, *[p[:, cut] for p in pre]) for k, cut in enumerate(cuts)], axis=1
        )

    def total(self, k, own, near_x, near_y, far):
        if k % 2 == 0:
            near_y = near_y + self.along_x(far.astype(low)).astype(wide)
        else:
            near_x = near_x + self.along_y(far.astype(low)).astype(wide)
        from_x, from_y = self.along_x(near_x.astype(low)), self.along_y(near_y.astype(low))
        return own + from_x.astype(wide) + from_y.astype(wide)

    def experts(self, first, second, call, filler, ready=()):
        if not self.tree:
            split = lambda a: jnp.split(lax.all_gather(a, plane, axis=0, tiled=True), self.shards)
            halves, made = list(zip(split(first), split(second), strict=True)), []
            for i in range(0, self.shards, 2):
                made += call(i, [*halves[i], *halves[i + 1]])
            return lax.psum_scatter(
                jnp.concatenate(made, axis=0), plane, scatter_dimension=0, tiled=True
            )
        parts, step = 4, first.shape[1] // 2
        middle = step
        pre = lambda made, other: [
            added(made[:, k * step : (k + 1) * step], other[:, k * step : (k + 1) * step])
            for k in range(parts)
        ]
        narrow = lambda a: a.astype(low)

        def beyond(x_half, y_half):
            return self.along_y(x_half[:, :middle]), self.along_x(y_half[:, middle:])

        x_first, y_first = self.along_x(first), self.along_y(first)
        second = tie(second, x_first, y_first, ready)
        own_pieces = [first, second, self.core(first), self.core(second)]
        far_first = beyond(x_first, y_first)
        x_second, y_second = self.along_x(second), self.along_y(second)
        over_x, over_y = self.core(x_first), self.core(y_first)
        own = tie(call(0, tie(own_pieces, over_x, over_y)), far_first)
        x_second, y_second = tie((x_second, y_second), own[0])
        far_second = beyond(x_second, y_second)
        far_pieces = [self.core(piece) for piece in far_first]
        over_y = [over_y, self.core(y_second)]
        near_x = call(2, [x_first, x_second, over_x, self.core(x_second)])
        near_x = tie(near_x, far_second, far_pieces, over_y)
        other_own, other_x = self.core(own[1]), self.core(near_x[1])
        far_pieces += [self.core(piece) for piece in far_second]
        near_y = tie(call(4, [y_first, y_second, *over_y]), other_own, other_x, far_pieces)
        other_y = self.core(near_y[1])
        sum_x, sum_y = pre(near_x[0], other_x), pre(near_y[0], other_y)
        early_x = [narrow(sum_x[k]) for k in (0, 2)]
        early_y = [narrow(sum_y[k]) for k in (1, 3)]
        last = call(6, tie([*far_first, *far_second, *far_pieces], early_x, early_y))
        sent_x = [self.along_x(a) for a in early_x]
        sent_y = [self.along_y(a) for a in early_y]
        last = tie(last, sent_x, sent_y)
        sum_far = pre(last[0], self.core(last[1]))
        sum_own = pre(own[0], other_own)
        fillers = iter(filler())
        far = [(self.along_y if k % 2 else self.along_x)(narrow(sum_far[k])) for k in range(parts)]
        far = tie(far, next(fillers))
        near = [
            self.along_x(narrow(added(sum_x[k], far[k])))
            if k % 2
            else self.along_y(narrow(added(sum_y[k], far[k])))
            for k in range(parts)
        ]
        near = tie(near, next(fillers))
        sent = [sent_x[0], sent_y[0], sent_x[1], sent_y[1]]
        return jnp.concatenate(
            [added(sum_own[k], sent[k]) + near[k].astype(wide) for k in range(parts)], axis=1
        ).astype(low)


def per_device(
    states,
    teacher,
    lengths,
    routes,
    gate_weights,
    w_qkv,
    w_out,
    norm_gains,
    qk_gains,
    w_gate_up,
    w_down,
):
    seq_count, slot_count, width = states.shape
    top_count = routes.shape[-1]
    ctx_size = lax.axis_size("ctx")
    tp_size = lax.axis_size("tp")
    shards = lax.axis_size(plane)
    ctx_index = lax.axis_index("ctx")
    tp_index = lax.axis_index("tp")
    plane_index = lax.axis_index(plane)
    tokens = seq_count * slot_count
    part = tokens // tp_size
    shard_experts = w_gate_up.shape[0]
    hidden_local = w_gate_up.shape[3]
    experts = shard_experts * shards
    capacity = 5 * tokens * top_count // (4 * experts)
    own_slots = jnp.arange(slot_count, dtype=jnp.int32)
    position = ctx_index * slot_count + own_slots
    tok_position = jnp.tile(position, seq_count)
    row_valid = (position[None, :] < lengths[:, None]).reshape(tokens).astype(wide)
    mirror = [(i, (i + 1) % ctx_size) for i in range(ctx_size)]

    gain_cols, head_cols = norm_gains.shape[1], qk_gains.shape[1]
    small = jnp.concatenate(
        [
            norm_gains.astype(wide).reshape(-1),
            qk_gains.astype(wide).reshape(-1),
            jnp.sum(lengths).astype(wide)[None],
        ]
    )
    places = Plane()
    small_all = places.gather_whole(small[None])
    gain_rows = small_all[:, : 2 * gain_cols].reshape(shards, 2, gain_cols)
    full_gains = jnp.swapaxes(gain_rows, 0, 1).reshape(2, shards * gain_cols)
    head_rows = small_all[:, 2 * gain_cols : 2 * (gain_cols + head_cols)]
    qk_float = jnp.swapaxes(head_rows.reshape(shards, 2, head_cols), 0, 1).reshape(
        2, shards * head_cols
    )
    valid_count = jnp.sum(small_all[:, -1]) / ctx_size
    gain_attn, gain_ffn = full_gains[0], full_gains[1]
    head_dim = qk_float.shape[1]
    heads_local = w_qkv.shape[2] // head_dim
    score_scale = head_dim ** (-0.5)

    tables = route_tables(
        routes.reshape(tokens, top_count), gate_weights.reshape(tokens, top_count), experts
    )
    table = lax.all_to_all(tables, plane, split_axis=0, concat_axis=0, tiled=True).reshape(
        shards, shard_experts, 2, tokens
    )
    rank = table[:, :, 0].astype(jnp.int32)
    offset = (jnp.arange(shard_experts, dtype=jnp.int32) * capacity)[None, :, None]
    place = jnp.swapaxes(jnp.where(rank >= 0, rank + offset, -1), 1, 2)
    w_up = w_gate_up.reshape(shard_experts, width, 2 * hidden_local)
    order = places.order()
    sort = lambda a: jnp.concatenate(
        [lax.dynamic_slice_in_dim(a, block, 1, 0) for block in order], axis=0
    )
    table, place = sort(table), sort(place)
    some = lambda a, begin, pieces: a[begin : begin + blocks_in(pieces)]

    def blocks_in(pieces):
        return sum(piece.shape[1] for piece in pieces) // width

    full_qkv = lax.all_gather(
        w_qkv.reshape(w_qkv.shape[0], -1), plane, axis=0, tiled=True
    )
    rows_out = tie(line_gather(w_out), full_qkv[:1])
    full_out = lax.all_gather(rows_out, plane, axis=1, tiled=True)
    flat_states = states.astype(wide).reshape(tokens, width)
    normed = rms_norm(flat_states, gain_attn).astype(low)
    projected = jnp.dot(normed, full_qkv, preferred_element_type=wide).reshape(
        tokens, 3, heads_local, head_dim
    )

    def prepare_query(projected_in, gain):
        return rotate(rms_norm(projected_in, gain), tok_position)

    queries, query_back = jax.vjp(prepare_query, projected[:, 0], qk_float[0])
    key_states, key_back = jax.vjp(prepare_query, projected[:, 1], qk_float[1])
    query_low = queries.astype(low).reshape(seq_count, slot_count, heads_local, head_dim)
    key_value = (
        jnp.stack([key_states, projected[:, 2]], axis=1)
        .astype(low)
        .reshape(seq_count, slot_count, 2, heads_local, head_dim)
    )
    other_kv = lax.ppermute(key_value, "ctx", mirror)
    gathered = jnp.concatenate([key_value, other_kv], axis=1)
    other_position = (1 - ctx_index) * slot_count + own_slots
    key_position = jnp.concatenate([position, other_position])
    key_valid = key_position[None, :] < lengths[:, None]
    pieces = [
        attend_sequence(query_low[i], gathered[i], key_valid[i], score_scale)
        for i in range(seq_count)
    ]
    attended_low = (
        jnp.stack([p[0] for p in pieces]).astype(low).reshape(tokens, heads_local * head_dim)
    )
    begin = tp_index * part
    own = lambda a: lax.dynamic_slice_in_dim(a, begin, part, 0)
    attended_own = lax.all_to_all(
        attended_low, "tp", split_axis=0, concat_axis=1, tiled=True
    )
    states_own = own(flat_states)
    middle_own = states_own + jnp.dot(attended_own, full_out, preferred_element_type=wide)
    normed_own = rms_norm(middle_own, gain_ffn).astype(low)

    middle_col = width // 2
    cols = (slice(0, middle_col), slice(middle_col, width))

    def spread(*halves):
        return [lax.all_gather(half.astype(low), "tp", axis=0, tiled=True) for half in halves]

    saved = [()]

    def forward(begin, pieces):
        made, saved[0] = expert_call(
            begin, pieces, some(table, begin, pieces), some(place, begin, pieces), w_up, w_down,
            None, saved[0], capacity, shards,
        )
        return made

    def finish(half):
        return lax.psum_scatter(half, "tp", scatter_dimension=0, tiled=True).astype(wide)

    teacher_own = own(teacher.reshape(tokens, width)).astype(wide)
    valid_own = own(row_valid)
    grad_scale = (2.0 * loss_scale / valid_count * valid_own)[:, None]
    mixture = places.experts(
        *spread(normed_own[:, cols[0]], normed_own[:, cols[1]]),
        forward,
        lambda: ((), ()),
        (w_up, table, place),
    )
    rows_in, gate_up, hidden = saved[0]
    final_own = middle_own + finish(mixture)
    difference = final_own - teacher_own
    local_loss = jnp.sum(valid_own * jnp.sum(difference * difference, axis=-1))
    grad_final = grad_scale * difference
    spread_halves = spread(grad_final[:, cols[0]], grad_final[:, cols[1]])
    activations = lax.all_gather(final_own.astype(low), "tp", axis=0, tiled=True).reshape(
        seq_count, slot_count, width
    )

    saved[0] = ()

    def backward(begin, pieces):
        made, saved[0] = expert_call(
            begin, pieces, some(table, begin, pieces), some(place, begin, pieces), w_up, w_down,
            gate_up, saved[0], capacity, shards,
        )
        if begin == 2:
            made = tie(made, activations)
        return made

    def weight_grads():
        rows_back, grad_rows = saved[0]
        made.append(
            jnp.einsum("ebcf,ebcd->efd", hidden, rows_back, preferred_element_type=wide)
        )
        yield [made[0]]
        grad_up = jnp.einsum("ebcd,ebcf->edf", rows_in, grad_rows, preferred_element_type=wide)
        made.append(grad_up)
        yield [grad_up]

    made = []
    total_in = places.experts(*spread_halves, backward, weight_grads)
    if not made:
        for _ in weight_grads():
            pass
    grad_down, grad_up = made
    grad_gate_up = with_layout_constraint(
        grad_up.reshape(shard_experts, width, 2, hidden_local),
        Layout(major_to_minor=(0, 1, 2, 3)),
    )
    grad_ffn = tie(finish(total_in), grad_gate_up, grad_down)

    grad_middle_norm, grad_gain_ffn = norm_back(grad_ffn, middle_own, gain_ffn)
    grad_middle = grad_final + grad_middle_norm
    grad_branch = grad_middle.astype(low)

    grad_attended = lax.all_to_all(
        nt_dot(grad_branch, full_out).astype(low), "tp", split_axis=1, concat_axis=0, tiled=True
    )
    branch_block = lax.all_gather(grad_branch, "tp", axis=0, tiled=True)
    grad_w_out = jnp.einsum("nd,nf->df", branch_block, attended_low, preferred_element_type=wide)
    grad_heads = grad_attended.reshape(seq_count, slot_count, heads_local, head_dim)
    backs = [
        back_sequence(
            query_low[i], gathered[i], key_valid[i], pieces[i][1], grad_heads[i], score_scale
        )
        for i in range(seq_count)
    ]
    grad_query = jnp.stack([b[0] for b in backs])
    grad_kv = jnp.stack([b[1] for b in backs])
    sent_kv = grad_kv[:, slot_count:].astype(low)
    own_kv = grad_kv[:, :slot_count] + lax.ppermute(sent_kv, "ctx", mirror).astype(wide)
    grad_q, grad_q_gain = query_back(grad_query.reshape(tokens, heads_local, head_dim))
    grad_k, grad_k_gain = key_back(own_kv[:, :, 0].reshape(tokens, heads_local, head_dim))
    grad_v = own_kv[:, :, 1].reshape(tokens, heads_local, head_dim)
    flat = lambda a: a.astype(low).reshape(tokens, -1)
    grad_proj_low = jnp.concatenate([flat(grad_q), flat(grad_k), flat(grad_v)], axis=1)
    grad_qk = jnp.stack([grad_q_gain, grad_k_gain])
    grad_normed = lax.psum_scatter(
        nt_dot(grad_proj_low, full_qkv).astype(low),
        "tp",
        scatter_dimension=0,
        tiled=True,
    ).astype(wide)
    grad_w_qkv = jnp.einsum("nd,nk->dk", normed, grad_proj_low, preferred_element_type=wide)
    grad_states_norm, grad_gain_attn = norm_back(grad_normed, states_own, gain_attn)
    grad_states = (
        lax.all_gather((grad_middle + grad_states_norm).astype(low), "tp", axis=0, tiled=True)
        .astype(wide)
        .reshape(seq_count, slot_count, width)
    )
    sums = sum_everywhere(
        jnp.concatenate([grad_gain_attn, grad_gain_ffn, grad_qk.reshape(-1), local_loss[None]])
    )
    out_gains = lax.dynamic_slice_in_dim(
        sums[: 2 * width].reshape(2, width), plane_index * gain_cols, gain_cols, 1
    )
    out_qk = lax.dynamic_slice_in_dim(
        sums[2 * width : 2 * (width + head_dim)].reshape(2, head_dim),
        plane_index * head_cols,
        head_cols,
        1,
    )
    loss_value = sums[-1] / valid_count
    weights_own = places.reduce_whole(
        jnp.concatenate([grad_w_qkv.astype(low), grad_w_out.astype(low)], axis=1)
    )
    qkv_cols = grad_w_qkv.shape[1]
    out_qkv = weights_own[:, :qkv_cols].reshape(w_qkv.shape)
    out_w_out = weights_own[:, qkv_cols:].T
    return (
        activations,
        loss_value,
        valid_count,
        grad_states,
        out_qkv,
        out_w_out,
        out_gains,
        out_qk,
        grad_gate_up,
        grad_down,
    )


def solution(mesh):
    placed = (
        P("fsdp", "ctx", None),
        P("fsdp", "ctx", None),
        P("fsdp"),
        P("fsdp", "ctx", None),
        P("fsdp", "ctx", None),
        P(("fsdp", "ctx"), None, "tp"),
        P("tp", ("fsdp", "ctx")),
        P(None, ("fsdp", "ctx")),
        P(None, ("fsdp", "ctx")),
        P(("fsdp", "ctx"), None, None, "tp"),
        P(("fsdp", "ctx"), "tp", None),
    )
    return jax.shard_map(
        per_device,
        mesh=mesh,
        in_specs=placed,
        out_specs=(
            P("fsdp", "ctx", None),
            P(),
            P(),
            P("fsdp", "ctx", None),
            P(("fsdp", "ctx"), None, "tp"),
            P("tp", ("fsdp", "ctx")),
            P(None, ("fsdp", "ctx")),
            P(None, ("fsdp", "ctx")),
            P(("fsdp", "ctx"), None, None, "tp"),
            P(("fsdp", "ctx"), "tp", None),
        ),
        check_vma=False,
    )
```

```python
import functools

import jax
import jax.numpy as jnp
from jax import lax
from jax.experimental.layout import Layout, with_layout_constraint
from jax.experimental import pallas as pl
from jax.experimental.pallas import tpu as pltpu
from jax.sharding import PartitionSpec as P

norm_eps = 1e-05
rope_base = 10000.0
loss_scale = 4096.0
masked_score = -1e30
plane = ("fsdp", "ctx")
everywhere = ("fsdp", "ctx", "tp")
low = jnp.bfloat16
wide = jnp.float32


def rms_norm(values, gain_vec):
    return (
        values * lax.rsqrt(jnp.mean(values * values, axis=-1, keepdims=True) + norm_eps) * gain_vec
    )


def norm_back(grad_normed, values, gain_vec):
    inverse = lax.rsqrt(jnp.mean(values * values, axis=-1, keepdims=True) + norm_eps)
    scaled = values * inverse
    grad_scaled = grad_normed * gain_vec
    grad_values = inverse * (
        grad_scaled - scaled * jnp.mean(grad_scaled * scaled, axis=-1, keepdims=True)
    )
    return (grad_values, jnp.sum(grad_normed * scaled, axis=0))


def rotate(values, position):
    half_dim = values.shape[-1] // 2
    frequency = rope_base ** (-2.0 * jnp.arange(half_dim, dtype=wide) / values.shape[-1])
    angles = position.astype(wide)[:, None] * frequency[None, :]
    cosine = jnp.cos(angles)[:, None, :]
    sine_part = jnp.sin(angles)[:, None, :]
    first_half = values[..., :half_dim]
    second_half = values[..., half_dim:]
    return jnp.concatenate(
        [
            first_half * cosine - second_half * sine_part,
            second_half * cosine + first_half * sine_part,
        ],
        axis=-1,
    )


def prepare(projected, qk_float, position):
    queries = rotate(rms_norm(projected[:, 0], qk_float[0]), position)
    key_states = rotate(rms_norm(projected[:, 1], qk_float[1]), position)
    return (queries, key_states, projected[:, 2])


def attend_sequence(query_seq, key_seq, value_seq, valid_seq, score_scale):
    scores = (
        jnp.einsum("qhd,khd->hqk", query_seq, key_seq, preferred_element_type=wide)
        * score_scale
    )
    scores = jnp.where(valid_seq[None, None, :], scores, masked_score)
    peak_score = jnp.max(scores, axis=-1, keepdims=True)
    exponent = jnp.exp(scores - peak_score)
    row_total = jnp.sum(exponent, axis=-1, keepdims=True)
    probability = (exponent / row_total).astype(low)
    output = jnp.einsum("hqk,khd->qhd", probability, value_seq, preferred_element_type=wide)
    return (output, (peak_score + jnp.log(row_total))[..., 0])


def back_sequence(query_seq, key_seq, value_seq, valid_seq, log_seq, grad_seq, score_scale):
    scores = (
        jnp.einsum("qhd,khd->hqk", query_seq, key_seq, preferred_element_type=wide)
        * score_scale
    )
    scores = jnp.where(valid_seq[None, None, :], scores, masked_score)
    probability = jnp.exp(scores - log_seq[..., None])
    grad_prob = jnp.einsum("qhd,khd->hqk", grad_seq, value_seq, preferred_element_type=wide)
    grad_scores = (
        probability * (grad_prob - jnp.sum(probability * grad_prob, axis=-1, keepdims=True))
    ).astype(low)
    grad_query = (
        jnp.einsum("hqk,khd->qhd", grad_scores, key_seq, preferred_element_type=wide)
        * score_scale
    )
    grad_key = (
        jnp.einsum("hqk,qhd->khd", grad_scores, query_seq, preferred_element_type=wide)
        * score_scale
    )
    grad_value = jnp.einsum(
        "hqk,qhd->khd", probability.astype(low), grad_seq, preferred_element_type=wide
    )
    return (grad_query, grad_key, grad_value)


def route_tables(route_rows, gate_rows, experts):
    slots = route_rows.shape[0]
    hit = route_rows[None, :, :] == jnp.arange(experts, dtype=jnp.int32)[:, None, None]
    named = jnp.sum(hit.astype(wide), axis=-1)
    gates = jnp.sum(jnp.where(hit, gate_rows[None, :, :], 0.0), axis=-1)
    order = jnp.arange(slots, dtype=jnp.int32)
    before = (order[:, None] < order[None, :]).astype(low)
    rank = jnp.dot(named.astype(low), before, preferred_element_type=wide)
    return jnp.stack([jnp.where(named > 0.0, rank, -1.0), gates], axis=1)


def pick_rows(table_ref, block, capacity, slots):
    rank = table_ref[block, 0, 0:1, :].astype(jnp.int32)
    gate = table_ref[block, 0, 1:2, :]
    match = lax.broadcasted_iota(jnp.int32, (capacity, slots), 0) == rank
    chosen = jnp.where(match, 1.0, 0.0).astype(low)
    weight = jnp.sum(jnp.where(match, gate, 0.0), axis=1, keepdims=True)
    return (chosen, weight)


def spread_rows(place_ref, block, experts, capacity, slots):
    column = lax.broadcasted_iota(jnp.int32, (slots, experts * capacity), 1)
    match = column == place_ref[block, :, 0:1]
    for expert in range(1, experts):
        match = match | (column == place_ref[block, :, expert : expert + 1])
    return jnp.where(match, 1.0, 0.0).astype(low)


def nt_dot(left, right):
    return lax.dot_general(left, right, (((1,), (1,)), ((), ())), preferred_element_type=wide)


def tiles_of(width, most=512):
    step = min(width, most)
    return [slice(begin, begin + step) for begin in range(0, width, step)]


def take_rows(x_refs, table_ref, rows_ref):
    blocks, capacity, width = rows_ref.shape[1:]
    slots = table_ref.shape[3]
    weights, place = [], 0
    for block in range(blocks):
        chosen, weight = pick_rows(table_ref, block, capacity, slots)
        weights.append(weight)
        done = 0
        while done < width:
            x_ref = x_refs[place]
            for cut in tiles_of(x_ref.shape[1]):
                rows_ref[0, block, :, done + cut.start : done + cut.stop] = jnp.dot(
                    chosen, x_ref[:, cut], preferred_element_type=wide
                ).astype(low)
            done, place = done + x_ref.shape[1], place + 1
    return (rows_ref[0].reshape(blocks * capacity, width), jnp.concatenate(weights, axis=0))


def fill_spread(place_ref, spread_ref, capacity):
    blocks, slots, total = spread_ref.shape
    for block in range(blocks):
        spread_ref[block] = spread_rows(place_ref, block, total // capacity, capacity, slots)


def combine_blocks(spread_ref, y_ref, out_refs):
    for block, out_ref in enumerate(out_refs):
        for cut in tiles_of(y_ref.shape[2]):
            out_ref[:, cut] = jnp.dot(
                spread_ref[block], y_ref[block, :, cut], preferred_element_type=wide
            ).astype(low)


def forward_body(n_x, n_out, n_keep, *refs):
    x_refs, refs = refs[:n_x], refs[n_x:]
    (table_ref, place_ref, up_ref, down_ref), refs = refs[:4], refs[4 + n_keep :]
    out_refs, (rows_ref, gate_up_ref, hidden_ref, y_ref, spread_ref) = refs[:n_out], refs[n_out:]
    expert = pl.program_id(0)
    blocks, capacity, width = rows_ref.shape[1:]
    experts = y_ref.shape[1] // capacity

    @pl.when(expert == 0)
    def _():
        fill_spread(place_ref, spread_ref, capacity)

    half = down_ref.shape[1]
    rows, weight = take_rows(x_refs, table_ref, rows_ref)
    gate_up = jnp.dot(rows, up_ref[0], preferred_element_type=wide)
    gate_up_ref[0] = gate_up.reshape(blocks, capacity, 2 * half)
    gate_part = gate_up[:, :half]
    up_part = gate_up[:, half:]
    hidden = (gate_part * jax.nn.sigmoid(gate_part) * up_part * weight).astype(low)
    hidden_ref[0] = hidden.reshape(blocks, capacity, half)
    begin = pl.multiple_of(expert * capacity, 16)
    for cut in tiles_of(width):
        y_ref[:, pl.ds(begin, capacity), cut] = (
            jnp.dot(hidden, down_ref[0, :, cut], preferred_element_type=wide)
            .astype(low)
            .reshape(blocks, capacity, -1)
        )

    @pl.when(expert == experts - 1)
    def _():
        combine_blocks(spread_ref, y_ref, out_refs)


def backward_body(n_x, n_out, n_keep, *refs):
    x_refs, refs = refs[:n_x], refs[n_x:]
    (table_ref, place_ref, up_ref, down_ref, gate_up_ref), refs = refs[:5], refs[5 + n_keep :]
    out_refs, (rows_ref, grad_ref, y_ref, spread_ref) = refs[:n_out], refs[n_out:]
    expert = pl.program_id(0)
    blocks, capacity, width = rows_ref.shape[1:]
    experts = y_ref.shape[1] // capacity

    @pl.when(expert == 0)
    def _():
        fill_spread(place_ref, spread_ref, capacity)

    half = down_ref.shape[1]
    rows, weight = take_rows(x_refs, table_ref, rows_ref)
    grad_hidden = nt_dot(rows, down_ref[0]) * weight
    gate_up = gate_up_ref[0].reshape(blocks * capacity, 2 * half)
    gate_part = gate_up[:, :half]
    up_part = gate_up[:, half:]
    sigmoid = jax.nn.sigmoid(gate_part)
    grad_gate = grad_hidden * up_part * sigmoid * (1.0 + gate_part * (1.0 - sigmoid))
    grad_up = grad_hidden * gate_part * sigmoid
    grad_rows = jnp.concatenate([grad_gate, grad_up], axis=1).astype(low)
    grad_ref[0] = grad_rows.reshape(blocks, capacity, 2 * half)
    begin = pl.multiple_of(expert * capacity, 16)
    for cut in tiles_of(width):
        y_ref[:, pl.ds(begin, capacity), cut] = (
            nt_dot(grad_rows, up_ref[0, cut, :]).astype(low).reshape(blocks, capacity, -1)
        )

    @pl.when(expert == experts - 1)
    def _():
        combine_blocks(spread_ref, y_ref, out_refs)


def expert_call(begin, pieces, table, place, w_up, w_down, gate_up, kept, capacity, total):
    blocks, experts, _, slots = table.shape
    width = w_up.shape[1]
    double, half = w_up.shape[2], w_down.shape[1]
    backward = gate_up is not None
    once = pl.Buffered(1)
    row_spec = lambda last: pl.BlockSpec(
        (1, blocks, capacity, last), lambda e: (e, begin // blocks, 0, 0)
    )
    row_shape = lambda last, kind: jax.ShapeDtypeStruct((experts, total, capacity, last), kind)
    whole = lambda shape: pl.BlockSpec(shape, lambda e: (0,) * len(shape), pipeline_mode=once)
    in_specs = [whole(p.shape) for p in pieces] + [
        pl.BlockSpec((blocks, 1, 2, slots), lambda e: (0, e, 0, 0)),
        whole((blocks, slots, experts)),
        pl.BlockSpec((1, width, double), lambda e: (e, 0, 0)),
        pl.BlockSpec((1, half, width), lambda e: (e, 0, 0)),
    ]
    operands = [*pieces, table, place, w_up, w_down]
    n_out = blocks
    out_specs = [whole((slots, width))] * n_out + [row_spec(width), row_spec(double)]
    out_shape = [jax.ShapeDtypeStruct((slots, width), low)] * n_out + [row_shape(width, low)]
    if backward:
        in_specs.append(row_spec(double))
        operands.append(gate_up)
        out_shape.append(row_shape(double, low))
    else:
        out_specs.append(row_spec(half))
        out_shape += [row_shape(double, wide), row_shape(half, low)]
    aliases = {len(operands) + i: n_out + i for i in range(len(kept))}
    rows = experts * blocks * capacity
    body = functools.partial(
        backward_body if backward else forward_body, len(pieces), n_out, len(kept)
    )
    made = pl.pallas_call(
        body,
        grid=(experts,),
        in_specs=in_specs + [pl.BlockSpec(memory_space=pl.ANY)] * len(kept),
        out_specs=out_specs,
        out_shape=out_shape,
        input_output_aliases=aliases,
        scratch_shapes=[
            pltpu.VMEM((blocks, experts * capacity, width), low),
            pltpu.VMEM((blocks, slots, experts * capacity), low),
        ],
        compiler_params=pltpu.CompilerParams(
            dimension_semantics=("arbitrary",), vmem_limit_bytes=56 << 20
        ),
        cost_estimate=pl.CostEstimate(
            flops=2 * rows * width * (2 * slots + double + half),
            bytes_accessed=4 * blocks * slots * width + rows * (2 * width + 6 * double),
            transcendentals=rows * half,
        ),
    )(*operands, *kept)
    return (made[:n_out], made[n_out:])


def added(left, right):
    return left.astype(wide) + right.astype(wide)


def tie(values, *anchors):
    return lax.optimization_barrier((values, anchors))[0]


def sum_everywhere(values):
    values = values[None]
    for axis in everywhere:
        size, step = lax.axis_size(axis), 1
        while step < size:
            pairs = [(i, i ^ step) for i in range(size)]
            values = values + lax.ppermute(values, axis, pairs)
            step *= 2
    return values[0]


def line_gather(shard):
    size = lax.axis_size("tp")
    if size > 4:
        return lax.all_gather(shard, "tp", axis=0, tiled=True)
    move = lambda d: lax.ppermute(
        shard, "tp", [(i, i + d) for i in range(size) if 0 <= i + d < size]
    )
    near = [move(d) for d in range(size - 1, 0, -1)] + [shard] + [move(-d) for d in range(1, size)]
    rows = shard.shape[0]
    begin = (size - 1 - lax.axis_index("tp")) * rows
    return lax.dynamic_slice_in_dim(jnp.concatenate(near, axis=0), begin, size * rows, 0)


class Plane:
    def __init__(self):
        self.fsdp, self.ctx = lax.axis_size("fsdp"), lax.axis_size("ctx")
        self.tree = self.fsdp == 4 and self.ctx == 2
        self.shards = self.fsdp * self.ctx

    def core(self, a):
        return lax.ppermute(a, "fsdp", [(i, i ^ 1) for i in range(self.fsdp)])

    def along_x(self, a):
        return lax.ppermute(a, "fsdp", [(i, i ^ 2) for i in range(self.fsdp)])

    def along_y(self, a):
        return lax.ppermute(a, "ctx", [(i, i ^ 1) for i in range(self.ctx)])

    def order(self):
        if not self.tree:
            return list(range(self.shards))
        fsdp, ctx = lax.axis_index("fsdp"), lax.axis_index("ctx")
        chips = ((0, 0), (1, 0), (0, 1), (1, 1))
        return [(fsdp ^ (2 * x) ^ core) * 2 + (ctx ^ y) for x, y in chips for core in (0, 1)]

    def gather_whole(self, shard):
        rows = shard.shape[0]
        if not self.tree:
            return lax.all_gather(shard, plane, axis=0, tiled=True)
        halves = (shard[: rows // 2], shard[rows // 2 :]) if rows > 1 else (shard,)
        x = [self.along_x(h) for h in halves]
        y = [self.along_y(h) for h in halves]
        far = [self.along_y(x[0])] + [self.along_x(h) for h in y[1:]]
        whole = jnp.zeros((self.shards * rows, *shard.shape[1:]), shard.dtype)
        order = self.order()
        for c, pieces in enumerate((halves, x, y, far)):
            for core in (0, 1):
                begin = order[2 * c + core] * rows
                for piece in pieces:
                    found = self.core(piece) if core else piece
                    whole = lax.dynamic_update_slice_in_dim(whole, found, begin, 0)
                    begin = begin + piece.shape[0]
        return whole

    def reduce_whole(self, partial):
        rows = partial.shape[0] // self.shards
        if not self.tree:
            return lax.psum_scatter(partial, plane, scatter_dimension=0, tiled=True).astype(wide)
        blocks = [lax.dynamic_slice_in_dim(partial, i * rows, rows, 0) for i in self.order()]
        pre = [added(blocks[2 * c], self.core(blocks[2 * c + 1])) for c in range(4)]
        cuts = tiles_of(partial.shape[1], partial.shape[1] // 2)
        return jnp.concatenate(
            [self.total(k, *[p[:, cut] for p in pre]) for k, cut in enumerate(cuts)], axis=1
        )

    def total(self, k, own, near_x, near_y, far):
        if k % 2 == 0:
            near_y = near_y + self.along_x(far.astype(low)).astype(wide)
        else:
            near_x = near_x + self.along_y(far.astype(low)).astype(wide)
        from_x, from_y = self.along_x(near_x.astype(low)), self.along_y(near_y.astype(low))
        return own + from_x.astype(wide) + from_y.astype(wide)

    def experts(self, first, second, call, filler):
        if not self.tree:
            split = lambda a: jnp.split(lax.all_gather(a, plane, axis=0, tiled=True), self.shards)
            halves, made = list(zip(split(first), split(second), strict=True)), []
            for i in range(0, self.shards, 2):
                made += call(i, [*halves[i], *halves[i + 1]])
            return lax.psum_scatter(
                jnp.concatenate(made, axis=0), plane, scatter_dimension=0, tiled=True
            )
        step = first.shape[1]
        pre = lambda made, other: [
            added(made[:, k * step : (k + 1) * step], other[:, k * step : (k + 1) * step])
            for k in range(2)
        ]
        narrow = lambda a: a.astype(low)
        x_first, y_first = self.along_x(first), self.along_y(first)
        second = tie(second, x_first, y_first)
        own_pieces = [first, second, self.core(first), self.core(second)]
        x_second, y_second = self.along_x(second), self.along_y(second)
        over_x, over_y = self.core(x_first), self.core(y_first)
        own = call(0, tie(own_pieces, over_x, over_y))
        x_second, y_second = tie((x_second, y_second), own[0])
        far = [self.along_y(x_first), self.along_x(y_second)]
        over_y = [over_y, self.core(y_second)]
        near_x = call(2, [x_first, x_second, over_x, self.core(x_second)])
        near_x = tie(near_x, far, over_y)
        other_own, other_x = self.core(own[1]), self.core(near_x[1])
        far += [self.core(piece) for piece in far]
        near_y = tie(call(4, [y_first, y_second, *over_y]), other_own, other_x, far)
        other_y = self.core(near_y[1])
        sum_x, sum_y = pre(near_x[0], other_x), pre(near_y[0], other_y)
        early_x, early_y = narrow(sum_x[0]), narrow(sum_y[1])
        last = call(6, tie(far, early_x, early_y))
        sent = [self.along_x(early_x), self.along_y(early_y)]
        last = tie(last, sent)
        sum_far = pre(last[0], self.core(last[1]))
        sum_own = pre(own[0], other_own)
        fillers = iter(filler())
        far = [self.along_x(narrow(sum_far[0])), self.along_y(narrow(sum_far[1]))]
        far = tie(far, next(fillers))
        near = [
            self.along_y(narrow(added(sum_y[0], far[0]))),
            self.along_x(narrow(added(sum_x[1], far[1]))),
        ]
        near = tie(near, next(fillers))
        return jnp.concatenate(
            [added(sum_own[k], sent[k]) + near[k].astype(wide) for k in range(2)], axis=1
        ).astype(low)


def per_device(
    states,
    teacher,
    lengths,
    routes,
    gate_weights,
    w_qkv,
    w_out,
    norm_gains,
    qk_gains,
    w_gate_up,
    w_down,
):
    seq_count, slot_count, width = states.shape
    top_count = routes.shape[-1]
    ctx_size = lax.axis_size("ctx")
    tp_size = lax.axis_size("tp")
    shards = lax.axis_size(plane)
    ctx_index = lax.axis_index("ctx")
    tp_index = lax.axis_index("tp")
    plane_index = lax.axis_index(plane)
    tokens = seq_count * slot_count
    part = tokens // tp_size
    shard_experts = w_gate_up.shape[0]
    hidden_local = w_gate_up.shape[3]
    experts = shard_experts * shards
    capacity = 5 * tokens * top_count // (4 * experts)
    own_slots = jnp.arange(slot_count, dtype=jnp.int32)
    position = ctx_index * slot_count + own_slots
    tok_position = jnp.tile(position, seq_count)
    row_valid = (position[None, :] < lengths[:, None]).reshape(tokens).astype(wide)
    mirror = [(i, (i + 1) % ctx_size) for i in range(ctx_size)]

    gain_cols, head_cols = norm_gains.shape[1], qk_gains.shape[1]
    small = jnp.concatenate(
        [
            norm_gains.astype(wide).reshape(-1),
            qk_gains.astype(wide).reshape(-1),
            jnp.sum(lengths).astype(wide)[None],
        ]
    )
    places = Plane()
    small_all = places.gather_whole(small[None])
    gain_rows = small_all[:, : 2 * gain_cols].reshape(shards, 2, gain_cols)
    full_gains = jnp.swapaxes(gain_rows, 0, 1).reshape(2, shards * gain_cols)
    head_rows = small_all[:, 2 * gain_cols : 2 * (gain_cols + head_cols)]
    qk_float = jnp.swapaxes(head_rows.reshape(shards, 2, head_cols), 0, 1).reshape(
        2, shards * head_cols
    )
    valid_count = jnp.sum(small_all[:, -1]) / ctx_size
    gain_attn, gain_ffn = full_gains[0], full_gains[1]
    head_dim = qk_float.shape[1]
    heads_local = w_qkv.shape[2] // head_dim
    score_scale = head_dim ** (-0.5)

    tables = route_tables(
        routes.reshape(tokens, top_count), gate_weights.reshape(tokens, top_count), experts
    )
    table = lax.all_to_all(tables, plane, split_axis=0, concat_axis=0, tiled=True).reshape(
        shards, shard_experts, 2, tokens
    )
    rank = table[:, :, 0].astype(jnp.int32)
    offset = (jnp.arange(shard_experts, dtype=jnp.int32) * capacity)[None, :, None]
    place = jnp.swapaxes(jnp.where(rank >= 0, rank + offset, -1), 1, 2)
    w_up = w_gate_up.reshape(shard_experts, width, 2 * hidden_local)
    order = places.order()
    sort = lambda a: jnp.concatenate(
        [lax.dynamic_slice_in_dim(a, block, 1, 0) for block in order], axis=0
    )
    table, place = sort(table), sort(place)
    some = lambda a, begin, pieces: a[begin : begin + blocks_in(pieces)]

    def blocks_in(pieces):
        return sum(piece.shape[1] for piece in pieces) // width

    full_qkv = lax.all_gather(
        w_qkv.reshape(w_qkv.shape[0], -1), plane, axis=0, tiled=True
    )
    rows_out = tie(line_gather(w_out), full_qkv[:1])
    full_out = lax.all_gather(rows_out, plane, axis=1, tiled=True)
    flat_states = states.astype(wide).reshape(tokens, width)
    normed = rms_norm(flat_states, gain_attn).astype(low)
    projected = jnp.dot(normed, full_qkv, preferred_element_type=wide).reshape(
        tokens, 3, heads_local, head_dim
    )

    def prepare_query(projected_in, gain):
        return rotate(rms_norm(projected_in, gain), tok_position)

    queries, query_back = jax.vjp(prepare_query, projected[:, 0], qk_float[0])
    key_states, key_back = jax.vjp(prepare_query, projected[:, 1], qk_float[1])
    query_low = queries.astype(low).reshape(seq_count, slot_count, heads_local, head_dim)
    by_head = lambda a: a.astype(low).reshape(seq_count, slot_count, heads_local, head_dim)
    value_low, key_low = by_head(projected[:, 2]), by_head(key_states)
    other_value = lax.ppermute(value_low, "ctx", mirror)
    other_key = lax.ppermute(key_low, "ctx", mirror)
    gathered_value = jnp.concatenate([value_low, other_value], axis=1)
    gathered_key = jnp.concatenate([key_low, other_key], axis=1)
    other_position = (1 - ctx_index) * slot_count + own_slots
    key_position = jnp.concatenate([position, other_position])
    key_valid = key_position[None, :] < lengths[:, None]
    pieces = [
        attend_sequence(
            query_low[i], gathered_key[i], gathered_value[i], key_valid[i], score_scale
        )
        for i in range(seq_count)
    ]
    attended_low = (
        jnp.stack([p[0] for p in pieces]).astype(low).reshape(tokens, heads_local * head_dim)
    )
    begin = tp_index * part
    own = lambda a: lax.dynamic_slice_in_dim(a, begin, part, 0)
    attended_own = lax.all_to_all(
        attended_low, "tp", split_axis=0, concat_axis=1, tiled=True
    )
    states_own = own(flat_states)
    middle_own = states_own + jnp.dot(attended_own, full_out, preferred_element_type=wide)
    normed_own = rms_norm(middle_own, gain_ffn).astype(low)

    middle_col = width // 2
    cols = (slice(0, middle_col), slice(middle_col, width))

    def spread(*halves):
        return [lax.all_gather(half.astype(low), "tp", axis=0, tiled=True) for half in halves]

    saved = [()]

    def forward(begin, pieces):
        made, saved[0] = expert_call(
            begin, pieces, some(table, begin, pieces), some(place, begin, pieces), w_up, w_down,
            None, saved[0], capacity, shards,
        )
        return made

    def finish(half):
        return lax.psum_scatter(half, "tp", scatter_dimension=0, tiled=True).astype(wide)

    teacher_own = own(teacher.reshape(tokens, width)).astype(wide)
    valid_own = own(row_valid)
    grad_scale = (2.0 * loss_scale / valid_count * valid_own)[:, None]
    second_own, table, place = lax.optimization_barrier((normed_own[:, cols[1]], table, place))
    first_block, second_block = spread(normed_own[:, cols[0]], second_own)
    second_block, w_up = lax.optimization_barrier((second_block, w_up))
    mixture = places.experts(
        first_block,
        second_block,
        forward,
        lambda: ((), ()),
    )
    rows_in, gate_up, hidden = saved[0]
    final_own = middle_own + finish(mixture)
    difference = final_own - teacher_own
    local_loss = jnp.sum(valid_own * jnp.sum(difference * difference, axis=-1))
    grad_final = grad_scale * difference
    spread_halves = spread(grad_final[:, cols[0]], grad_final[:, cols[1]])
    activations = lax.all_gather(final_own.astype(low), "tp", axis=0, tiled=True).reshape(
        seq_count, slot_count, width
    )

    saved[0] = ()

    def backward(begin, pieces):
        made, saved[0] = expert_call(
            begin, pieces, some(table, begin, pieces), some(place, begin, pieces), w_up, w_down,
            gate_up, saved[0], capacity, shards,
        )
        if begin == 2:
            made = tie(made, activations)
        return made

    def weight_grads():
        rows_back, grad_rows = saved[0]
        made.append(
            jnp.einsum("ebcf,ebcd->efd", hidden, rows_back, preferred_element_type=wide)
        )
        yield [made[0]]
        grad_up = jnp.einsum("ebcd,ebcf->edf", rows_in, grad_rows, preferred_element_type=wide)
        made.append(grad_up)
        yield [grad_up]

    made = []
    total_in = places.experts(*spread_halves, backward, weight_grads)
    if not made:
        for _ in weight_grads():
            pass
    grad_down, grad_up = made
    grad_gate_up = with_layout_constraint(
        grad_up.reshape(shard_experts, width, 2, hidden_local),
        Layout(major_to_minor=(0, 1, 2, 3)),
    )
    grad_ffn = tie(finish(total_in), grad_gate_up, grad_down)

    grad_middle_norm, grad_gain_ffn = norm_back(grad_ffn, middle_own, gain_ffn)
    grad_middle = grad_final + grad_middle_norm
    grad_branch = grad_middle.astype(low)

    grad_attended = lax.all_to_all(
        nt_dot(grad_branch, full_out).astype(low), "tp", split_axis=1, concat_axis=0, tiled=True
    )
    grad_heads = grad_attended.reshape(seq_count, slot_count, heads_local, head_dim)
    backs = [
        back_sequence(
            query_low[i],
            gathered_key[i],
            gathered_value[i],
            key_valid[i],
            pieces[i][1],
            grad_heads[i],
            score_scale,
        )
        for i in range(seq_count)
    ]
    grad_query, grad_key, grad_value = [jnp.stack(parts) for parts in zip(*backs, strict=True)]

    def returned(grad):
        coming = lax.ppermute(grad[:, slot_count:].astype(low), "ctx", mirror)
        return added(grad[:, :slot_count], coming).reshape(tokens, heads_local, head_dim)

    grad_v, own_key = returned(grad_value), returned(grad_key)
    branch_block = line_gather(grad_branch)
    grad_w_out = jnp.einsum("nd,nf->df", branch_block, attended_low, preferred_element_type=wide)
    grad_q, grad_q_gain = query_back(grad_query.reshape(tokens, heads_local, head_dim))
    grad_k, grad_k_gain = key_back(own_key)
    flat = lambda a: a.astype(low).reshape(tokens, -1)
    grad_proj_low = jnp.concatenate([flat(grad_q), flat(grad_k), flat(grad_v)], axis=1)
    grad_qk = jnp.stack([grad_q_gain, grad_k_gain])
    grad_normed = lax.psum_scatter(
        nt_dot(grad_proj_low, full_qkv).astype(low),
        "tp",
        scatter_dimension=0,
        tiled=True,
    ).astype(wide)
    grad_w_qkv = jnp.einsum("nd,nk->dk", normed, grad_proj_low, preferred_element_type=wide)
    grad_states_norm, grad_gain_attn = norm_back(grad_normed, states_own, gain_attn)
    grad_states = (
        lax.all_gather((grad_middle + grad_states_norm).astype(low), "tp", axis=0, tiled=True)
        .astype(wide)
        .reshape(seq_count, slot_count, width)
    )
    sums = sum_everywhere(
        jnp.concatenate([grad_gain_attn, grad_gain_ffn, grad_qk.reshape(-1), local_loss[None]])
    )
    out_gains = lax.dynamic_slice_in_dim(
        sums[: 2 * width].reshape(2, width), plane_index * gain_cols, gain_cols, 1
    )
    out_qk = lax.dynamic_slice_in_dim(
        sums[2 * width : 2 * (width + head_dim)].reshape(2, head_dim),
        plane_index * head_cols,
        head_cols,
        1,
    )
    loss_value = sums[-1] / valid_count
    weights_own = places.reduce_whole(
        jnp.concatenate([grad_w_qkv.astype(low), grad_w_out.astype(low)], axis=1)
    )
    qkv_cols = grad_w_qkv.shape[1]
    out_qkv = weights_own[:, :qkv_cols].reshape(w_qkv.shape)
    out_w_out = weights_own[:, qkv_cols:].T
    return (
        activations,
        loss_value,
        valid_count,
        grad_states,
        out_qkv,
        out_w_out,
        out_gains,
        out_qk,
        grad_gate_up,
        grad_down,
    )


def solution(mesh):
    placed = (
        P("fsdp", "ctx", None),
        P("fsdp", "ctx", None),
        P("fsdp"),
        P("fsdp", "ctx", None),
        P("fsdp", "ctx", None),
        P(("fsdp", "ctx"), None, "tp"),
        P("tp", ("fsdp", "ctx")),
        P(None, ("fsdp", "ctx")),
        P(None, ("fsdp", "ctx")),
        P(("fsdp", "ctx"), None, None, "tp"),
        P(("fsdp", "ctx"), "tp", None),
    )
    return jax.shard_map(
        per_device,
        mesh=mesh,
        in_specs=placed,
        out_specs=(
            P("fsdp", "ctx", None),
            P(),
            P(),
            P("fsdp", "ctx", None),
            P(("fsdp", "ctx"), None, "tp"),
            P("tp", ("fsdp", "ctx")),
            P(None, ("fsdp", "ctx")),
            P(None, ("fsdp", "ctx")),
            P(("fsdp", "ctx"), None, None, "tp"),
            P(("fsdp", "ctx"), "tp", None),
        ),
        check_vma=False,
    )
```

```python
import functools

import jax
import jax.numpy as jnp
from jax import lax
from jax.experimental.layout import Layout, with_layout_constraint
from jax.experimental import pallas as pl
from jax.experimental.pallas import tpu as pltpu
from jax.sharding import PartitionSpec as P

norm_eps = 1e-05
rope_base = 10000.0
loss_scale = 4096.0
masked_score = -1e30
plane = ("fsdp", "ctx")
everywhere = ("fsdp", "ctx", "tp")
low = jnp.bfloat16
wide = jnp.float32


def rms_norm(values, gain_vec):
    return (
        values * lax.rsqrt(jnp.mean(values * values, axis=-1, keepdims=True) + norm_eps) * gain_vec
    )


def norm_back(grad_normed, values, gain_vec):
    inverse = lax.rsqrt(jnp.mean(values * values, axis=-1, keepdims=True) + norm_eps)
    scaled = values * inverse
    grad_scaled = grad_normed * gain_vec
    grad_values = inverse * (
        grad_scaled - scaled * jnp.mean(grad_scaled * scaled, axis=-1, keepdims=True)
    )
    return (grad_values, jnp.sum(grad_normed * scaled, axis=0))


def rotate(values, position):
    half_dim = values.shape[-1] // 2
    frequency = rope_base ** (-2.0 * jnp.arange(half_dim, dtype=wide) / values.shape[-1])
    angles = position.astype(wide)[:, None] * frequency[None, :]
    cosine = jnp.cos(angles)[:, None, :]
    sine_part = jnp.sin(angles)[:, None, :]
    first_half = values[..., :half_dim]
    second_half = values[..., half_dim:]
    return jnp.concatenate(
        [
            first_half * cosine - second_half * sine_part,
            second_half * cosine + first_half * sine_part,
        ],
        axis=-1,
    )


def prepare(projected, qk_float, position):
    queries = rotate(rms_norm(projected[:, 0], qk_float[0]), position)
    key_states = rotate(rms_norm(projected[:, 1], qk_float[1]), position)
    return (queries, key_states, projected[:, 2])


def attend_sequence(query_seq, key_seq, value_seq, valid_seq, score_scale):
    scores = (
        jnp.einsum("qhd,khd->hqk", query_seq, key_seq, preferred_element_type=wide)
        * score_scale
    )
    scores = jnp.where(valid_seq[None, None, :], scores, masked_score)
    peak_score = jnp.max(scores, axis=-1, keepdims=True)
    exponent = jnp.exp(scores - peak_score)
    row_total = jnp.sum(exponent, axis=-1, keepdims=True)
    probability = (exponent / row_total).astype(low)
    output = jnp.einsum("hqk,khd->qhd", probability, value_seq, preferred_element_type=wide)
    return (output, (peak_score + jnp.log(row_total))[..., 0])


def back_sequence(query_seq, key_seq, value_seq, valid_seq, log_seq, grad_seq, score_scale):
    scores = (
        jnp.einsum("qhd,khd->hqk", query_seq, key_seq, preferred_element_type=wide)
        * score_scale
    )
    scores = jnp.where(valid_seq[None, None, :], scores, masked_score)
    probability = jnp.exp(scores - log_seq[..., None])
    grad_prob = jnp.einsum("qhd,khd->hqk", grad_seq, value_seq, preferred_element_type=wide)
    grad_scores = (
        probability * (grad_prob - jnp.sum(probability * grad_prob, axis=-1, keepdims=True))
    ).astype(low)
    grad_query = (
        jnp.einsum("hqk,khd->qhd", grad_scores, key_seq, preferred_element_type=wide)
        * score_scale
    )
    grad_key = (
        jnp.einsum("hqk,qhd->khd", grad_scores, query_seq, preferred_element_type=wide)
        * score_scale
    )
    grad_value = jnp.einsum(
        "hqk,qhd->khd", probability.astype(low), grad_seq, preferred_element_type=wide
    )
    return (grad_query, grad_key, grad_value)


def route_tables(route_rows, gate_rows, experts):
    slots = route_rows.shape[0]
    hit = route_rows[None, :, :] == jnp.arange(experts, dtype=jnp.int32)[:, None, None]
    named = jnp.sum(hit.astype(wide), axis=-1)
    gates = jnp.sum(jnp.where(hit, gate_rows[None, :, :], 0.0), axis=-1)
    order = jnp.arange(slots, dtype=jnp.int32)
    before = (order[:, None] < order[None, :]).astype(low)
    rank = jnp.dot(named.astype(low), before, preferred_element_type=wide)
    return jnp.stack([jnp.where(named > 0.0, rank, -1.0), gates], axis=1)


def pick_rows(table_ref, block, capacity, slots):
    rank = table_ref[block, 0, 0:1, :].astype(jnp.int32)
    gate = table_ref[block, 0, 1:2, :]
    match = lax.broadcasted_iota(jnp.int32, (capacity, slots), 0) == rank
    chosen = jnp.where(match, 1.0, 0.0).astype(low)
    weight = jnp.sum(jnp.where(match, gate, 0.0), axis=1, keepdims=True)
    return (chosen, weight)


def spread_rows(place_ref, block, experts, capacity, slots):
    column = lax.broadcasted_iota(jnp.int32, (slots, experts * capacity), 1)
    match = column == place_ref[block, :, 0:1]
    for expert in range(1, experts):
        match = match | (column == place_ref[block, :, expert : expert + 1])
    return jnp.where(match, 1.0, 0.0).astype(low)


def nt_dot(left, right):
    return lax.dot_general(left, right, (((1,), (1,)), ((), ())), preferred_element_type=wide)


def tiles_of(width, most=512):
    step = min(width, most)
    return [slice(begin, begin + step) for begin in range(0, width, step)]


def take_rows(x_refs, table_ref, rows_ref):
    blocks, capacity, width = rows_ref.shape[1:]
    slots = table_ref.shape[3]
    weights, place = [], 0
    for block in range(blocks):
        chosen, weight = pick_rows(table_ref, block, capacity, slots)
        weights.append(weight)
        done = 0
        while done < width:
            x_ref = x_refs[place]
            for cut in tiles_of(x_ref.shape[1]):
                rows_ref[0, block, :, done + cut.start : done + cut.stop] = jnp.dot(
                    chosen, x_ref[:, cut], preferred_element_type=wide
                ).astype(low)
            done, place = done + x_ref.shape[1], place + 1
    return (rows_ref[0].reshape(blocks * capacity, width), jnp.concatenate(weights, axis=0))


def fill_spread(place_ref, spread_ref, capacity):
    blocks, slots, total = spread_ref.shape
    for block in range(blocks):
        spread_ref[block] = spread_rows(place_ref, block, total // capacity, capacity, slots)


def combine_blocks(spread_ref, y_ref, out_refs):
    for block, out_ref in enumerate(out_refs):
        for cut in tiles_of(y_ref.shape[2]):
            out_ref[:, cut] = jnp.dot(
                spread_ref[block], y_ref[block, :, cut], preferred_element_type=wide
            ).astype(low)


def forward_body(n_x, n_out, n_keep, *refs):
    x_refs, refs = refs[:n_x], refs[n_x:]
    (table_ref, place_ref, up_ref, down_ref), refs = refs[:4], refs[4 + n_keep :]
    out_refs, (rows_ref, gate_up_ref, hidden_ref, y_ref, spread_ref) = refs[:n_out], refs[n_out:]
    expert = pl.program_id(0)
    blocks, capacity, width = rows_ref.shape[1:]
    experts = y_ref.shape[1] // capacity

    @pl.when(expert == 0)
    def _():
        fill_spread(place_ref, spread_ref, capacity)

    half = down_ref.shape[1]
    rows, weight = take_rows(x_refs, table_ref, rows_ref)
    gate_up = jnp.dot(rows, up_ref[expert], preferred_element_type=wide)
    gate_up_ref[0] = gate_up.reshape(blocks, capacity, 2 * half)
    gate_part = gate_up[:, :half]
    up_part = gate_up[:, half:]
    hidden = (gate_part * jax.nn.sigmoid(gate_part) * up_part * weight).astype(low)
    hidden_ref[0] = hidden.reshape(blocks, capacity, half)
    begin = pl.multiple_of(expert * capacity, 16)
    for cut in tiles_of(width):
        y_ref[:, pl.ds(begin, capacity), cut] = (
            jnp.dot(hidden, down_ref[expert, :, cut], preferred_element_type=wide)
            .astype(low)
            .reshape(blocks, capacity, -1)
        )

    @pl.when(expert == experts - 1)
    def _():
        combine_blocks(spread_ref, y_ref, out_refs)


def backward_body(n_x, n_out, n_keep, *refs):
    x_refs, refs = refs[:n_x], refs[n_x:]
    (table_ref, place_ref, up_ref, down_ref, gate_up_ref), refs = refs[:5], refs[5 + n_keep :]
    out_refs, (rows_ref, grad_ref, y_ref, spread_ref) = refs[:n_out], refs[n_out:]
    expert = pl.program_id(0)
    blocks, capacity, width = rows_ref.shape[1:]
    experts = y_ref.shape[1] // capacity

    @pl.when(expert == 0)
    def _():
        fill_spread(place_ref, spread_ref, capacity)

    half = down_ref.shape[1]
    rows, weight = take_rows(x_refs, table_ref, rows_ref)
    grad_hidden = nt_dot(rows, down_ref[expert]) * weight
    gate_up = gate_up_ref[0].reshape(blocks * capacity, 2 * half)
    gate_part = gate_up[:, :half]
    up_part = gate_up[:, half:]
    sigmoid = jax.nn.sigmoid(gate_part)
    grad_gate = grad_hidden * up_part * sigmoid * (1.0 + gate_part * (1.0 - sigmoid))
    grad_up = grad_hidden * gate_part * sigmoid
    grad_rows = jnp.concatenate([grad_gate, grad_up], axis=1).astype(low)
    grad_ref[0] = grad_rows.reshape(blocks, capacity, 2 * half)
    begin = pl.multiple_of(expert * capacity, 16)
    for cut in tiles_of(width):
        y_ref[:, pl.ds(begin, capacity), cut] = (
            nt_dot(grad_rows, up_ref[expert, cut, :]).astype(low).reshape(blocks, capacity, -1)
        )

    @pl.when(expert == experts - 1)
    def _():
        combine_blocks(spread_ref, y_ref, out_refs)


def expert_call(begin, pieces, table, place, w_up, w_down, gate_up, kept, capacity, total):
    blocks, experts, _, slots = table.shape
    width = w_up.shape[1]
    double, half = w_up.shape[2], w_down.shape[1]
    backward = gate_up is not None
    once = pl.Buffered(1)
    row_spec = lambda last: pl.BlockSpec(
        (1, blocks, capacity, last), lambda e: (e, begin // blocks, 0, 0)
    )
    row_shape = lambda last, kind: pltpu.HBM((experts, total, capacity, last), kind)
    whole = lambda shape: pl.BlockSpec(shape, lambda e: (0,) * len(shape), pipeline_mode=once)
    in_specs = [whole(p.shape) for p in pieces] + [
        pl.BlockSpec((blocks, 1, 2, slots), lambda e: (0, e, 0, 0)),
        whole((blocks, slots, experts)),
        pl.BlockSpec(memory_space=pltpu.VMEM),
        pl.BlockSpec(memory_space=pltpu.VMEM),
    ]
    operands = [*pieces, table, place, w_up, w_down]
    n_out = blocks
    out_specs = [whole((slots, width))] * n_out + [row_spec(width), row_spec(double)]
    out_shape = [jax.ShapeDtypeStruct((slots, width), low)] * n_out + [row_shape(width, low)]
    if backward:
        in_specs.append(row_spec(double))
        operands.append(pltpu.with_memory_space_constraint(gate_up, pltpu.HBM))
        out_shape.append(row_shape(double, low))
    else:
        out_specs.append(row_spec(half))
        out_shape += [row_shape(double, wide), row_shape(half, low)]
    aliases = {len(operands) + i: n_out + i for i in range(len(kept))}
    rows = experts * blocks * capacity
    body = functools.partial(
        backward_body if backward else forward_body, len(pieces), n_out, len(kept)
    )
    made = pl.pallas_call(
        body,
        grid=(experts,),
        in_specs=in_specs + [pl.BlockSpec(memory_space=pl.ANY)] * len(kept),
        out_specs=out_specs,
        out_shape=out_shape,
        input_output_aliases=aliases,
        scratch_shapes=[
            pltpu.VMEM((blocks, experts * capacity, width), low),
            pltpu.VMEM((blocks, slots, experts * capacity), low),
        ],
        compiler_params=pltpu.CompilerParams(
            dimension_semantics=("arbitrary",), vmem_limit_bytes=(28 if backward else 28) << 20
        ),
        cost_estimate=pl.CostEstimate(
            flops=2 * rows * width * (2 * slots + double + half),
            bytes_accessed=4 * blocks * slots * width + rows * (2 * width + 6 * double),
            transcendentals=rows * half,
        ),
    )(*operands, *kept)
    return (made[:n_out], made[n_out:])


def on_chip(*arrays):
    count = len(arrays)

    def body(*refs):
        sources, targets, sems = refs[:count], refs[count : 2 * count], refs[-1]
        copies = [
            pltpu.make_async_copy(sources[i], targets[i], sems.at[i]) for i in range(count)
        ]
        for copy in copies:
            copy.start()
        for copy in copies:
            copy.wait()

    return pl.pallas_call(
        body,
        in_specs=[pl.BlockSpec(memory_space=pltpu.HBM)] * count,
        out_specs=[pl.BlockSpec(memory_space=pltpu.VMEM)] * count,
        out_shape=[pltpu.VMEM(a.shape, a.dtype) for a in arrays],
        scratch_shapes=[pltpu.SemaphoreType.DMA((count,))],
        compiler_params=pltpu.CompilerParams(vmem_limit_bytes=24 << 20),
    )(*[pltpu.with_memory_space_constraint(a, pltpu.HBM) for a in arrays])


def added(left, right):
    return left.astype(wide) + right.astype(wide)


def tie(values, *anchors):
    return lax.optimization_barrier((values, anchors))[0]


def sum_everywhere(values):
    values = values[None]
    for axis in everywhere:
        size, step = lax.axis_size(axis), 1
        while step < size:
            pairs = [(i, i ^ step) for i in range(size)]
            values = values + lax.ppermute(values, axis, pairs)
            step *= 2
    return values[0]


def line_gather(shard):
    size = lax.axis_size("tp")
    if size > 4:
        return lax.all_gather(shard, "tp", axis=0, tiled=True)
    move = lambda d: lax.ppermute(
        shard, "tp", [(i, i + d) for i in range(size) if 0 <= i + d < size]
    )
    near = [move(d) for d in range(size - 1, 0, -1)] + [shard] + [move(-d) for d in range(1, size)]
    rows = shard.shape[0]
    begin = (size - 1 - lax.axis_index("tp")) * rows
    return lax.dynamic_slice_in_dim(jnp.concatenate(near, axis=0), begin, size * rows, 0)


class Plane:
    def __init__(self):
        self.fsdp, self.ctx = lax.axis_size("fsdp"), lax.axis_size("ctx")
        self.tree = self.fsdp == 4 and self.ctx == 2
        self.shards = self.fsdp * self.ctx

    def core(self, a):
        return lax.ppermute(a, "fsdp", [(i, i ^ 1) for i in range(self.fsdp)])

    def along_x(self, a):
        return lax.ppermute(a, "fsdp", [(i, i ^ 2) for i in range(self.fsdp)])

    def along_y(self, a):
        return lax.ppermute(a, "ctx", [(i, i ^ 1) for i in range(self.ctx)])

    def order(self):
        if not self.tree:
            return list(range(self.shards))
        fsdp, ctx = lax.axis_index("fsdp"), lax.axis_index("ctx")
        chips = ((0, 0), (1, 0), (0, 1), (1, 1))
        return [(fsdp ^ (2 * x) ^ core) * 2 + (ctx ^ y) for x, y in chips for core in (0, 1)]

    def gather_whole(self, shard):
        rows = shard.shape[0]
        if not self.tree:
            return lax.all_gather(shard, plane, axis=0, tiled=True)
        halves = (shard[: rows // 2], shard[rows // 2 :]) if rows > 1 else (shard,)
        x = [self.along_x(h) for h in halves]
        y = [self.along_y(h) for h in halves]
        far = [self.along_y(x[0])] + [self.along_x(h) for h in y[1:]]
        whole = jnp.zeros((self.shards * rows, *shard.shape[1:]), shard.dtype)
        order = self.order()
        for c, pieces in enumerate((halves, x, y, far)):
            for core in (0, 1):
                begin = order[2 * c + core] * rows
                for piece in pieces:
                    found = self.core(piece) if core else piece
                    whole = lax.dynamic_update_slice_in_dim(whole, found, begin, 0)
                    begin = begin + piece.shape[0]
        return whole

    def reduce_whole(self, partial):
        rows = partial.shape[0] // self.shards
        if not self.tree:
            return lax.psum_scatter(partial, plane, scatter_dimension=0, tiled=True).astype(wide)
        blocks = [lax.dynamic_slice_in_dim(partial, i * rows, rows, 0) for i in self.order()]
        pre = [added(blocks[2 * c], self.core(blocks[2 * c + 1])) for c in range(4)]
        cuts = tiles_of(partial.shape[1], partial.shape[1] // 2)
        return jnp.concatenate(
            [self.total(k, *[p[:, cut] for p in pre]) for k, cut in enumerate(cuts)], axis=1
        )

    def total(self, k, own, near_x, near_y, far):
        if k % 2 == 0:
            near_y = near_y + self.along_x(far.astype(low)).astype(wide)
        else:
            near_x = near_x + self.along_y(far.astype(low)).astype(wide)
        from_x, from_y = self.along_x(near_x.astype(low)), self.along_y(near_y.astype(low))
        return own + from_x.astype(wide) + from_y.astype(wide)

    def experts(self, first, second, call, filler):
        if not self.tree:
            split = lambda a: jnp.split(lax.all_gather(a, plane, axis=0, tiled=True), self.shards)
            halves, made = list(zip(split(first), split(second), strict=True)), []
            for i in range(0, self.shards, 2):
                made += call(i, [*halves[i], *halves[i + 1]])
            return lax.psum_scatter(
                jnp.concatenate(made, axis=0), plane, scatter_dimension=0, tiled=True
            )
        step = first.shape[1]
        pre = lambda made, other: [
            added(made[:, k * step : (k + 1) * step], other[:, k * step : (k + 1) * step])
            for k in range(2)
        ]
        narrow = lambda a: a.astype(low)
        x_first, y_first = self.along_x(first), self.along_y(first)
        second = tie(second, x_first, y_first)
        own_pieces = [first, second, self.core(first), self.core(second)]
        x_second, y_second = self.along_x(second), self.along_y(second)
        over_x, over_y = self.core(x_first), self.core(y_first)
        own = call(0, tie(own_pieces, over_x, over_y))
        x_second, y_second = tie((x_second, y_second), own[0])
        far = [self.along_y(x_first), self.along_x(y_second)]
        over_y = [over_y, self.core(y_second)]
        near_x = call(2, [x_first, x_second, over_x, self.core(x_second)])
        near_x = tie(near_x, over_y)
        other_own, other_x = self.core(own[1]), self.core(near_x[1])
        far += [self.core(piece) for piece in far]
        near_y = tie(call(4, [y_first, y_second, *over_y]), other_own, other_x, far)
        other_y = self.core(near_y[1])
        sum_x, sum_y = pre(near_x[0], other_x), pre(near_y[0], other_y)
        early_x, early_y = narrow(sum_x[0]), narrow(sum_y[1])
        last = call(6, tie(far, early_x, early_y))
        sent = [self.along_x(early_x), self.along_y(early_y)]
        last = tie(last, sent)
        sum_far = pre(last[0], self.core(last[1]))
        sum_own = pre(own[0], other_own)
        fillers = iter(filler())
        far = [self.along_x(narrow(sum_far[0])), self.along_y(narrow(sum_far[1]))]
        far = tie(far, next(fillers))
        near = [
            self.along_y(narrow(added(sum_y[0], far[0]))),
            self.along_x(narrow(added(sum_x[1], far[1]))),
        ]
        near = tie(near, next(fillers))
        return jnp.concatenate(
            [added(sum_own[k], sent[k]) + near[k].astype(wide) for k in range(2)], axis=1
        ).astype(low)


def per_device(
    states,
    teacher,
    lengths,
    routes,
    gate_weights,
    w_qkv,
    w_out,
    norm_gains,
    qk_gains,
    w_gate_up,
    w_down,
):
    seq_count, slot_count, width = states.shape
    top_count = routes.shape[-1]
    ctx_size = lax.axis_size("ctx")
    tp_size = lax.axis_size("tp")
    shards = lax.axis_size(plane)
    ctx_index = lax.axis_index("ctx")
    tp_index = lax.axis_index("tp")
    plane_index = lax.axis_index(plane)
    tokens = seq_count * slot_count
    part = tokens // tp_size
    shard_experts = w_gate_up.shape[0]
    hidden_local = w_gate_up.shape[3]
    experts = shard_experts * shards
    capacity = 5 * tokens * top_count // (4 * experts)
    own_slots = jnp.arange(slot_count, dtype=jnp.int32)
    position = ctx_index * slot_count + own_slots
    tok_position = jnp.tile(position, seq_count)
    row_valid = (position[None, :] < lengths[:, None]).reshape(tokens).astype(wide)
    mirror = [(i, (i + 1) % ctx_size) for i in range(ctx_size)]

    gain_cols, head_cols = norm_gains.shape[1], qk_gains.shape[1]
    small = jnp.concatenate(
        [
            norm_gains.astype(wide).reshape(-1),
            qk_gains.astype(wide).reshape(-1),
            jnp.sum(lengths).astype(wide)[None],
        ]
    )
    places = Plane()
    small_all = places.gather_whole(small[None])
    gain_rows = small_all[:, : 2 * gain_cols].reshape(shards, 2, gain_cols)
    full_gains = jnp.swapaxes(gain_rows, 0, 1).reshape(2, shards * gain_cols)
    head_rows = small_all[:, 2 * gain_cols : 2 * (gain_cols + head_cols)]
    qk_float = jnp.swapaxes(head_rows.reshape(shards, 2, head_cols), 0, 1).reshape(
        2, shards * head_cols
    )
    valid_count = jnp.sum(small_all[:, -1]) / ctx_size
    gain_attn, gain_ffn = full_gains[0], full_gains[1]
    head_dim = qk_float.shape[1]
    heads_local = w_qkv.shape[2] // head_dim
    score_scale = head_dim ** (-0.5)

    tables = route_tables(
        routes.reshape(tokens, top_count), gate_weights.reshape(tokens, top_count), experts
    )
    table = lax.all_to_all(tables, plane, split_axis=0, concat_axis=0, tiled=True).reshape(
        shards, shard_experts, 2, tokens
    )
    rank = table[:, :, 0].astype(jnp.int32)
    offset = (jnp.arange(shard_experts, dtype=jnp.int32) * capacity)[None, :, None]
    place = jnp.swapaxes(jnp.where(rank >= 0, rank + offset, -1), 1, 2)
    w_up = w_gate_up.reshape(shard_experts, width, 2 * hidden_local)
    order = places.order()
    sort = lambda a: jnp.concatenate(
        [lax.dynamic_slice_in_dim(a, block, 1, 0) for block in order], axis=0
    )
    table, place = sort(table), sort(place)
    some = lambda a, begin, pieces: a[begin : begin + blocks_in(pieces)]

    def blocks_in(pieces):
        return sum(piece.shape[1] for piece in pieces) // width

    full_qkv = lax.all_gather(
        w_qkv.reshape(w_qkv.shape[0], -1), plane, axis=0, tiled=True
    )
    rows_out = tie(line_gather(w_out), full_qkv[:1])
    full_out = lax.all_gather(rows_out, plane, axis=1, tiled=True)
    flat_states = states.astype(wide).reshape(tokens, width)
    normed = rms_norm(flat_states, gain_attn).astype(low)
    projected = jnp.dot(normed, full_qkv, preferred_element_type=wide).reshape(
        tokens, 3, heads_local, head_dim
    )

    def prepare_query(projected_in, gain):
        return rotate(rms_norm(projected_in, gain), tok_position)

    queries, query_back = jax.vjp(prepare_query, projected[:, 0], qk_float[0])
    key_states, key_back = jax.vjp(prepare_query, projected[:, 1], qk_float[1])
    query_low = queries.astype(low).reshape(seq_count, slot_count, heads_local, head_dim)
    by_head = lambda a: a.astype(low).reshape(seq_count, slot_count, heads_local, head_dim)
    value_low, key_low = by_head(projected[:, 2]), by_head(key_states)
    other_value = lax.ppermute(value_low, "ctx", mirror)
    other_key = lax.ppermute(key_low, "ctx", mirror)
    gathered_value = jnp.concatenate([value_low, other_value], axis=1)
    gathered_key = jnp.concatenate([key_low, other_key], axis=1)
    other_position = (1 - ctx_index) * slot_count + own_slots
    key_position = jnp.concatenate([position, other_position])
    key_valid = key_position[None, :] < lengths[:, None]
    pieces = [
        attend_sequence(
            query_low[i], gathered_key[i], gathered_value[i], key_valid[i], score_scale
        )
        for i in range(seq_count)
    ]
    attended_low = (
        jnp.stack([p[0] for p in pieces]).astype(low).reshape(tokens, heads_local * head_dim)
    )
    begin = tp_index * part
    own = lambda a: lax.dynamic_slice_in_dim(a, begin, part, 0)
    attended_own = lax.all_to_all(
        attended_low, "tp", split_axis=0, concat_axis=1, tiled=True
    )
    states_own = own(flat_states)
    middle_own = states_own + jnp.dot(attended_own, full_out, preferred_element_type=wide)
    normed_own = rms_norm(middle_own, gain_ffn).astype(low)

    middle_col = width // 2
    cols = (slice(0, middle_col), slice(middle_col, width))

    def spread(*halves):
        return [lax.all_gather(half.astype(low), "tp", axis=0, tiled=True) for half in halves]

    saved = [()]

    def forward(begin, pieces):
        made, saved[0] = expert_call(
            begin, pieces, some(table, begin, pieces), some(place, begin, pieces), *near_weights,
            None, saved[0], capacity, shards,
        )
        return made

    def finish(half):
        return lax.psum_scatter(half, "tp", scatter_dimension=0, tiled=True).astype(wide)

    teacher_own = own(teacher.reshape(tokens, width)).astype(wide)
    valid_own = own(row_valid)
    grad_scale = (2.0 * loss_scale / valid_count * valid_own)[:, None]
    second_own, table, place = lax.optimization_barrier((normed_own[:, cols[1]], table, place))
    first_block, second_block = spread(normed_own[:, cols[0]], second_own)
    second_block, w_up = lax.optimization_barrier((second_block, w_up))
    near_weights = on_chip(w_up, w_down)
    mixture = places.experts(
        first_block,
        second_block,
        forward,
        lambda: ((), ()),
    )
    rows_in, gate_up, hidden = saved[0]
    final_own = middle_own + finish(mixture)
    difference = final_own - teacher_own
    local_loss = jnp.sum(valid_own * jnp.sum(difference * difference, axis=-1))
    grad_final = grad_scale * difference
    spread_halves = spread(grad_final[:, cols[0]], grad_final[:, cols[1]])
    activations = lax.all_gather(final_own.astype(low), "tp", axis=0, tiled=True).reshape(
        seq_count, slot_count, width
    )

    saved[0] = ()

    def backward(begin, pieces):
        made, saved[0] = expert_call(
            begin, pieces, some(table, begin, pieces), some(place, begin, pieces), *back_weights,
            gate_up, saved[0], capacity, shards,
        )
        return made

    def weight_grads():
        rows_back, grad_rows = saved[0]
        made.append(
            jnp.einsum("ebcf,ebcd->efd", hidden, rows_back, preferred_element_type=wide)
        )
        yield [made[0]]
        grad_up = jnp.einsum("ebcd,ebcf->edf", rows_in, grad_rows, preferred_element_type=wide)
        made.append(grad_up)
        yield [grad_up, activations]

    made = []
    first_block, second_block = spread_halves
    second_block, w_up = lax.optimization_barrier((second_block, w_up))
    back_weights = on_chip(w_up, w_down)
    total_in = places.experts(first_block, second_block, backward, weight_grads)
    if not made:
        for _ in weight_grads():
            pass
    grad_down, grad_up = made
    grad_gate_up = with_layout_constraint(
        grad_up.reshape(shard_experts, width, 2, hidden_local),
        Layout(major_to_minor=(0, 1, 2, 3)),
    )
    grad_ffn = tie(finish(total_in), grad_gate_up, grad_down)

    grad_middle_norm, grad_gain_ffn = norm_back(grad_ffn, middle_own, gain_ffn)
    grad_middle = grad_final + grad_middle_norm
    grad_branch = grad_middle.astype(low)

    grad_attended = lax.all_to_all(
        nt_dot(grad_branch, full_out).astype(low), "tp", split_axis=1, concat_axis=0, tiled=True
    )
    grad_heads = grad_attended.reshape(seq_count, slot_count, heads_local, head_dim)
    backs = [
        back_sequence(
            query_low[i],
            gathered_key[i],
            gathered_value[i],
            key_valid[i],
            pieces[i][1],
            grad_heads[i],
            score_scale,
        )
        for i in range(seq_count)
    ]
    grad_query, grad_key, grad_value = [jnp.stack(parts) for parts in zip(*backs, strict=True)]

    def returned(grad):
        coming = lax.ppermute(grad[:, slot_count:].astype(low), "ctx", mirror)
        return added(grad[:, :slot_count], coming).reshape(tokens, heads_local, head_dim)

    grad_v, own_key = returned(grad_value), returned(grad_key)
    branch_block = line_gather(grad_branch)
    grad_w_out = jnp.einsum("nd,nf->df", branch_block, attended_low, preferred_element_type=wide)
    grad_q, grad_q_gain = query_back(grad_query.reshape(tokens, heads_local, head_dim))
    grad_k, grad_k_gain = key_back(own_key)
    flat = lambda a: a.astype(low).reshape(tokens, -1)
    grad_proj_low = jnp.concatenate([flat(grad_q), flat(grad_k), flat(grad_v)], axis=1)
    grad_qk = jnp.stack([grad_q_gain, grad_k_gain])
    grad_normed = lax.psum_scatter(
        nt_dot(grad_proj_low, full_qkv).astype(low),
        "tp",
        scatter_dimension=0,
        tiled=True,
    ).astype(wide)
    grad_w_qkv = jnp.einsum("nd,nk->dk", normed, grad_proj_low, preferred_element_type=wide)
    grad_states_norm, grad_gain_attn = norm_back(grad_normed, states_own, gain_attn)
    grad_states = (
        lax.all_gather((grad_middle + grad_states_norm).astype(low), "tp", axis=0, tiled=True)
        .astype(wide)
        .reshape(seq_count, slot_count, width)
    )
    sums = sum_everywhere(
        jnp.concatenate([grad_gain_attn, grad_gain_ffn, grad_qk.reshape(-1), local_loss[None]])
    )
    out_gains = lax.dynamic_slice_in_dim(
        sums[: 2 * width].reshape(2, width), plane_index * gain_cols, gain_cols, 1
    )
    out_qk = lax.dynamic_slice_in_dim(
        sums[2 * width : 2 * (width + head_dim)].reshape(2, head_dim),
        plane_index * head_cols,
        head_cols,
        1,
    )
    loss_value = sums[-1] / valid_count
    weights_own = places.reduce_whole(
        jnp.concatenate([grad_w_qkv.astype(low), grad_w_out.astype(low)], axis=1)
    )
    qkv_cols = grad_w_qkv.shape[1]
    out_qkv = weights_own[:, :qkv_cols].reshape(w_qkv.shape)
    out_w_out = weights_own[:, qkv_cols:].T
    return (
        activations,
        loss_value,
        valid_count,
        grad_states,
        out_qkv,
        out_w_out,
        out_gains,
        out_qk,
        grad_gate_up,
        grad_down,
    )


def solution(mesh):
    placed = (
        P("fsdp", "ctx", None),
        P("fsdp", "ctx", None),
        P("fsdp"),
        P("fsdp", "ctx", None),
        P("fsdp", "ctx", None),
        P(("fsdp", "ctx"), None, "tp"),
        P("tp", ("fsdp", "ctx")),
        P(None, ("fsdp", "ctx")),
        P(None, ("fsdp", "ctx")),
        P(("fsdp", "ctx"), None, None, "tp"),
        P(("fsdp", "ctx"), "tp", None),
    )
    return jax.shard_map(
        per_device,
        mesh=mesh,
        in_specs=placed,
        out_specs=(
            P("fsdp", "ctx", None),
            P(),
            P(),
            P("fsdp", "ctx", None),
            P(("fsdp", "ctx"), None, "tp"),
            P("tp", ("fsdp", "ctx")),
            P(None, ("fsdp", "ctx")),
            P(None, ("fsdp", "ctx")),
            P(("fsdp", "ctx"), None, None, "tp"),
            P(("fsdp", "ctx"), "tp", None),
        ),
        check_vma=False,
    )
```

```python
import functools

import jax
import jax.numpy as jnp
from jax import lax
from jax.experimental.layout import Layout, with_layout_constraint
from jax.experimental import pallas as pl
from jax.experimental.pallas import tpu as pltpu
from jax.sharding import PartitionSpec as P

norm_eps = 1e-05
rope_base = 10000.0
loss_scale = 4096.0
masked_score = -1e30
plane = ("fsdp", "ctx")
everywhere = ("fsdp", "ctx", "tp")
low = jnp.bfloat16
wide = jnp.float32


def rms_norm(values, gain_vec):
    return (
        values * lax.rsqrt(jnp.mean(values * values, axis=-1, keepdims=True) + norm_eps) * gain_vec
    )


def norm_back(grad_normed, values, gain_vec):
    inverse = lax.rsqrt(jnp.mean(values * values, axis=-1, keepdims=True) + norm_eps)
    scaled = values * inverse
    grad_scaled = grad_normed * gain_vec
    grad_values = inverse * (
        grad_scaled - scaled * jnp.mean(grad_scaled * scaled, axis=-1, keepdims=True)
    )
    return (grad_values, jnp.sum(grad_normed * scaled, axis=0))


def rotate(values, position):
    half_dim = values.shape[-1] // 2
    frequency = rope_base ** (-2.0 * jnp.arange(half_dim, dtype=wide) / values.shape[-1])
    angles = position.astype(wide)[:, None] * frequency[None, :]
    cosine = jnp.cos(angles)[:, None, :]
    sine_part = jnp.sin(angles)[:, None, :]
    first_half = values[..., :half_dim]
    second_half = values[..., half_dim:]
    return jnp.concatenate(
        [
            first_half * cosine - second_half * sine_part,
            second_half * cosine + first_half * sine_part,
        ],
        axis=-1,
    )


def prepare(projected, qk_float, position):
    queries = rotate(rms_norm(projected[:, 0], qk_float[0]), position)
    key_states = rotate(rms_norm(projected[:, 1], qk_float[1]), position)
    return (queries, key_states, projected[:, 2])


def attend_sequence(query_seq, key_seq, value_seq, valid_seq, score_scale):
    scores = (
        jnp.einsum("qhd,khd->hqk", query_seq, key_seq, preferred_element_type=wide)
        * score_scale
    )
    scores = jnp.where(valid_seq[None, None, :], scores, masked_score)
    peak_score = jnp.max(scores, axis=-1, keepdims=True)
    exponent = jnp.exp(scores - peak_score)
    row_total = jnp.sum(exponent, axis=-1, keepdims=True)
    probability = (exponent / row_total).astype(low)
    output = jnp.einsum("hqk,khd->qhd", probability, value_seq, preferred_element_type=wide)
    return (output, (peak_score + jnp.log(row_total))[..., 0])


def back_sequence(query_seq, key_seq, value_seq, valid_seq, log_seq, grad_seq, score_scale):
    scores = (
        jnp.einsum("qhd,khd->hqk", query_seq, key_seq, preferred_element_type=wide)
        * score_scale
    )
    scores = jnp.where(valid_seq[None, None, :], scores, masked_score)
    probability = jnp.exp(scores - log_seq[..., None])
    grad_prob = jnp.einsum("qhd,khd->hqk", grad_seq, value_seq, preferred_element_type=wide)
    grad_scores = (
        probability * (grad_prob - jnp.sum(probability * grad_prob, axis=-1, keepdims=True))
    ).astype(low)
    grad_query = (
        jnp.einsum("hqk,khd->qhd", grad_scores, key_seq, preferred_element_type=wide)
        * score_scale
    )
    grad_key = (
        jnp.einsum("hqk,qhd->khd", grad_scores, query_seq, preferred_element_type=wide)
        * score_scale
    )
    grad_value = jnp.einsum(
        "hqk,qhd->khd", probability.astype(low), grad_seq, preferred_element_type=wide
    )
    return (grad_query, grad_key, grad_value)


def route_tables(route_rows, gate_rows, experts):
    slots = route_rows.shape[0]
    hit = route_rows[None, :, :] == jnp.arange(experts, dtype=jnp.int32)[:, None, None]
    named = jnp.sum(hit.astype(wide), axis=-1)
    gates = jnp.sum(jnp.where(hit, gate_rows[None, :, :], 0.0), axis=-1)
    order = jnp.arange(slots, dtype=jnp.int32)
    before = (order[:, None] < order[None, :]).astype(low)
    rank = jnp.dot(named.astype(low), before, preferred_element_type=wide)
    return jnp.stack([jnp.where(named > 0.0, rank, -1.0), gates], axis=1)


def pick_rows(table_ref, block, capacity, slots):
    rank = table_ref[block, 0, 0:1, :].astype(jnp.int32)
    gate = table_ref[block, 0, 1:2, :]
    match = lax.broadcasted_iota(jnp.int32, (capacity, slots), 0) == rank
    chosen = jnp.where(match, 1.0, 0.0).astype(low)
    weight = jnp.sum(jnp.where(match, gate, 0.0), axis=1, keepdims=True)
    return (chosen, weight)


def spread_rows(place_ref, block, experts, capacity, slots):
    column = lax.broadcasted_iota(jnp.int32, (slots, experts * capacity), 1)
    match = column == place_ref[block, :, 0:1]
    for expert in range(1, experts):
        match = match | (column == place_ref[block, :, expert : expert + 1])
    return jnp.where(match, 1.0, 0.0).astype(low)


def nt_dot(left, right):
    return lax.dot_general(left, right, (((1,), (1,)), ((), ())), preferred_element_type=wide)


def tiles_of(width, most=512):
    step = min(width, most)
    return [slice(begin, begin + step) for begin in range(0, width, step)]


def take_rows(x_refs, table_ref, rows_ref):
    blocks, capacity, width = rows_ref.shape[1:]
    slots = table_ref.shape[3]
    weights, place = [], 0
    for block in range(blocks):
        chosen, weight = pick_rows(table_ref, block, capacity, slots)
        weights.append(weight)
        done = 0
        while done < width:
            x_ref = x_refs[place]
            for cut in tiles_of(x_ref.shape[1]):
                rows_ref[0, block, :, done + cut.start : done + cut.stop] = jnp.dot(
                    chosen, x_ref[:, cut], preferred_element_type=wide
                ).astype(low)
            done, place = done + x_ref.shape[1], place + 1
    return (rows_ref[0].reshape(blocks * capacity, width), jnp.concatenate(weights, axis=0))


def fill_spread(place_ref, spread_ref, capacity):
    blocks, slots, total = spread_ref.shape
    for block in range(blocks):
        spread_ref[block] = spread_rows(place_ref, block, total // capacity, capacity, slots)


def combine_blocks(spread_ref, y_ref, out_refs):
    for block, out_ref in enumerate(out_refs):
        for cut in tiles_of(y_ref.shape[2]):
            out_ref[:, cut] = jnp.dot(
                spread_ref[block], y_ref[block, :, cut], preferred_element_type=wide
            ).astype(low)


def forward_body(n_x, n_out, n_keep, *refs):
    x_refs, refs = refs[:n_x], refs[n_x:]
    (table_ref, place_ref, up_ref, down_ref), refs = refs[:4], refs[4 + n_keep :]
    out_refs, (rows_ref, gate_up_ref, hidden_ref, y_ref, spread_ref) = refs[:n_out], refs[n_out:]
    expert = pl.program_id(0)
    blocks, capacity, width = rows_ref.shape[1:]
    experts = y_ref.shape[1] // capacity

    @pl.when(expert == 0)
    def _():
        fill_spread(place_ref, spread_ref, capacity)

    half = down_ref.shape[1]
    rows, weight = take_rows(x_refs, table_ref, rows_ref)
    gate_up = jnp.dot(rows, up_ref[expert], preferred_element_type=wide)
    gate_up_ref[0] = gate_up.reshape(blocks, capacity, 2 * half)
    gate_part = gate_up[:, :half]
    up_part = gate_up[:, half:]
    hidden = (gate_part * jax.nn.sigmoid(gate_part) * up_part * weight).astype(low)
    hidden_ref[0] = hidden.reshape(blocks, capacity, half)
    begin = pl.multiple_of(expert * capacity, 16)
    for cut in tiles_of(width):
        y_ref[:, pl.ds(begin, capacity), cut] = (
            jnp.dot(hidden, down_ref[expert, :, cut], preferred_element_type=wide)
            .astype(low)
            .reshape(blocks, capacity, -1)
        )

    @pl.when(expert == experts - 1)
    def _():
        combine_blocks(spread_ref, y_ref, out_refs)


def backward_body(n_x, n_out, n_keep, *refs):
    x_refs, refs = refs[:n_x], refs[n_x:]
    (table_ref, place_ref, up_ref, down_ref, gate_up_ref), refs = refs[:5], refs[5 + n_keep :]
    out_refs, (rows_ref, grad_ref, y_ref, spread_ref) = refs[:n_out], refs[n_out:]
    expert = pl.program_id(0)
    blocks, capacity, width = rows_ref.shape[1:]
    experts = y_ref.shape[1] // capacity

    @pl.when(expert == 0)
    def _():
        fill_spread(place_ref, spread_ref, capacity)

    half = down_ref.shape[1]
    rows, weight = take_rows(x_refs, table_ref, rows_ref)
    grad_hidden = nt_dot(rows, down_ref[expert]) * weight
    gate_up = gate_up_ref[0].reshape(blocks * capacity, 2 * half)
    gate_part = gate_up[:, :half]
    up_part = gate_up[:, half:]
    sigmoid = jax.nn.sigmoid(gate_part)
    grad_gate = grad_hidden * up_part * sigmoid * (1.0 + gate_part * (1.0 - sigmoid))
    grad_up = grad_hidden * gate_part * sigmoid
    grad_rows = jnp.concatenate([grad_gate, grad_up], axis=1).astype(low)
    grad_ref[0] = grad_rows.reshape(blocks, capacity, 2 * half)
    begin = pl.multiple_of(expert * capacity, 16)
    for cut in tiles_of(width):
        y_ref[:, pl.ds(begin, capacity), cut] = (
            nt_dot(grad_rows, up_ref[expert, cut, :]).astype(low).reshape(blocks, capacity, -1)
        )

    @pl.when(expert == experts - 1)
    def _():
        combine_blocks(spread_ref, y_ref, out_refs)


def expert_call(begin, pieces, table, place, w_up, w_down, gate_up, kept, capacity, total):
    blocks, experts, _, slots = table.shape
    width = w_up.shape[1]
    double, half = w_up.shape[2], w_down.shape[1]
    backward = gate_up is not None
    once = pl.Buffered(1)
    row_spec = lambda last: pl.BlockSpec(
        (1, blocks, capacity, last), lambda e: (e, begin // blocks, 0, 0)
    )
    row_shape = lambda last, kind: pltpu.HBM((experts, total, capacity, last), kind)
    whole = lambda shape: pl.BlockSpec(shape, lambda e: (0,) * len(shape), pipeline_mode=once)
    in_specs = [whole(p.shape) for p in pieces] + [
        pl.BlockSpec((blocks, 1, 2, slots), lambda e: (0, e, 0, 0)),
        whole((blocks, slots, experts)),
        pl.BlockSpec(memory_space=pltpu.VMEM),
        pl.BlockSpec(memory_space=pltpu.VMEM),
    ]
    operands = [*pieces, table, place, w_up, w_down]
    n_out = blocks
    out_specs = [whole((slots, width))] * n_out + [row_spec(width), row_spec(double)]
    out_shape = [jax.ShapeDtypeStruct((slots, width), low)] * n_out + [row_shape(width, low)]
    if backward:
        in_specs.append(row_spec(double))
        operands.append(pltpu.with_memory_space_constraint(gate_up, pltpu.HBM))
        out_shape.append(row_shape(double, low))
    else:
        out_specs.append(row_spec(half))
        out_shape += [row_shape(double, wide), row_shape(half, low)]
    aliases = {len(operands) + i: n_out + i for i in range(len(kept))}
    rows = experts * blocks * capacity
    body = functools.partial(
        backward_body if backward else forward_body, len(pieces), n_out, len(kept)
    )
    made = pl.pallas_call(
        body,
        grid=(experts,),
        in_specs=in_specs + [pl.BlockSpec(memory_space=pl.ANY)] * len(kept),
        out_specs=out_specs,
        out_shape=out_shape,
        input_output_aliases=aliases,
        scratch_shapes=[
            pltpu.VMEM((blocks, experts * capacity, width), low),
            pltpu.VMEM((blocks, slots, experts * capacity), low),
        ],
        compiler_params=pltpu.CompilerParams(
            dimension_semantics=("arbitrary",), vmem_limit_bytes=(28 if backward else 28) << 20
        ),
        cost_estimate=pl.CostEstimate(
            flops=2 * rows * width * (2 * slots + double + half),
            bytes_accessed=4 * blocks * slots * width + rows * (2 * width + 6 * double),
            transcendentals=rows * half,
        ),
    )(*operands, *kept)
    return (made[:n_out], made[n_out:])


def on_chip(*arrays):
    count = len(arrays)

    def body(*refs):
        sources, targets, sems = refs[:count], refs[count : 2 * count], refs[-1]
        copies = [
            pltpu.make_async_copy(sources[i], targets[i], sems.at[i]) for i in range(count)
        ]
        for copy in copies:
            copy.start()
        for copy in copies:
            copy.wait()

    return pl.pallas_call(
        body,
        in_specs=[pl.BlockSpec(memory_space=pltpu.HBM)] * count,
        out_specs=[pl.BlockSpec(memory_space=pltpu.VMEM)] * count,
        out_shape=[pltpu.VMEM(a.shape, a.dtype) for a in arrays],
        scratch_shapes=[pltpu.SemaphoreType.DMA((count,))],
        compiler_params=pltpu.CompilerParams(vmem_limit_bytes=24 << 20),
    )(*[pltpu.with_memory_space_constraint(a, pltpu.HBM) for a in arrays])


def added(left, right):
    return left.astype(wide) + right.astype(wide)


def tie(values, *anchors):
    return lax.optimization_barrier((values, anchors))[0]


def sum_everywhere(values):
    values = values[None]
    for axis in everywhere:
        size, step = lax.axis_size(axis), 1
        while step < size:
            pairs = [(i, i ^ step) for i in range(size)]
            values = values + lax.ppermute(values, axis, pairs)
            step *= 2
    return values[0]


def line_gather(shard):
    size = lax.axis_size("tp")
    if size > 4:
        return lax.all_gather(shard, "tp", axis=0, tiled=True)
    move = lambda d: lax.ppermute(
        shard, "tp", [(i, i + d) for i in range(size) if 0 <= i + d < size]
    )
    near = [move(d) for d in range(size - 1, 0, -1)] + [shard] + [move(-d) for d in range(1, size)]
    rows = shard.shape[0]
    begin = (size - 1 - lax.axis_index("tp")) * rows
    return lax.dynamic_slice_in_dim(jnp.concatenate(near, axis=0), begin, size * rows, 0)


class Plane:
    def __init__(self):
        self.fsdp, self.ctx = lax.axis_size("fsdp"), lax.axis_size("ctx")
        self.tree = self.fsdp == 4 and self.ctx == 2
        self.shards = self.fsdp * self.ctx

    def core(self, a):
        return lax.ppermute(a, "fsdp", [(i, i ^ 1) for i in range(self.fsdp)])

    def along_x(self, a):
        return lax.ppermute(a, "fsdp", [(i, i ^ 2) for i in range(self.fsdp)])

    def along_y(self, a):
        return lax.ppermute(a, "ctx", [(i, i ^ 1) for i in range(self.ctx)])

    def order(self):
        if not self.tree:
            return list(range(self.shards))
        fsdp, ctx = lax.axis_index("fsdp"), lax.axis_index("ctx")
        chips = ((0, 0), (1, 0), (0, 1), (1, 1))
        return [(fsdp ^ (2 * x) ^ core) * 2 + (ctx ^ y) for x, y in chips for core in (0, 1)]

    def gather_whole(self, shard):
        rows = shard.shape[0]
        if not self.tree:
            return lax.all_gather(shard, plane, axis=0, tiled=True)
        halves = (shard[: rows // 2], shard[rows // 2 :]) if rows > 1 else (shard,)
        x = [self.along_x(h) for h in halves]
        y = [self.along_y(h) for h in halves]
        far = [self.along_y(x[0])] + [self.along_x(h) for h in y[1:]]
        whole = jnp.zeros((self.shards * rows, *shard.shape[1:]), shard.dtype)
        order = self.order()
        for c, pieces in enumerate((halves, x, y, far)):
            for core in (0, 1):
                begin = order[2 * c + core] * rows
                for piece in pieces:
                    found = self.core(piece) if core else piece
                    whole = lax.dynamic_update_slice_in_dim(whole, found, begin, 0)
                    begin = begin + piece.shape[0]
        return whole

    def reduce_whole(self, partial):
        rows = partial.shape[0] // self.shards
        if not self.tree:
            return lax.psum_scatter(partial, plane, scatter_dimension=0, tiled=True).astype(wide)
        blocks = [lax.dynamic_slice_in_dim(partial, i * rows, rows, 0) for i in self.order()]
        pre = [added(blocks[2 * c], self.core(blocks[2 * c + 1])) for c in range(4)]
        cuts = tiles_of(partial.shape[1], partial.shape[1] // 2)
        return jnp.concatenate(
            [self.total(k, *[p[:, cut] for p in pre]) for k, cut in enumerate(cuts)], axis=1
        )

    def total(self, k, own, near_x, near_y, far):
        if k % 2 == 0:
            near_y = near_y + self.along_x(far.astype(low)).astype(wide)
        else:
            near_x = near_x + self.along_y(far.astype(low)).astype(wide)
        from_x, from_y = self.along_x(near_x.astype(low)), self.along_y(near_y.astype(low))
        return own + from_x.astype(wide) + from_y.astype(wide)

    def experts(self, first, second, call, filler):
        if not self.tree:
            split = lambda a: jnp.split(lax.all_gather(a, plane, axis=0, tiled=True), self.shards)
            halves, made = list(zip(split(first), split(second), strict=True)), []
            for i in range(0, self.shards, 2):
                made += call(i, [*halves[i], *halves[i + 1]])
            return lax.psum_scatter(
                jnp.concatenate(made, axis=0), plane, scatter_dimension=0, tiled=True
            )
        step = first.shape[1]
        pre = lambda made, other: [
            added(made[:, k * step : (k + 1) * step], other[:, k * step : (k + 1) * step])
            for k in range(2)
        ]
        narrow = lambda a: a.astype(low)
        x_first, y_first = self.along_x(first), self.along_y(first)
        second = tie(second, x_first, y_first)
        own_pieces = [first, second, self.core(first), self.core(second)]
        x_second, y_second = self.along_x(second), self.along_y(second)
        over_x, over_y = self.core(x_first), self.core(y_first)
        own = call(0, tie(own_pieces, over_x, over_y))
        x_second, y_second = tie((x_second, y_second), own[0])
        far = [self.along_y(x_first), self.along_x(y_second)]
        over_y = [over_y, self.core(y_second)]
        near_x = call(2, [x_first, x_second, over_x, self.core(x_second)])
        near_x = tie(near_x, over_y)
        other_own, other_x = self.core(own[1]), self.core(near_x[1])
        far += [self.core(piece) for piece in far]
        near_y = tie(call(4, [y_first, y_second, *over_y]), other_own, other_x, far)
        other_y = self.core(near_y[1])
        sum_x, sum_y = pre(near_x[0], other_x), pre(near_y[0], other_y)
        early_x, early_y = narrow(sum_x[0]), narrow(sum_y[1])
        last = call(6, tie(far, early_x, early_y))
        sent = [self.along_x(early_x), self.along_y(early_y)]
        last = tie(last, sent)
        sum_far = pre(last[0], self.core(last[1]))
        sum_own = pre(own[0], other_own)
        fillers = iter(filler())
        far = [self.along_x(narrow(sum_far[0])), self.along_y(narrow(sum_far[1]))]
        far = tie(far, next(fillers))
        near = [
            self.along_y(narrow(added(sum_y[0], far[0]))),
            self.along_x(narrow(added(sum_x[1], far[1]))),
        ]
        near = tie(near, next(fillers))
        return jnp.concatenate(
            [added(sum_own[k], sent[k]) + near[k].astype(wide) for k in range(2)], axis=1
        ).astype(low)


def per_device(
    states,
    teacher,
    lengths,
    routes,
    gate_weights,
    w_qkv,
    w_out,
    norm_gains,
    qk_gains,
    w_gate_up,
    w_down,
):
    seq_count, slot_count, width = states.shape
    top_count = routes.shape[-1]
    ctx_size = lax.axis_size("ctx")
    tp_size = lax.axis_size("tp")
    shards = lax.axis_size(plane)
    ctx_index = lax.axis_index("ctx")
    tp_index = lax.axis_index("tp")
    plane_index = lax.axis_index(plane)
    tokens = seq_count * slot_count
    part = tokens // tp_size
    shard_experts = w_gate_up.shape[0]
    hidden_local = w_gate_up.shape[3]
    experts = shard_experts * shards
    capacity = 5 * tokens * top_count // (4 * experts)
    own_slots = jnp.arange(slot_count, dtype=jnp.int32)
    position = ctx_index * slot_count + own_slots
    tok_position = jnp.tile(position, seq_count)
    row_valid = (position[None, :] < lengths[:, None]).reshape(tokens).astype(wide)
    mirror = [(i, (i + 1) % ctx_size) for i in range(ctx_size)]

    gain_cols, head_cols = norm_gains.shape[1], qk_gains.shape[1]
    small = jnp.concatenate(
        [
            norm_gains.astype(wide).reshape(-1),
            qk_gains.astype(wide).reshape(-1),
            jnp.sum(lengths).astype(wide)[None],
        ]
    )
    places = Plane()
    small_all = places.gather_whole(small[None])
    gain_rows = small_all[:, : 2 * gain_cols].reshape(shards, 2, gain_cols)
    full_gains = jnp.swapaxes(gain_rows, 0, 1).reshape(2, shards * gain_cols)
    head_rows = small_all[:, 2 * gain_cols : 2 * (gain_cols + head_cols)]
    qk_float = jnp.swapaxes(head_rows.reshape(shards, 2, head_cols), 0, 1).reshape(
        2, shards * head_cols
    )
    valid_count = jnp.sum(small_all[:, -1]) / ctx_size
    gain_attn, gain_ffn = full_gains[0], full_gains[1]
    head_dim = qk_float.shape[1]
    heads_local = w_qkv.shape[2] // head_dim
    score_scale = head_dim ** (-0.5)

    tables = route_tables(
        routes.reshape(tokens, top_count), gate_weights.reshape(tokens, top_count), experts
    )
    table = lax.all_to_all(tables, plane, split_axis=0, concat_axis=0, tiled=True).reshape(
        shards, shard_experts, 2, tokens
    )
    rank = table[:, :, 0].astype(jnp.int32)
    offset = (jnp.arange(shard_experts, dtype=jnp.int32) * capacity)[None, :, None]
    place = jnp.swapaxes(jnp.where(rank >= 0, rank + offset, -1), 1, 2)
    w_up = w_gate_up.reshape(shard_experts, width, 2 * hidden_local)
    order = places.order()
    sort = lambda a: jnp.concatenate(
        [lax.dynamic_slice_in_dim(a, block, 1, 0) for block in order], axis=0
    )
    table, place = sort(table), sort(place)
    some = lambda a, begin, pieces: a[begin : begin + blocks_in(pieces)]

    def blocks_in(pieces):
        return sum(piece.shape[1] for piece in pieces) // width

    full_qkv = lax.all_gather(
        w_qkv.reshape(w_qkv.shape[0], -1), plane, axis=0, tiled=True
    )
    rows_out = tie(line_gather(w_out), full_qkv[:1])
    full_out = lax.all_gather(rows_out, plane, axis=1, tiled=True)
    flat_states = states.astype(wide).reshape(tokens, width)
    normed = rms_norm(flat_states, gain_attn).astype(low)
    projected = jnp.dot(normed, full_qkv, preferred_element_type=wide).reshape(
        tokens, 3, heads_local, head_dim
    )

    def prepare_query(projected_in, gain):
        return rotate(rms_norm(projected_in, gain), tok_position)

    queries, query_back = jax.vjp(prepare_query, projected[:, 0], qk_float[0])
    key_states, key_back = jax.vjp(prepare_query, projected[:, 1], qk_float[1])
    query_low = queries.astype(low).reshape(seq_count, slot_count, heads_local, head_dim)
    by_head = lambda a: a.astype(low).reshape(seq_count, slot_count, heads_local, head_dim)
    value_low, key_low = by_head(projected[:, 2]), by_head(key_states)
    other_value = lax.ppermute(value_low, "ctx", mirror)
    other_key = lax.ppermute(key_low, "ctx", mirror)
    gathered_value = jnp.concatenate([value_low, other_value], axis=1)
    gathered_key = jnp.concatenate([key_low, other_key], axis=1)
    other_position = (1 - ctx_index) * slot_count + own_slots
    key_position = jnp.concatenate([position, other_position])
    key_valid = key_position[None, :] < lengths[:, None]
    pieces = [
        attend_sequence(
            query_low[i], gathered_key[i], gathered_value[i], key_valid[i], score_scale
        )
        for i in range(seq_count)
    ]
    attended_low = (
        jnp.stack([p[0] for p in pieces]).astype(low).reshape(tokens, heads_local * head_dim)
    )
    begin = tp_index * part
    own = lambda a: lax.dynamic_slice_in_dim(a, begin, part, 0)
    attended_low, table, place = lax.optimization_barrier((attended_low, table, place))
    attended_own = lax.all_to_all(
        attended_low, "tp", split_axis=0, concat_axis=1, tiled=True
    )
    states_own = own(flat_states)
    middle_own = states_own + jnp.dot(attended_own, full_out, preferred_element_type=wide)
    normed_own = rms_norm(middle_own, gain_ffn).astype(low)

    middle_col = width // 2
    cols = (slice(0, middle_col), slice(middle_col, width))

    def spread(*halves):
        return [lax.all_gather(half.astype(low), "tp", axis=0, tiled=True) for half in halves]

    saved = [()]

    def forward(begin, pieces):
        made, saved[0] = expert_call(
            begin, pieces, some(table, begin, pieces), some(place, begin, pieces), *near_weights,
            None, saved[0], capacity, shards,
        )
        return made

    def finish(half):
        return lax.psum_scatter(half, "tp", scatter_dimension=0, tiled=True).astype(wide)

    teacher_own = own(teacher.reshape(tokens, width)).astype(wide)
    valid_own = own(row_valid)
    grad_scale = (2.0 * loss_scale / valid_count * valid_own)[:, None]
    second_own = normed_own[:, cols[1]]
    first_block, second_block = spread(normed_own[:, cols[0]], second_own)
    second_block, w_up = lax.optimization_barrier((second_block, w_up))
    near_weights = on_chip(w_up, w_down)
    mixture = places.experts(
        first_block,
        second_block,
        forward,
        lambda: ((), ()),
    )
    rows_in, gate_up, hidden = saved[0]
    final_own = middle_own + finish(mixture)
    difference = final_own - teacher_own
    local_loss = jnp.sum(valid_own * jnp.sum(difference * difference, axis=-1))
    grad_final = grad_scale * difference
    spread_halves = spread(grad_final[:, cols[0]], grad_final[:, cols[1]])
    activations = lax.all_gather(final_own.astype(low), "tp", axis=0, tiled=True).reshape(
        seq_count, slot_count, width
    )

    saved[0] = ()

    def backward(begin, pieces):
        made, saved[0] = expert_call(
            begin, pieces, some(table, begin, pieces), some(place, begin, pieces), *back_weights,
            gate_up, saved[0], capacity, shards,
        )
        return made

    def weight_grads():
        rows_back, grad_rows = saved[0]
        made.append(
            jnp.einsum("ebcf,ebcd->efd", hidden, rows_back, preferred_element_type=wide)
        )
        yield [made[0]]
        grad_up = jnp.einsum("ebcd,ebcf->edf", rows_in, grad_rows, preferred_element_type=wide)
        made.append(grad_up)
        yield [grad_up, activations]

    made = []
    first_block, second_block = spread_halves
    second_block, w_up = lax.optimization_barrier((second_block, w_up))
    back_weights = on_chip(w_up, w_down)
    total_in = places.experts(first_block, second_block, backward, weight_grads)
    if not made:
        for _ in weight_grads():
            pass
    grad_down, grad_up = made
    grad_gate_up = with_layout_constraint(
        grad_up.reshape(shard_experts, width, 2, hidden_local),
        Layout(major_to_minor=(0, 1, 2, 3)),
    )
    grad_ffn = tie(finish(total_in), grad_gate_up, grad_down)

    grad_middle_norm, grad_gain_ffn = norm_back(grad_ffn, middle_own, gain_ffn)
    grad_middle = grad_final + grad_middle_norm
    grad_branch = grad_middle.astype(low)

    grad_attended = lax.all_to_all(
        nt_dot(grad_branch, full_out).astype(low), "tp", split_axis=1, concat_axis=0, tiled=True
    )
    grad_heads = grad_attended.reshape(seq_count, slot_count, heads_local, head_dim)
    backs = [
        back_sequence(
            query_low[i],
            gathered_key[i],
            gathered_value[i],
            key_valid[i],
            pieces[i][1],
            grad_heads[i],
            score_scale,
        )
        for i in range(seq_count)
    ]
    grad_query, grad_key, grad_value = [jnp.stack(parts) for parts in zip(*backs, strict=True)]

    def returned(grad):
        coming = lax.ppermute(grad[:, slot_count:].astype(low), "ctx", mirror)
        return added(grad[:, :slot_count], coming).reshape(tokens, heads_local, head_dim)

    branch_block = lax.all_gather(grad_branch, "tp", axis=0, tiled=True)
    grad_v, own_key = returned(grad_value), returned(grad_key)
    grad_v, branch_block = lax.optimization_barrier((grad_v, branch_block))
    grad_w_out = jnp.einsum("nd,nf->df", branch_block, attended_low, preferred_element_type=wide)
    grad_q, grad_q_gain = query_back(grad_query.reshape(tokens, heads_local, head_dim))
    grad_k, grad_k_gain = key_back(own_key)
    flat = lambda a: a.astype(low).reshape(tokens, -1)
    grad_proj_low = jnp.concatenate([flat(grad_q), flat(grad_k), flat(grad_v)], axis=1)
    grad_qk = jnp.stack([grad_q_gain, grad_k_gain])
    grad_normed = lax.psum_scatter(
        nt_dot(grad_proj_low, full_qkv).astype(low),
        "tp",
        scatter_dimension=0,
        tiled=True,
    ).astype(wide)
    grad_w_qkv = jnp.einsum("nd,nk->dk", normed, grad_proj_low, preferred_element_type=wide)
    grad_states_norm, grad_gain_attn = norm_back(grad_normed, states_own, gain_attn)
    grad_states = (
        lax.all_gather((grad_middle + grad_states_norm).astype(low), "tp", axis=0, tiled=True)
        .astype(wide)
        .reshape(seq_count, slot_count, width)
    )
    sums = sum_everywhere(
        jnp.concatenate([grad_gain_attn, grad_gain_ffn, grad_qk.reshape(-1), local_loss[None]])
    )
    out_gains = lax.dynamic_slice_in_dim(
        sums[: 2 * width].reshape(2, width), plane_index * gain_cols, gain_cols, 1
    )
    out_qk = lax.dynamic_slice_in_dim(
        sums[2 * width : 2 * (width + head_dim)].reshape(2, head_dim),
        plane_index * head_cols,
        head_cols,
        1,
    )
    loss_value = sums[-1] / valid_count
    weights_own = places.reduce_whole(
        jnp.concatenate([grad_w_qkv.astype(low), grad_w_out.astype(low)], axis=1)
    )
    qkv_cols = grad_w_qkv.shape[1]
    out_qkv = weights_own[:, :qkv_cols].reshape(w_qkv.shape)
    out_w_out = weights_own[:, qkv_cols:].T
    return (
        activations,
        loss_value,
        valid_count,
        grad_states,
        out_qkv,
        out_w_out,
        out_gains,
        out_qk,
        grad_gate_up,
        grad_down,
    )


def solution(mesh):
    placed = (
        P("fsdp", "ctx", None),
        P("fsdp", "ctx", None),
        P("fsdp"),
        P("fsdp", "ctx", None),
        P("fsdp", "ctx", None),
        P(("fsdp", "ctx"), None, "tp"),
        P("tp", ("fsdp", "ctx")),
        P(None, ("fsdp", "ctx")),
        P(None, ("fsdp", "ctx")),
        P(("fsdp", "ctx"), None, None, "tp"),
        P(("fsdp", "ctx"), "tp", None),
    )
    return jax.shard_map(
        per_device,
        mesh=mesh,
        in_specs=placed,
        out_specs=(
            P("fsdp", "ctx", None),
            P(),
            P(),
            P("fsdp", "ctx", None),
            P(("fsdp", "ctx"), None, "tp"),
            P("tp", ("fsdp", "ctx")),
            P(None, ("fsdp", "ctx")),
            P(None, ("fsdp", "ctx")),
            P(("fsdp", "ctx"), None, None, "tp"),
            P(("fsdp", "ctx"), "tp", None),
        ),
        check_vma=False,
    )
```

```python
import functools

import jax
import jax.numpy as jnp
from jax import lax
from jax.experimental.layout import Layout, with_layout_constraint
from jax.experimental import pallas as pl
from jax.experimental.pallas import tpu as pltpu
from jax.sharding import PartitionSpec as P

norm_eps = 1e-05
rope_base = 10000.0
loss_scale = 4096.0
masked_score = -1e30
plane = ("fsdp", "ctx")
everywhere = ("fsdp", "ctx", "tp")
low = jnp.bfloat16
wide = jnp.float32


def rms_norm(values, gain_vec):
    return (
        values * lax.rsqrt(jnp.mean(values * values, axis=-1, keepdims=True) + norm_eps) * gain_vec
    )


def norm_back(grad_normed, values, gain_vec):
    inverse = lax.rsqrt(jnp.mean(values * values, axis=-1, keepdims=True) + norm_eps)
    scaled = values * inverse
    grad_scaled = grad_normed * gain_vec
    grad_values = inverse * (
        grad_scaled - scaled * jnp.mean(grad_scaled * scaled, axis=-1, keepdims=True)
    )
    return (grad_values, jnp.sum(grad_normed * scaled, axis=0))


def rotate(values, position):
    half_dim = values.shape[-1] // 2
    frequency = rope_base ** (-2.0 * jnp.arange(half_dim, dtype=wide) / values.shape[-1])
    angles = position.astype(wide)[:, None] * frequency[None, :]
    cosine = jnp.cos(angles)[:, None, :]
    sine_part = jnp.sin(angles)[:, None, :]
    first_half = values[..., :half_dim]
    second_half = values[..., half_dim:]
    return jnp.concatenate(
        [
            first_half * cosine - second_half * sine_part,
            second_half * cosine + first_half * sine_part,
        ],
        axis=-1,
    )


def prepare(projected, qk_float, position):
    queries = rotate(rms_norm(projected[:, 0], qk_float[0]), position)
    key_states = rotate(rms_norm(projected[:, 1], qk_float[1]), position)
    return (queries, key_states, projected[:, 2])


def attend_sequence(query_seq, key_seq, value_seq, valid_seq, score_scale):
    scores = (
        jnp.einsum("qhd,khd->hqk", query_seq, key_seq, preferred_element_type=wide)
        * score_scale
    )
    scores = jnp.where(valid_seq[None, None, :], scores, masked_score)
    peak_score = jnp.max(scores, axis=-1, keepdims=True)
    exponent = jnp.exp(scores - peak_score)
    row_total = jnp.sum(exponent, axis=-1, keepdims=True)
    probability = (exponent / row_total).astype(low)
    output = jnp.einsum("hqk,khd->qhd", probability, value_seq, preferred_element_type=wide)
    return (output, (peak_score + jnp.log(row_total))[..., 0])


def back_sequence(query_seq, key_seq, value_seq, valid_seq, log_seq, grad_seq, score_scale):
    scores = (
        jnp.einsum("qhd,khd->hqk", query_seq, key_seq, preferred_element_type=wide)
        * score_scale
    )
    scores = jnp.where(valid_seq[None, None, :], scores, masked_score)
    probability = jnp.exp(scores - log_seq[..., None])
    grad_prob = jnp.einsum("qhd,khd->hqk", grad_seq, value_seq, preferred_element_type=wide)
    grad_scores = (
        probability * (grad_prob - jnp.sum(probability * grad_prob, axis=-1, keepdims=True))
    ).astype(low)
    grad_query = (
        jnp.einsum("hqk,khd->qhd", grad_scores, key_seq, preferred_element_type=wide)
        * score_scale
    )
    grad_key = (
        jnp.einsum("hqk,qhd->khd", grad_scores, query_seq, preferred_element_type=wide)
        * score_scale
    )
    grad_value = jnp.einsum(
        "hqk,qhd->khd", probability.astype(low), grad_seq, preferred_element_type=wide
    )
    return (grad_query, grad_key, grad_value)


def route_tables(route_rows, gate_rows, experts):
    slots = route_rows.shape[0]
    hit = route_rows[None, :, :] == jnp.arange(experts, dtype=jnp.int32)[:, None, None]
    named = jnp.sum(hit.astype(wide), axis=-1)
    gates = jnp.sum(jnp.where(hit, gate_rows[None, :, :], 0.0), axis=-1)
    order = jnp.arange(slots, dtype=jnp.int32)
    before = (order[:, None] < order[None, :]).astype(low)
    rank = jnp.dot(named.astype(low), before, preferred_element_type=wide)
    return jnp.stack([jnp.where(named > 0.0, rank, -1.0), gates], axis=1)


def pick_rows(table_ref, block, capacity, slots):
    rank = table_ref[block, 0, 0:1, :].astype(jnp.int32)
    gate = table_ref[block, 0, 1:2, :]
    match = lax.broadcasted_iota(jnp.int32, (capacity, slots), 0) == rank
    chosen = jnp.where(match, 1.0, 0.0).astype(low)
    weight = jnp.sum(jnp.where(match, gate, 0.0), axis=1, keepdims=True)
    return (chosen, weight)


def spread_rows(place_ref, block, experts, capacity, slots):
    column = lax.broadcasted_iota(jnp.int32, (slots, experts * capacity), 1)
    match = column == place_ref[block, :, 0:1]
    for expert in range(1, experts):
        match = match | (column == place_ref[block, :, expert : expert + 1])
    return jnp.where(match, 1.0, 0.0).astype(low)


def nt_dot(left, right):
    return lax.dot_general(left, right, (((1,), (1,)), ((), ())), preferred_element_type=wide)


def tiles_of(width, most=512):
    step = min(width, most)
    return [slice(begin, begin + step) for begin in range(0, width, step)]


def take_rows(x_refs, table_ref, rows_ref):
    blocks, capacity, width = rows_ref.shape[1:]
    slots = table_ref.shape[3]
    weights, place = [], 0
    for block in range(blocks):
        chosen, weight = pick_rows(table_ref, block, capacity, slots)
        weights.append(weight)
        done = 0
        while done < width:
            x_ref = x_refs[place]
            for cut in tiles_of(x_ref.shape[1]):
                rows_ref[0, block, :, done + cut.start : done + cut.stop] = jnp.dot(
                    chosen, x_ref[:, cut], preferred_element_type=wide
                ).astype(low)
            done, place = done + x_ref.shape[1], place + 1
    return (rows_ref[0].reshape(blocks * capacity, width), jnp.concatenate(weights, axis=0))


def fill_spread(place_ref, spread_ref, capacity):
    blocks, slots, total = spread_ref.shape
    for block in range(blocks):
        spread_ref[block] = spread_rows(place_ref, block, total // capacity, capacity, slots)


def combine_blocks(spread_ref, y_ref, out_refs):
    for block, out_ref in enumerate(out_refs):
        for cut in tiles_of(y_ref.shape[2]):
            out_ref[:, cut] = jnp.dot(
                spread_ref[block], y_ref[block, :, cut], preferred_element_type=wide
            ).astype(low)


def forward_body(n_x, n_out, n_keep, *refs):
    x_refs, refs = refs[:n_x], refs[n_x:]
    (table_ref, place_ref, up_ref, down_ref), refs = refs[:4], refs[4 + n_keep :]
    out_refs, (rows_ref, gate_up_ref, hidden_ref, y_ref, spread_ref) = refs[:n_out], refs[n_out:]
    expert = pl.program_id(0)
    blocks, capacity, width = rows_ref.shape[1:]
    experts = y_ref.shape[1] // capacity

    @pl.when(expert == 0)
    def _():
        fill_spread(place_ref, spread_ref, capacity)

    half = down_ref.shape[1]
    rows, weight = take_rows(x_refs, table_ref, rows_ref)
    gate_up = jnp.dot(rows, up_ref[expert], preferred_element_type=wide)
    gate_up_ref[0] = gate_up.reshape(blocks, capacity, 2 * half)
    gate_part = gate_up[:, :half]
    up_part = gate_up[:, half:]
    hidden = (gate_part * jax.nn.sigmoid(gate_part) * up_part * weight).astype(low)
    hidden_ref[0] = hidden.reshape(blocks, capacity, half)
    begin = pl.multiple_of(expert * capacity, 16)
    for cut in tiles_of(width):
        y_ref[:, pl.ds(begin, capacity), cut] = (
            jnp.dot(hidden, down_ref[expert, :, cut], preferred_element_type=wide)
            .astype(low)
            .reshape(blocks, capacity, -1)
        )

    @pl.when(expert == experts - 1)
    def _():
        combine_blocks(spread_ref, y_ref, out_refs)


def backward_body(n_x, n_out, n_keep, *refs):
    x_refs, refs = refs[:n_x], refs[n_x:]
    (table_ref, place_ref, up_ref, down_ref, gate_up_ref), refs = refs[:5], refs[5 + n_keep :]
    out_refs, (rows_ref, grad_ref, y_ref, spread_ref) = refs[:n_out], refs[n_out:]
    expert = pl.program_id(0)
    blocks, capacity, width = rows_ref.shape[1:]
    experts = y_ref.shape[1] // capacity

    @pl.when(expert == 0)
    def _():
        fill_spread(place_ref, spread_ref, capacity)

    half = down_ref.shape[1]
    rows, weight = take_rows(x_refs, table_ref, rows_ref)
    grad_hidden = nt_dot(rows, down_ref[expert]) * weight
    gate_up = gate_up_ref[0].reshape(blocks * capacity, 2 * half)
    gate_part = gate_up[:, :half]
    up_part = gate_up[:, half:]
    sigmoid = jax.nn.sigmoid(gate_part)
    grad_gate = grad_hidden * up_part * sigmoid * (1.0 + gate_part * (1.0 - sigmoid))
    grad_up = grad_hidden * gate_part * sigmoid
    grad_rows = jnp.concatenate([grad_gate, grad_up], axis=1).astype(low)
    grad_ref[0] = grad_rows.reshape(blocks, capacity, 2 * half)
    begin = pl.multiple_of(expert * capacity, 16)
    for cut in tiles_of(width):
        y_ref[:, pl.ds(begin, capacity), cut] = (
            nt_dot(grad_rows, up_ref[expert, cut, :]).astype(low).reshape(blocks, capacity, -1)
        )

    @pl.when(expert == experts - 1)
    def _():
        combine_blocks(spread_ref, y_ref, out_refs)


def expert_call(begin, pieces, table, place, w_up, w_down, gate_up, kept, capacity, total):
    blocks, experts, _, slots = table.shape
    width = w_up.shape[1]
    double, half = w_up.shape[2], w_down.shape[1]
    backward = gate_up is not None
    once = pl.Buffered(1)
    row_spec = lambda last: pl.BlockSpec(
        (1, blocks, capacity, last), lambda e: (e, begin // blocks, 0, 0)
    )
    row_shape = lambda last, kind: pltpu.HBM((experts, total, capacity, last), kind)
    whole = lambda shape: pl.BlockSpec(shape, lambda e: (0,) * len(shape), pipeline_mode=once)
    in_specs = [pl.BlockSpec(memory_space=pltpu.VMEM)] * len(pieces) + [
        pl.BlockSpec((blocks, 1, 2, slots), lambda e: (0, e, 0, 0)),
        whole((blocks, slots, experts)),
        pl.BlockSpec(memory_space=pltpu.VMEM),
        pl.BlockSpec(memory_space=pltpu.VMEM),
    ]
    held = [pltpu.with_memory_space_constraint(p, pltpu.VMEM) for p in pieces]
    operands = [*held, table, place, w_up, w_down]
    n_out = blocks
    out_specs = [pl.BlockSpec(memory_space=pltpu.VMEM)] * n_out + [row_spec(width), row_spec(double)]
    out_shape = [pltpu.VMEM((slots, width), low)] * n_out + [row_shape(width, low)]
    if backward:
        in_specs.append(row_spec(double))
        operands.append(pltpu.with_memory_space_constraint(gate_up, pltpu.HBM))
        out_shape.append(row_shape(double, low))
    else:
        out_specs.append(row_spec(half))
        out_shape += [row_shape(double, wide), row_shape(half, low)]
    aliases = {len(operands) + i: n_out + i for i in range(len(kept))}
    rows = experts * blocks * capacity
    body = functools.partial(
        backward_body if backward else forward_body, len(pieces), n_out, len(kept)
    )
    made = pl.pallas_call(
        body,
        grid=(experts,),
        in_specs=in_specs + [pl.BlockSpec(memory_space=pl.ANY)] * len(kept),
        out_specs=out_specs,
        out_shape=out_shape,
        input_output_aliases=aliases,
        scratch_shapes=[
            pltpu.VMEM((blocks, experts * capacity, width), low),
            pltpu.VMEM((blocks, slots, experts * capacity), low),
        ],
        compiler_params=pltpu.CompilerParams(
            dimension_semantics=("arbitrary",), vmem_limit_bytes=20 << 20
        ),
        cost_estimate=pl.CostEstimate(
            flops=2 * rows * width * (2 * slots + double + half),
            bytes_accessed=4 * blocks * slots * width + rows * (2 * width + 6 * double),
            transcendentals=rows * half,
        ),
    )(*operands, *kept)
    return (made[:n_out], made[n_out:])


def on_chip(*arrays):
    count = len(arrays)

    def body(*refs):
        sources, targets, sems = refs[:count], refs[count : 2 * count], refs[-1]
        copies = [
            pltpu.make_async_copy(sources[i], targets[i], sems.at[i]) for i in range(count)
        ]
        for copy in copies:
            copy.start()
        for copy in copies:
            copy.wait()

    return pl.pallas_call(
        body,
        in_specs=[pl.BlockSpec(memory_space=pltpu.HBM)] * count,
        out_specs=[pl.BlockSpec(memory_space=pltpu.VMEM)] * count,
        out_shape=[pltpu.VMEM(a.shape, a.dtype) for a in arrays],
        scratch_shapes=[pltpu.SemaphoreType.DMA((count,))],
        compiler_params=pltpu.CompilerParams(vmem_limit_bytes=24 << 20),
    )(*[pltpu.with_memory_space_constraint(a, pltpu.HBM) for a in arrays])


def added(left, right):
    return left.astype(wide) + right.astype(wide)


def tie(values, *anchors):
    return lax.optimization_barrier((values, anchors))[0]


def sum_everywhere(values):
    values = values[None]
    for axis in everywhere:
        size, step = lax.axis_size(axis), 1
        while step < size:
            pairs = [(i, i ^ step) for i in range(size)]
            values = values + lax.ppermute(values, axis, pairs)
            step *= 2
    return values[0]


def line_gather(shard):
    size = lax.axis_size("tp")
    if size > 4:
        return lax.all_gather(shard, "tp", axis=0, tiled=True)
    move = lambda d: lax.ppermute(
        shard, "tp", [(i, i + d) for i in range(size) if 0 <= i + d < size]
    )
    near = [move(d) for d in range(size - 1, 0, -1)] + [shard] + [move(-d) for d in range(1, size)]
    rows = shard.shape[0]
    begin = (size - 1 - lax.axis_index("tp")) * rows
    return lax.dynamic_slice_in_dim(jnp.concatenate(near, axis=0), begin, size * rows, 0)


class Plane:
    def __init__(self):
        self.fsdp, self.ctx = lax.axis_size("fsdp"), lax.axis_size("ctx")
        self.tree = self.fsdp == 4 and self.ctx == 2
        self.shards = self.fsdp * self.ctx

    def core(self, a):
        return lax.ppermute(a, "fsdp", [(i, i ^ 1) for i in range(self.fsdp)])

    def along_x(self, a):
        return lax.ppermute(a, "fsdp", [(i, i ^ 2) for i in range(self.fsdp)])

    def along_y(self, a):
        return lax.ppermute(a, "ctx", [(i, i ^ 1) for i in range(self.ctx)])

    def order(self):
        if not self.tree:
            return list(range(self.shards))
        fsdp, ctx = lax.axis_index("fsdp"), lax.axis_index("ctx")
        chips = ((0, 0), (1, 0), (0, 1), (1, 1))
        return [(fsdp ^ (2 * x) ^ core) * 2 + (ctx ^ y) for x, y in chips for core in (0, 1)]

    def gather_whole(self, shard):
        rows = shard.shape[0]
        if not self.tree:
            return lax.all_gather(shard, plane, axis=0, tiled=True)
        halves = (shard[: rows // 2], shard[rows // 2 :]) if rows > 1 else (shard,)
        x = [self.along_x(h) for h in halves]
        y = [self.along_y(h) for h in halves]
        far = [self.along_y(x[0])] + [self.along_x(h) for h in y[1:]]
        whole = jnp.zeros((self.shards * rows, *shard.shape[1:]), shard.dtype)
        order = self.order()
        for c, pieces in enumerate((halves, x, y, far)):
            for core in (0, 1):
                begin = order[2 * c + core] * rows
                for piece in pieces:
                    found = self.core(piece) if core else piece
                    whole = lax.dynamic_update_slice_in_dim(whole, found, begin, 0)
                    begin = begin + piece.shape[0]
        return whole

    def reduce_whole(self, partial):
        rows = partial.shape[0] // self.shards
        if not self.tree:
            return lax.psum_scatter(partial, plane, scatter_dimension=0, tiled=True).astype(wide)
        blocks = [lax.dynamic_slice_in_dim(partial, i * rows, rows, 0) for i in self.order()]
        pre = [added(blocks[2 * c], self.core(blocks[2 * c + 1])) for c in range(4)]
        cuts = tiles_of(partial.shape[1], partial.shape[1] // 2)
        return jnp.concatenate(
            [self.total(k, *[p[:, cut] for p in pre]) for k, cut in enumerate(cuts)], axis=1
        )

    def total(self, k, own, near_x, near_y, far):
        if k % 2 == 0:
            near_y = near_y + self.along_x(far.astype(low)).astype(wide)
        else:
            near_x = near_x + self.along_y(far.astype(low)).astype(wide)
        from_x, from_y = self.along_x(near_x.astype(low)), self.along_y(near_y.astype(low))
        return own + from_x.astype(wide) + from_y.astype(wide)

    def experts(self, first, second, call, filler):
        if not self.tree:
            split = lambda a: jnp.split(lax.all_gather(a, plane, axis=0, tiled=True), self.shards)
            halves, made = list(zip(split(first), split(second), strict=True)), []
            for i in range(0, self.shards, 2):
                made += call(i, [*halves[i], *halves[i + 1]])
            return lax.psum_scatter(
                jnp.concatenate(made, axis=0), plane, scatter_dimension=0, tiled=True
            )
        step = first.shape[1]
        pre = lambda made, other: [
            added(made[:, k * step : (k + 1) * step], other[:, k * step : (k + 1) * step])
            for k in range(2)
        ]
        narrow = lambda a: a.astype(low)
        x_first, y_first = self.along_x(first), self.along_y(first)
        second = tie(second, x_first, y_first)
        own_pieces = [first, second, self.core(first), self.core(second)]
        x_second, y_second = self.along_x(second), self.along_y(second)
        over_x, over_y = self.core(x_first), self.core(y_first)
        own = call(0, tie(own_pieces, over_x, over_y))
        x_second, y_second = tie((x_second, y_second), own[0])
        far = [self.along_y(x_first), self.along_x(y_second)]
        over_y = [over_y, self.core(y_second)]
        near_x = call(2, [x_first, x_second, over_x, self.core(x_second)])
        near_x = tie(near_x, over_y)
        other_own, other_x = self.core(own[1]), self.core(near_x[1])
        far += [self.core(piece) for piece in far]
        near_y = tie(call(4, [y_first, y_second, *over_y]), other_own, other_x, far)
        other_y = self.core(near_y[1])
        sum_x, sum_y = pre(near_x[0], other_x), pre(near_y[0], other_y)
        early_x, early_y = narrow(sum_x[0]), narrow(sum_y[1])
        last = call(6, tie(far, early_x, early_y))
        sent = [self.along_x(early_x), self.along_y(early_y)]
        last = tie(last, sent)
        sum_far = pre(last[0], self.core(last[1]))
        sum_own = pre(own[0], other_own)
        fillers = iter(filler())
        far = [self.along_x(narrow(sum_far[0])), self.along_y(narrow(sum_far[1]))]
        far = tie(far, next(fillers))
        near = [
            self.along_y(narrow(added(sum_y[0], far[0]))),
            self.along_x(narrow(added(sum_x[1], far[1]))),
        ]
        near = tie(near, next(fillers))
        return jnp.concatenate(
            [added(sum_own[k], sent[k]) + near[k].astype(wide) for k in range(2)], axis=1
        ).astype(low)


def per_device(
    states,
    teacher,
    lengths,
    routes,
    gate_weights,
    w_qkv,
    w_out,
    norm_gains,
    qk_gains,
    w_gate_up,
    w_down,
):
    seq_count, slot_count, width = states.shape
    top_count = routes.shape[-1]
    ctx_size = lax.axis_size("ctx")
    tp_size = lax.axis_size("tp")
    shards = lax.axis_size(plane)
    ctx_index = lax.axis_index("ctx")
    tp_index = lax.axis_index("tp")
    plane_index = lax.axis_index(plane)
    tokens = seq_count * slot_count
    part = tokens // tp_size
    shard_experts = w_gate_up.shape[0]
    hidden_local = w_gate_up.shape[3]
    experts = shard_experts * shards
    capacity = 5 * tokens * top_count // (4 * experts)
    own_slots = jnp.arange(slot_count, dtype=jnp.int32)
    position = ctx_index * slot_count + own_slots
    tok_position = jnp.tile(position, seq_count)
    row_valid = (position[None, :] < lengths[:, None]).reshape(tokens).astype(wide)
    mirror = [(i, (i + 1) % ctx_size) for i in range(ctx_size)]

    gain_cols, head_cols = norm_gains.shape[1], qk_gains.shape[1]
    small = jnp.concatenate(
        [
            norm_gains.astype(wide).reshape(-1),
            qk_gains.astype(wide).reshape(-1),
            jnp.sum(lengths).astype(wide)[None],
        ]
    )
    places = Plane()
    small_all = places.gather_whole(small[None])
    gain_rows = small_all[:, : 2 * gain_cols].reshape(shards, 2, gain_cols)
    full_gains = jnp.swapaxes(gain_rows, 0, 1).reshape(2, shards * gain_cols)
    head_rows = small_all[:, 2 * gain_cols : 2 * (gain_cols + head_cols)]
    qk_float = jnp.swapaxes(head_rows.reshape(shards, 2, head_cols), 0, 1).reshape(
        2, shards * head_cols
    )
    valid_count = jnp.sum(small_all[:, -1]) / ctx_size
    gain_attn, gain_ffn = full_gains[0], full_gains[1]
    head_dim = qk_float.shape[1]
    heads_local = w_qkv.shape[2] // head_dim
    score_scale = head_dim ** (-0.5)

    tables = route_tables(
        routes.reshape(tokens, top_count), gate_weights.reshape(tokens, top_count), experts
    )
    table = lax.all_to_all(tables, plane, split_axis=0, concat_axis=0, tiled=True).reshape(
        shards, shard_experts, 2, tokens
    )
    rank = table[:, :, 0].astype(jnp.int32)
    offset = (jnp.arange(shard_experts, dtype=jnp.int32) * capacity)[None, :, None]
    place = jnp.swapaxes(jnp.where(rank >= 0, rank + offset, -1), 1, 2)
    w_up = w_gate_up.reshape(shard_experts, width, 2 * hidden_local)
    order = places.order()
    sort = lambda a: jnp.concatenate(
        [lax.dynamic_slice_in_dim(a, block, 1, 0) for block in order], axis=0
    )
    table, place = sort(table), sort(place)
    some = lambda a, begin, pieces: a[begin : begin + blocks_in(pieces)]

    def blocks_in(pieces):
        return sum(piece.shape[1] for piece in pieces) // width

    full_qkv = lax.all_gather(
        w_qkv.reshape(w_qkv.shape[0], -1), plane, axis=0, tiled=True
    )
    rows_out = tie(line_gather(w_out), full_qkv[:1])
    full_out = lax.all_gather(rows_out, plane, axis=1, tiled=True)
    flat_states = states.astype(wide).reshape(tokens, width)
    normed = rms_norm(flat_states, gain_attn).astype(low)
    projected = jnp.dot(normed, full_qkv, preferred_element_type=wide).reshape(
        tokens, 3, heads_local, head_dim
    )

    def prepare_query(projected_in, gain):
        return rotate(rms_norm(projected_in, gain), tok_position)

    queries, query_back = jax.vjp(prepare_query, projected[:, 0], qk_float[0])
    key_states, key_back = jax.vjp(prepare_query, projected[:, 1], qk_float[1])
    query_low = queries.astype(low).reshape(seq_count, slot_count, heads_local, head_dim)
    by_head = lambda a: a.astype(low).reshape(seq_count, slot_count, heads_local, head_dim)
    value_low, key_low = by_head(projected[:, 2]), by_head(key_states)
    other_value = lax.ppermute(value_low, "ctx", mirror)
    other_key = lax.ppermute(key_low, "ctx", mirror)
    gathered_value = jnp.concatenate([value_low, other_value], axis=1)
    gathered_key = jnp.concatenate([key_low, other_key], axis=1)
    other_position = (1 - ctx_index) * slot_count + own_slots
    key_position = jnp.concatenate([position, other_position])
    key_valid = key_position[None, :] < lengths[:, None]
    pieces = [
        attend_sequence(
            query_low[i], gathered_key[i], gathered_value[i], key_valid[i], score_scale
        )
        for i in range(seq_count)
    ]
    attended_low = (
        jnp.stack([p[0] for p in pieces]).astype(low).reshape(tokens, heads_local * head_dim)
    )
    begin = tp_index * part
    own = lambda a: lax.dynamic_slice_in_dim(a, begin, part, 0)
    attended_low, table, place = lax.optimization_barrier((attended_low, table, place))
    attended_own = lax.all_to_all(
        attended_low, "tp", split_axis=0, concat_axis=1, tiled=True
    )
    states_own = own(flat_states)
    middle_own = states_own + jnp.dot(attended_own, full_out, preferred_element_type=wide)
    normed_own = rms_norm(middle_own, gain_ffn).astype(low)

    middle_col = width // 2
    cols = (slice(0, middle_col), slice(middle_col, width))

    def spread(*halves):
        return [lax.all_gather(half.astype(low), "tp", axis=0, tiled=True) for half in halves]

    saved = [()]

    def forward(begin, pieces):
        made, saved[0] = expert_call(
            begin, pieces, some(table, begin, pieces), some(place, begin, pieces), *near_weights,
            None, saved[0], capacity, shards,
        )
        return made

    def finish(half):
        return lax.psum_scatter(half, "tp", scatter_dimension=0, tiled=True).astype(wide)

    teacher_own = own(teacher.reshape(tokens, width)).astype(wide)
    valid_own = own(row_valid)
    grad_scale = (2.0 * loss_scale / valid_count * valid_own)[:, None]
    second_own = normed_own[:, cols[1]]
    first_block, second_block = spread(normed_own[:, cols[0]], second_own)
    second_block, w_up = lax.optimization_barrier((second_block, w_up))
    near_weights = on_chip(w_up, w_down)
    mixture = places.experts(
        first_block,
        second_block,
        forward,
        lambda: ((), ()),
    )
    rows_in, gate_up, hidden = saved[0]
    final_own = middle_own + finish(mixture)
    difference = final_own - teacher_own
    local_loss = jnp.sum(valid_own * jnp.sum(difference * difference, axis=-1))
    grad_final = grad_scale * difference
    spread_halves = spread(grad_final[:, cols[0]], grad_final[:, cols[1]])
    activations = lax.all_gather(final_own.astype(low), "tp", axis=0, tiled=True).reshape(
        seq_count, slot_count, width
    )

    saved[0] = ()

    def backward(begin, pieces):
        made, saved[0] = expert_call(
            begin, pieces, some(table, begin, pieces), some(place, begin, pieces), *back_weights,
            gate_up, saved[0], capacity, shards,
        )
        return made

    def weight_grads():
        rows_back, grad_rows = saved[0]
        made.append(
            jnp.einsum("ebcf,ebcd->efd", hidden, rows_back, preferred_element_type=wide)
        )
        yield [made[0]]
        grad_up = jnp.einsum("ebcd,ebcf->edf", rows_in, grad_rows, preferred_element_type=wide)
        made.append(grad_up)
        yield [grad_up, activations]

    made = []
    first_block, second_block = spread_halves
    second_block, w_up = lax.optimization_barrier((second_block, w_up))
    back_weights = on_chip(w_up, w_down)
    total_in = places.experts(first_block, second_block, backward, weight_grads)
    if not made:
        for _ in weight_grads():
            pass
    grad_down, grad_up = made
    grad_gate_up = with_layout_constraint(
        grad_up.reshape(shard_experts, width, 2, hidden_local),
        Layout(major_to_minor=(0, 1, 2, 3)),
    )
    grad_ffn = tie(finish(total_in), grad_gate_up, grad_down)

    grad_middle_norm, grad_gain_ffn = norm_back(grad_ffn, middle_own, gain_ffn)
    grad_middle = grad_final + grad_middle_norm
    grad_branch = grad_middle.astype(low)

    grad_attended = lax.all_to_all(
        nt_dot(grad_branch, full_out).astype(low), "tp", split_axis=1, concat_axis=0, tiled=True
    )
    grad_heads = grad_attended.reshape(seq_count, slot_count, heads_local, head_dim)
    backs = [
        back_sequence(
            query_low[i],
            gathered_key[i],
            gathered_value[i],
            key_valid[i],
            pieces[i][1],
            grad_heads[i],
            score_scale,
        )
        for i in range(seq_count)
    ]
    grad_query, grad_key, grad_value = [jnp.stack(parts) for parts in zip(*backs, strict=True)]

    def returned(grad):
        coming = lax.ppermute(grad[:, slot_count:].astype(low), "ctx", mirror)
        return added(grad[:, :slot_count], coming).reshape(tokens, heads_local, head_dim)

    branch_block = lax.all_gather(grad_branch, "tp", axis=0, tiled=True)
    grad_v, own_key = returned(grad_value), returned(grad_key)
    grad_v, branch_block = lax.optimization_barrier((grad_v, branch_block))
    grad_w_out = jnp.einsum("nd,nf->df", branch_block, attended_low, preferred_element_type=wide)
    grad_q, grad_q_gain = query_back(grad_query.reshape(tokens, heads_local, head_dim))
    grad_k, grad_k_gain = key_back(own_key)
    flat = lambda a: a.astype(low).reshape(tokens, -1)
    grad_proj_low = jnp.concatenate([flat(grad_q), flat(grad_k), flat(grad_v)], axis=1)
    grad_qk = jnp.stack([grad_q_gain, grad_k_gain])
    grad_normed = lax.psum_scatter(
        nt_dot(grad_proj_low, full_qkv).astype(low),
        "tp",
        scatter_dimension=0,
        tiled=True,
    ).astype(wide)
    grad_w_qkv = jnp.einsum("nd,nk->dk", normed, grad_proj_low, preferred_element_type=wide)
    grad_states_norm, grad_gain_attn = norm_back(grad_normed, states_own, gain_attn)
    grad_states = (
        lax.all_gather((grad_middle + grad_states_norm).astype(low), "tp", axis=0, tiled=True)
        .astype(wide)
        .reshape(seq_count, slot_count, width)
    )
    sums = sum_everywhere(
        jnp.concatenate([grad_gain_attn, grad_gain_ffn, grad_qk.reshape(-1), local_loss[None]])
    )
    out_gains = lax.dynamic_slice_in_dim(
        sums[: 2 * width].reshape(2, width), plane_index * gain_cols, gain_cols, 1
    )
    out_qk = lax.dynamic_slice_in_dim(
        sums[2 * width : 2 * (width + head_dim)].reshape(2, head_dim),
        plane_index * head_cols,
        head_cols,
        1,
    )
    loss_value = sums[-1] / valid_count
    weights_own = places.reduce_whole(
        jnp.concatenate([grad_w_qkv.astype(low), grad_w_out.astype(low)], axis=1)
    )
    qkv_cols = grad_w_qkv.shape[1]
    out_qkv = weights_own[:, :qkv_cols].reshape(w_qkv.shape)
    out_w_out = weights_own[:, qkv_cols:].T
    return (
        activations,
        loss_value,
        valid_count,
        grad_states,
        out_qkv,
        out_w_out,
        out_gains,
        out_qk,
        grad_gate_up,
        grad_down,
    )


def solution(mesh):
    placed = (
        P("fsdp", "ctx", None),
        P("fsdp", "ctx", None),
        P("fsdp"),
        P("fsdp", "ctx", None),
        P("fsdp", "ctx", None),
        P(("fsdp", "ctx"), None, "tp"),
        P("tp", ("fsdp", "ctx")),
        P(None, ("fsdp", "ctx")),
        P(None, ("fsdp", "ctx")),
        P(("fsdp", "ctx"), None, None, "tp"),
        P(("fsdp", "ctx"), "tp", None),
    )
    return jax.shard_map(
        per_device,
        mesh=mesh,
        in_specs=placed,
        out_specs=(
            P("fsdp", "ctx", None),
            P(),
            P(),
            P("fsdp", "ctx", None),
            P(("fsdp", "ctx"), None, "tp"),
            P("tp", ("fsdp", "ctx")),
            P(None, ("fsdp", "ctx")),
            P(None, ("fsdp", "ctx")),
            P(("fsdp", "ctx"), None, None, "tp"),
            P(("fsdp", "ctx"), "tp", None),
        ),
        check_vma=False,
    )
```

```python
import functools

import jax
import jax.numpy as jnp
from jax import lax
from jax.experimental.layout import Layout, with_layout_constraint
from jax.experimental import pallas as pl
from jax.experimental.pallas import tpu as pltpu
from jax.sharding import PartitionSpec as P

norm_eps = 1e-05
rope_base = 10000.0
loss_scale = 4096.0
masked_score = -1e30
plane = ("fsdp", "ctx")
everywhere = ("fsdp", "ctx", "tp")
low = jnp.bfloat16
wide = jnp.float32


def rms_norm(values, gain_vec):
    return (
        values * lax.rsqrt(jnp.mean(values * values, axis=-1, keepdims=True) + norm_eps) * gain_vec
    )


def norm_back(grad_normed, values, gain_vec):
    inverse = lax.rsqrt(jnp.mean(values * values, axis=-1, keepdims=True) + norm_eps)
    scaled = values * inverse
    grad_scaled = grad_normed * gain_vec
    grad_values = inverse * (
        grad_scaled - scaled * jnp.mean(grad_scaled * scaled, axis=-1, keepdims=True)
    )
    return (grad_values, jnp.sum(grad_normed * scaled, axis=0))


def rotate(values, position):
    half_dim = values.shape[-1] // 2
    frequency = rope_base ** (-2.0 * jnp.arange(half_dim, dtype=wide) / values.shape[-1])
    angles = position.astype(wide)[:, None] * frequency[None, :]
    cosine = jnp.cos(angles)[:, None, :]
    sine_part = jnp.sin(angles)[:, None, :]
    first_half = values[..., :half_dim]
    second_half = values[..., half_dim:]
    return jnp.concatenate(
        [
            first_half * cosine - second_half * sine_part,
            second_half * cosine + first_half * sine_part,
        ],
        axis=-1,
    )


def prepare(projected, qk_float, position):
    queries = rotate(rms_norm(projected[:, 0], qk_float[0]), position)
    key_states = rotate(rms_norm(projected[:, 1], qk_float[1]), position)
    return (queries, key_states, projected[:, 2])


def attend_sequence(query_seq, key_seq, value_seq, valid_seq, score_scale):
    scores = (
        jnp.einsum("qhd,khd->hqk", query_seq, key_seq, preferred_element_type=wide)
        * score_scale
    )
    scores = jnp.where(valid_seq[None, None, :], scores, masked_score)
    peak_score = jnp.max(scores, axis=-1, keepdims=True)
    exponent = jnp.exp(scores - peak_score)
    row_total = jnp.sum(exponent, axis=-1, keepdims=True)
    probability = (exponent / row_total).astype(low)
    output = jnp.einsum("hqk,khd->qhd", probability, value_seq, preferred_element_type=wide)
    return (output, (peak_score + jnp.log(row_total))[..., 0])


def back_sequence(query_seq, key_seq, value_seq, valid_seq, log_seq, grad_seq, score_scale):
    scores = (
        jnp.einsum("qhd,khd->hqk", query_seq, key_seq, preferred_element_type=wide)
        * score_scale
    )
    scores = jnp.where(valid_seq[None, None, :], scores, masked_score)
    probability = jnp.exp(scores - log_seq[..., None])
    grad_prob = jnp.einsum("qhd,khd->hqk", grad_seq, value_seq, preferred_element_type=wide)
    grad_scores = (
        probability * (grad_prob - jnp.sum(probability * grad_prob, axis=-1, keepdims=True))
    ).astype(low)
    grad_query = (
        jnp.einsum("hqk,khd->qhd", grad_scores, key_seq, preferred_element_type=wide)
        * score_scale
    )
    grad_key = (
        jnp.einsum("hqk,qhd->khd", grad_scores, query_seq, preferred_element_type=wide)
        * score_scale
    )
    grad_value = jnp.einsum(
        "hqk,qhd->khd", probability.astype(low), grad_seq, preferred_element_type=wide
    )
    return (grad_query, grad_key, grad_value)


def route_tables(route_rows, gate_rows, experts):
    slots = route_rows.shape[0]
    hit = route_rows[None, :, :] == jnp.arange(experts, dtype=jnp.int32)[:, None, None]
    named = jnp.sum(hit.astype(wide), axis=-1)
    gates = jnp.sum(jnp.where(hit, gate_rows[None, :, :], 0.0), axis=-1)
    order = jnp.arange(slots, dtype=jnp.int32)
    before = (order[:, None] < order[None, :]).astype(low)
    rank = jnp.dot(named.astype(low), before, preferred_element_type=wide)
    return jnp.stack([jnp.where(named > 0.0, rank, -1.0), gates], axis=1)


def pick_rows(table_ref, block, capacity, slots):
    rank = table_ref[block, 0, 0:1, :].astype(jnp.int32)
    gate = table_ref[block, 0, 1:2, :]
    match = lax.broadcasted_iota(jnp.int32, (capacity, slots), 0) == rank
    chosen = jnp.where(match, 1.0, 0.0).astype(low)
    weight = jnp.sum(jnp.where(match, gate, 0.0), axis=1, keepdims=True)
    return (chosen, weight)


def spread_rows(place_ref, block, experts, capacity, slots):
    column = lax.broadcasted_iota(jnp.int32, (slots, experts * capacity), 1)
    match = column == place_ref[block, :, 0:1]
    for expert in range(1, experts):
        match = match | (column == place_ref[block, :, expert : expert + 1])
    return jnp.where(match, 1.0, 0.0).astype(low)


def nt_dot(left, right):
    return lax.dot_general(left, right, (((1,), (1,)), ((), ())), preferred_element_type=wide)


def tiles_of(width, most=512):
    step = min(width, most)
    return [slice(begin, begin + step) for begin in range(0, width, step)]


def take_rows(x_refs, table_ref, rows_ref):
    blocks, capacity, width = rows_ref.shape[1:]
    slots = table_ref.shape[3]
    weights, place = [], 0
    for block in range(blocks):
        chosen, weight = pick_rows(table_ref, block, capacity, slots)
        weights.append(weight)
        done = 0
        while done < width:
            x_ref = x_refs[place]
            for cut in tiles_of(x_ref.shape[1]):
                rows_ref[0, block, :, done + cut.start : done + cut.stop] = jnp.dot(
                    chosen, x_ref[:, cut], preferred_element_type=wide
                ).astype(low)
            done, place = done + x_ref.shape[1], place + 1
    return (rows_ref[0].reshape(blocks * capacity, width), jnp.concatenate(weights, axis=0))


def fill_spread(place_ref, spread_ref, capacity):
    blocks, slots, total = spread_ref.shape
    for block in range(blocks):
        spread_ref[block] = spread_rows(place_ref, block, total // capacity, capacity, slots)


def combine_blocks(spread_ref, y_ref, out_refs):
    for block, out_ref in enumerate(out_refs):
        for cut in tiles_of(y_ref.shape[2]):
            out_ref[:, cut] = jnp.dot(
                spread_ref[block], y_ref[block, :, cut], preferred_element_type=wide
            ).astype(low)


def forward_body(n_x, n_out, n_keep, *refs):
    x_refs, refs = refs[:n_x], refs[n_x:]
    (table_ref, place_ref, up_ref, down_ref), refs = refs[:4], refs[4 + n_keep :]
    out_refs, (rows_ref, gate_up_ref, hidden_ref, y_ref, spread_ref) = refs[:n_out], refs[n_out:]
    expert = pl.program_id(0)
    blocks, capacity, width = rows_ref.shape[1:]
    experts = y_ref.shape[1] // capacity

    @pl.when(expert == 0)
    def _():
        fill_spread(place_ref, spread_ref, capacity)

    half = down_ref.shape[1]
    rows, weight = take_rows(x_refs, table_ref, rows_ref)
    gate_up = jnp.dot(rows, up_ref[expert], preferred_element_type=wide)
    gate_up_ref[0] = gate_up.astype(low).reshape(blocks, capacity, 2 * half)
    gate_part = gate_up[:, :half]
    up_part = gate_up[:, half:]
    hidden = (gate_part * jax.nn.sigmoid(gate_part) * up_part * weight).astype(low)
    hidden_ref[0] = hidden.reshape(blocks, capacity, half)
    begin = pl.multiple_of(expert * capacity, 16)
    for cut in tiles_of(width):
        y_ref[:, pl.ds(begin, capacity), cut] = (
            jnp.dot(hidden, down_ref[expert, :, cut], preferred_element_type=wide)
            .astype(low)
            .reshape(blocks, capacity, -1)
        )

    @pl.when(expert == experts - 1)
    def _():
        combine_blocks(spread_ref, y_ref, out_refs)


def backward_body(n_x, n_out, n_keep, *refs):
    x_refs, refs = refs[:n_x], refs[n_x:]
    (table_ref, place_ref, up_ref, down_ref, gate_up_ref), refs = refs[:5], refs[5 + n_keep :]
    out_refs, (rows_ref, grad_ref, y_ref, spread_ref) = refs[:n_out], refs[n_out:]
    expert = pl.program_id(0)
    blocks, capacity, width = rows_ref.shape[1:]
    experts = y_ref.shape[1] // capacity

    @pl.when(expert == 0)
    def _():
        fill_spread(place_ref, spread_ref, capacity)

    half = down_ref.shape[1]
    rows, weight = take_rows(x_refs, table_ref, rows_ref)
    grad_hidden = nt_dot(rows, down_ref[expert]) * weight
    gate_up = gate_up_ref[0].astype(wide).reshape(blocks * capacity, 2 * half)
    gate_part = gate_up[:, :half]
    up_part = gate_up[:, half:]
    sigmoid = jax.nn.sigmoid(gate_part)
    grad_gate = grad_hidden * up_part * sigmoid * (1.0 + gate_part * (1.0 - sigmoid))
    grad_up = grad_hidden * gate_part * sigmoid
    grad_rows = jnp.concatenate([grad_gate, grad_up], axis=1).astype(low)
    grad_ref[0] = grad_rows.reshape(blocks, capacity, 2 * half)
    begin = pl.multiple_of(expert * capacity, 16)
    for cut in tiles_of(width):
        y_ref[:, pl.ds(begin, capacity), cut] = (
            nt_dot(grad_rows, up_ref[expert, cut, :]).astype(low).reshape(blocks, capacity, -1)
        )

    @pl.when(expert == experts - 1)
    def _():
        combine_blocks(spread_ref, y_ref, out_refs)


def expert_call(begin, pieces, table, place, w_up, w_down, gate_up, kept, capacity, total):
    blocks, experts, _, slots = table.shape
    width = w_up.shape[1]
    double, half = w_up.shape[2], w_down.shape[1]
    backward = gate_up is not None
    once = pl.Buffered(1)
    row_spec = lambda last: pl.BlockSpec(
        (1, blocks, capacity, last), lambda e: (e, begin // blocks, 0, 0)
    )
    row_shape = lambda last, kind: pltpu.HBM((experts, total, capacity, last), kind)
    whole = lambda shape: pl.BlockSpec(shape, lambda e: (0,) * len(shape), pipeline_mode=once)
    in_specs = [pl.BlockSpec(memory_space=pltpu.VMEM)] * len(pieces) + [
        pl.BlockSpec((blocks, 1, 2, slots), lambda e: (0, e, 0, 0)),
        whole((blocks, slots, experts)),
        pl.BlockSpec(memory_space=pltpu.VMEM),
        pl.BlockSpec(memory_space=pltpu.VMEM),
    ]
    held = [pltpu.with_memory_space_constraint(p, pltpu.VMEM) for p in pieces]
    operands = [*held, table, place, w_up, w_down]
    n_out = blocks
    out_specs = [pl.BlockSpec(memory_space=pltpu.VMEM)] * n_out + [row_spec(width), row_spec(double)]
    out_shape = [pltpu.VMEM((slots, width), low)] * n_out + [row_shape(width, low)]
    if backward:
        in_specs.append(row_spec(double))
        operands.append(pltpu.with_memory_space_constraint(gate_up, pltpu.HBM))
        out_shape.append(row_shape(double, low))
    else:
        out_specs.append(row_spec(half))
        out_shape += [row_shape(double, low), row_shape(half, low)]
    aliases = {len(operands) + i: n_out + i for i in range(len(kept))}
    rows = experts * blocks * capacity
    body = functools.partial(
        backward_body if backward else forward_body, len(pieces), n_out, len(kept)
    )
    made = pl.pallas_call(
        body,
        grid=(experts,),
        in_specs=in_specs + [pl.BlockSpec(memory_space=pl.ANY)] * len(kept),
        out_specs=out_specs,
        out_shape=out_shape,
        input_output_aliases=aliases,
        scratch_shapes=[
            pltpu.VMEM((blocks, experts * capacity, width), low),
            pltpu.VMEM((blocks, slots, experts * capacity), low),
        ],
        compiler_params=pltpu.CompilerParams(
            dimension_semantics=("arbitrary",), vmem_limit_bytes=20 << 20
        ),
        cost_estimate=pl.CostEstimate(
            flops=2 * rows * width * (2 * slots + double + half),
            bytes_accessed=4 * blocks * slots * width + rows * (2 * width + 6 * double),
            transcendentals=rows * half,
        ),
    )(*operands, *kept)
    return (made[:n_out], made[n_out:])


def on_chip(*arrays):
    count = len(arrays)

    def body(*refs):
        sources, targets, sems = refs[:count], refs[count : 2 * count], refs[-1]
        copies = [
            pltpu.make_async_copy(sources[i], targets[i], sems.at[i]) for i in range(count)
        ]
        for copy in copies:
            copy.start()
        for copy in copies:
            copy.wait()

    return pl.pallas_call(
        body,
        in_specs=[pl.BlockSpec(memory_space=pltpu.HBM)] * count,
        out_specs=[pl.BlockSpec(memory_space=pltpu.VMEM)] * count,
        out_shape=[pltpu.VMEM(a.shape, a.dtype) for a in arrays],
        scratch_shapes=[pltpu.SemaphoreType.DMA((count,))],
        compiler_params=pltpu.CompilerParams(vmem_limit_bytes=24 << 20),
    )(*[pltpu.with_memory_space_constraint(a, pltpu.HBM) for a in arrays])


def added(left, right):
    return left.astype(wide) + right.astype(wide)


def tie(values, *anchors):
    return lax.optimization_barrier((values, anchors))[0]


def sum_everywhere(values):
    values = values[None]
    for axis in everywhere:
        size, step = lax.axis_size(axis), 1
        while step < size:
            pairs = [(i, i ^ step) for i in range(size)]
            values = values + lax.ppermute(values, axis, pairs)
            step *= 2
    return values[0]


def line_gather(shard):
    size = lax.axis_size("tp")
    if size > 4:
        return lax.all_gather(shard, "tp", axis=0, tiled=True)
    move = lambda d: lax.ppermute(
        shard, "tp", [(i, i + d) for i in range(size) if 0 <= i + d < size]
    )
    near = [move(d) for d in range(size - 1, 0, -1)] + [shard] + [move(-d) for d in range(1, size)]
    rows = shard.shape[0]
    begin = (size - 1 - lax.axis_index("tp")) * rows
    return lax.dynamic_slice_in_dim(jnp.concatenate(near, axis=0), begin, size * rows, 0)


class Plane:
    def __init__(self):
        self.fsdp, self.ctx = lax.axis_size("fsdp"), lax.axis_size("ctx")
        self.tree = self.fsdp == 4 and self.ctx == 2
        self.shards = self.fsdp * self.ctx

    def core(self, a):
        return lax.ppermute(a, "fsdp", [(i, i ^ 1) for i in range(self.fsdp)])

    def along_x(self, a):
        return lax.ppermute(a, "fsdp", [(i, i ^ 2) for i in range(self.fsdp)])

    def along_y(self, a):
        return lax.ppermute(a, "ctx", [(i, i ^ 1) for i in range(self.ctx)])

    def order(self):
        if not self.tree:
            return list(range(self.shards))
        fsdp, ctx = lax.axis_index("fsdp"), lax.axis_index("ctx")
        chips = ((0, 0), (1, 0), (0, 1), (1, 1))
        return [(fsdp ^ (2 * x) ^ core) * 2 + (ctx ^ y) for x, y in chips for core in (0, 1)]

    def gather_whole(self, shard):
        rows = shard.shape[0]
        if not self.tree:
            return lax.all_gather(shard, plane, axis=0, tiled=True)
        halves = (shard[: rows // 2], shard[rows // 2 :]) if rows > 1 else (shard,)
        x = [self.along_x(h) for h in halves]
        y = [self.along_y(h) for h in halves]
        far = [self.along_y(x[0])] + [self.along_x(h) for h in y[1:]]
        whole = jnp.zeros((self.shards * rows, *shard.shape[1:]), shard.dtype)
        order = self.order()
        for c, pieces in enumerate((halves, x, y, far)):
            for core in (0, 1):
                begin = order[2 * c + core] * rows
                for piece in pieces:
                    found = self.core(piece) if core else piece
                    whole = lax.dynamic_update_slice_in_dim(whole, found, begin, 0)
                    begin = begin + piece.shape[0]
        return whole

    def reduce_whole(self, partial):
        rows = partial.shape[0] // self.shards
        if not self.tree:
            return lax.psum_scatter(partial, plane, scatter_dimension=0, tiled=True).astype(wide)
        blocks = [lax.dynamic_slice_in_dim(partial, i * rows, rows, 0) for i in self.order()]
        pre = [added(blocks[2 * c], self.core(blocks[2 * c + 1])) for c in range(4)]
        cuts = tiles_of(partial.shape[1], partial.shape[1] // 2)
        return jnp.concatenate(
            [self.total(k, *[p[:, cut] for p in pre]) for k, cut in enumerate(cuts)], axis=1
        )

    def total(self, k, own, near_x, near_y, far):
        if k % 2 == 0:
            near_y = near_y + self.along_x(far.astype(low)).astype(wide)
        else:
            near_x = near_x + self.along_y(far.astype(low)).astype(wide)
        from_x, from_y = self.along_x(near_x.astype(low)), self.along_y(near_y.astype(low))
        return own + from_x.astype(wide) + from_y.astype(wide)

    def experts(self, first, second, call, filler):
        if not self.tree:
            split = lambda a: jnp.split(lax.all_gather(a, plane, axis=0, tiled=True), self.shards)
            halves, made = list(zip(split(first), split(second), strict=True)), []
            for i in range(0, self.shards, 2):
                made += call(i, [*halves[i], *halves[i + 1]])
            return lax.psum_scatter(
                jnp.concatenate(made, axis=0), plane, scatter_dimension=0, tiled=True
            )
        step = first.shape[1]
        pre = lambda made, other: [
            added(made[:, k * step : (k + 1) * step], other[:, k * step : (k + 1) * step])
            for k in range(2)
        ]
        narrow = lambda a: a.astype(low)
        x_first, y_first = self.along_x(first), self.along_y(first)
        second = tie(second, x_first, y_first)
        own_pieces = [first, second, self.core(first), self.core(second)]
        x_second, y_second = self.along_x(second), self.along_y(second)
        over_x, over_y = self.core(x_first), self.core(y_first)
        own = call(0, tie(own_pieces, over_x, over_y))
        x_second, y_second = tie((x_second, y_second), own[0])
        far = [self.along_y(x_first), self.along_x(y_second)]
        over_y = [over_y, self.core(y_second)]
        near_x = call(2, [x_first, x_second, over_x, self.core(x_second)])
        near_x = tie(near_x, over_y)
        other_own, other_x = self.core(own[1]), self.core(near_x[1])
        far += [self.core(piece) for piece in far]
        near_y = tie(call(4, [y_first, y_second, *over_y]), other_own, other_x, far)
        other_y = self.core(near_y[1])
        sum_x, sum_y = pre(near_x[0], other_x), pre(near_y[0], other_y)
        early_x, early_y = narrow(sum_x[0]), narrow(sum_y[1])
        last = call(6, tie(far, early_x, early_y))
        sent = [self.along_x(early_x), self.along_y(early_y)]
        last = tie(last, sent)
        sum_far = pre(last[0], self.core(last[1]))
        sum_own = pre(own[0], other_own)
        fillers = iter(filler())
        far = [self.along_x(narrow(sum_far[0])), self.along_y(narrow(sum_far[1]))]
        far = tie(far, next(fillers))
        near = [
            self.along_y(narrow(added(sum_y[0], far[0]))),
            self.along_x(narrow(added(sum_x[1], far[1]))),
        ]
        near = tie(near, next(fillers))
        return jnp.concatenate(
            [added(sum_own[k], sent[k]) + near[k].astype(wide) for k in range(2)], axis=1
        ).astype(low)


def per_device(
    states,
    teacher,
    lengths,
    routes,
    gate_weights,
    w_qkv,
    w_out,
    norm_gains,
    qk_gains,
    w_gate_up,
    w_down,
):
    seq_count, slot_count, width = states.shape
    top_count = routes.shape[-1]
    ctx_size = lax.axis_size("ctx")
    tp_size = lax.axis_size("tp")
    shards = lax.axis_size(plane)
    ctx_index = lax.axis_index("ctx")
    tp_index = lax.axis_index("tp")
    plane_index = lax.axis_index(plane)
    tokens = seq_count * slot_count
    part = tokens // tp_size
    shard_experts = w_gate_up.shape[0]
    hidden_local = w_gate_up.shape[3]
    experts = shard_experts * shards
    capacity = 5 * tokens * top_count // (4 * experts)
    own_slots = jnp.arange(slot_count, dtype=jnp.int32)
    position = ctx_index * slot_count + own_slots
    tok_position = jnp.tile(position, seq_count)
    row_valid = (position[None, :] < lengths[:, None]).reshape(tokens).astype(wide)
    mirror = [(i, (i + 1) % ctx_size) for i in range(ctx_size)]

    gain_cols, head_cols = norm_gains.shape[1], qk_gains.shape[1]
    small = jnp.concatenate(
        [
            norm_gains.astype(wide).reshape(-1),
            qk_gains.astype(wide).reshape(-1),
            jnp.sum(lengths).astype(wide)[None],
        ]
    )
    places = Plane()
    small_all = places.gather_whole(small[None])
    gain_rows = small_all[:, : 2 * gain_cols].reshape(shards, 2, gain_cols)
    full_gains = jnp.swapaxes(gain_rows, 0, 1).reshape(2, shards * gain_cols)
    head_rows = small_all[:, 2 * gain_cols : 2 * (gain_cols + head_cols)]
    qk_float = jnp.swapaxes(head_rows.reshape(shards, 2, head_cols), 0, 1).reshape(
        2, shards * head_cols
    )
    valid_count = jnp.sum(small_all[:, -1]) / ctx_size
    gain_attn, gain_ffn = full_gains[0], full_gains[1]
    head_dim = qk_float.shape[1]
    heads_local = w_qkv.shape[2] // head_dim
    score_scale = head_dim ** (-0.5)

    tables = route_tables(
        routes.reshape(tokens, top_count), gate_weights.reshape(tokens, top_count), experts
    )
    table = lax.all_to_all(tables, plane, split_axis=0, concat_axis=0, tiled=True).reshape(
        shards, shard_experts, 2, tokens
    )
    rank = table[:, :, 0].astype(jnp.int32)
    offset = (jnp.arange(shard_experts, dtype=jnp.int32) * capacity)[None, :, None]
    place = jnp.swapaxes(jnp.where(rank >= 0, rank + offset, -1), 1, 2)
    w_up = w_gate_up.reshape(shard_experts, width, 2 * hidden_local)
    order = places.order()
    sort = lambda a: jnp.concatenate(
        [lax.dynamic_slice_in_dim(a, block, 1, 0) for block in order], axis=0
    )
    table, place = sort(table), sort(place)
    some = lambda a, begin, pieces: a[begin : begin + blocks_in(pieces)]

    def blocks_in(pieces):
        return sum(piece.shape[1] for piece in pieces) // width

    full_qkv = lax.all_gather(
        w_qkv.reshape(w_qkv.shape[0], -1), plane, axis=0, tiled=True
    )
    rows_out = tie(line_gather(w_out), full_qkv[:1])
    full_out = lax.all_gather(rows_out, plane, axis=1, tiled=True)
    flat_states = states.astype(wide).reshape(tokens, width)
    normed = rms_norm(flat_states, gain_attn).astype(low)
    projected = jnp.dot(normed, full_qkv, preferred_element_type=wide).reshape(
        tokens, 3, heads_local, head_dim
    )

    def prepare_query(projected_in, gain):
        return rotate(rms_norm(projected_in, gain), tok_position)

    queries, query_back = jax.vjp(prepare_query, projected[:, 0], qk_float[0])
    key_states, key_back = jax.vjp(prepare_query, projected[:, 1], qk_float[1])
    query_low = queries.astype(low).reshape(seq_count, slot_count, heads_local, head_dim)
    by_head = lambda a: a.astype(low).reshape(seq_count, slot_count, heads_local, head_dim)
    value_low, key_low = by_head(projected[:, 2]), by_head(key_states)
    other_value = lax.ppermute(value_low, "ctx", mirror)
    other_key = lax.ppermute(key_low, "ctx", mirror)
    gathered_value = jnp.concatenate([value_low, other_value], axis=1)
    gathered_key = jnp.concatenate([key_low, other_key], axis=1)
    other_position = (1 - ctx_index) * slot_count + own_slots
    key_position = jnp.concatenate([position, other_position])
    key_valid = key_position[None, :] < lengths[:, None]
    pieces = [
        attend_sequence(
            query_low[i], gathered_key[i], gathered_value[i], key_valid[i], score_scale
        )
        for i in range(seq_count)
    ]
    attended_low = (
        jnp.stack([p[0] for p in pieces]).astype(low).reshape(tokens, heads_local * head_dim)
    )
    begin = tp_index * part
    own = lambda a: lax.dynamic_slice_in_dim(a, begin, part, 0)
    attended_low, table, place = lax.optimization_barrier((attended_low, table, place))
    attended_own = lax.all_to_all(
        attended_low, "tp", split_axis=0, concat_axis=1, tiled=True
    )
    states_own = own(flat_states)
    middle_own = states_own + jnp.dot(attended_own, full_out, preferred_element_type=wide)
    normed_own = rms_norm(middle_own, gain_ffn).astype(low)

    middle_col = width // 2
    cols = (slice(0, middle_col), slice(middle_col, width))

    def spread(*halves):
        return [lax.all_gather(half.astype(low), "tp", axis=0, tiled=True) for half in halves]

    saved = [()]

    def forward(begin, pieces):
        made, saved[0] = expert_call(
            begin, pieces, some(table, begin, pieces), some(place, begin, pieces), *near_weights,
            None, saved[0], capacity, shards,
        )
        return made

    def finish(half):
        return lax.psum_scatter(half, "tp", scatter_dimension=0, tiled=True).astype(wide)

    teacher_own = own(teacher.reshape(tokens, width)).astype(wide)
    valid_own = own(row_valid)
    grad_scale = (2.0 * loss_scale / valid_count * valid_own)[:, None]
    second_own = normed_own[:, cols[1]]
    first_block, second_block = spread(normed_own[:, cols[0]], second_own)
    second_block, w_up = lax.optimization_barrier((second_block, w_up))
    near_weights = on_chip(w_up, w_down)
    mixture = places.experts(
        first_block,
        second_block,
        forward,
        lambda: ((), ()),
    )
    rows_in, gate_up, hidden = saved[0]
    final_own = middle_own + finish(mixture)
    difference = final_own - teacher_own
    local_loss = jnp.sum(valid_own * jnp.sum(difference * difference, axis=-1))
    grad_final = grad_scale * difference
    spread_halves = spread(grad_final[:, cols[0]], grad_final[:, cols[1]])
    activations = lax.all_gather(final_own.astype(low), "tp", axis=0, tiled=True).reshape(
        seq_count, slot_count, width
    )

    saved[0] = ()

    def backward(begin, pieces):
        made, saved[0] = expert_call(
            begin, pieces, some(table, begin, pieces), some(place, begin, pieces), *back_weights,
            gate_up, saved[0], capacity, shards,
        )
        return made

    def weight_grads():
        rows_back, grad_rows = saved[0]
        made.append(
            jnp.einsum("ebcf,ebcd->efd", hidden, rows_back, preferred_element_type=wide)
        )
        yield [made[0]]
        grad_up = jnp.einsum("ebcd,ebcf->edf", rows_in, grad_rows, preferred_element_type=wide)
        made.append(grad_up)
        yield [grad_up, activations]

    made = []
    first_block, second_block = spread_halves
    second_block, w_up = lax.optimization_barrier((second_block, w_up))
    back_weights = on_chip(w_up, w_down)
    total_in = places.experts(first_block, second_block, backward, weight_grads)
    if not made:
        for _ in weight_grads():
            pass
    grad_down, grad_up = made
    grad_gate_up = with_layout_constraint(
        grad_up.reshape(shard_experts, width, 2, hidden_local),
        Layout(major_to_minor=(0, 1, 2, 3)),
    )
    grad_ffn = tie(finish(total_in), grad_gate_up, grad_down)

    grad_middle_norm, grad_gain_ffn = norm_back(grad_ffn, middle_own, gain_ffn)
    grad_middle = grad_final + grad_middle_norm
    grad_branch = grad_middle.astype(low)

    grad_attended = lax.all_to_all(
        nt_dot(grad_branch, full_out).astype(low), "tp", split_axis=1, concat_axis=0, tiled=True
    )
    grad_heads = grad_attended.reshape(seq_count, slot_count, heads_local, head_dim)
    backs = [
        back_sequence(
            query_low[i],
            gathered_key[i],
            gathered_value[i],
            key_valid[i],
            pieces[i][1],
            grad_heads[i],
            score_scale,
        )
        for i in range(seq_count)
    ]
    grad_query, grad_key, grad_value = [jnp.stack(parts) for parts in zip(*backs, strict=True)]

    def returned(grad):
        coming = lax.ppermute(grad[:, slot_count:].astype(low), "ctx", mirror)
        return added(grad[:, :slot_count], coming).reshape(tokens, heads_local, head_dim)

    branch_block = lax.all_gather(grad_branch, "tp", axis=0, tiled=True)
    grad_v, own_key = returned(grad_value), returned(grad_key)
    grad_v, branch_block = lax.optimization_barrier((grad_v, branch_block))
    grad_w_out = jnp.einsum("nd,nf->df", branch_block, attended_low, preferred_element_type=wide)
    grad_q, grad_q_gain = query_back(grad_query.reshape(tokens, heads_local, head_dim))
    grad_k, grad_k_gain = key_back(own_key)
    flat = lambda a: a.astype(low).reshape(tokens, -1)
    grad_proj_low = jnp.concatenate([flat(grad_q), flat(grad_k), flat(grad_v)], axis=1)
    grad_qk = jnp.stack([grad_q_gain, grad_k_gain])
    grad_normed = lax.psum_scatter(
        nt_dot(grad_proj_low, full_qkv).astype(low),
        "tp",
        scatter_dimension=0,
        tiled=True,
    ).astype(wide)
    grad_w_qkv = jnp.einsum("nd,nk->dk", normed, grad_proj_low, preferred_element_type=wide)
    grad_states_norm, grad_gain_attn = norm_back(grad_normed, states_own, gain_attn)
    grad_states = (
        lax.all_gather((grad_middle + grad_states_norm).astype(low), "tp", axis=0, tiled=True)
        .astype(wide)
        .reshape(seq_count, slot_count, width)
    )
    sums = sum_everywhere(
        jnp.concatenate([grad_gain_attn, grad_gain_ffn, grad_qk.reshape(-1), local_loss[None]])
    )
    out_gains = lax.dynamic_slice_in_dim(
        sums[: 2 * width].reshape(2, width), plane_index * gain_cols, gain_cols, 1
    )
    out_qk = lax.dynamic_slice_in_dim(
        sums[2 * width : 2 * (width + head_dim)].reshape(2, head_dim),
        plane_index * head_cols,
        head_cols,
        1,
    )
    loss_value = sums[-1] / valid_count
    weights_own = places.reduce_whole(
        jnp.concatenate([grad_w_qkv.astype(low), grad_w_out.astype(low)], axis=1)
    )
    qkv_cols = grad_w_qkv.shape[1]
    out_qkv = weights_own[:, :qkv_cols].reshape(w_qkv.shape)
    out_w_out = weights_own[:, qkv_cols:].T
    return (
        activations,
        loss_value,
        valid_count,
        grad_states,
        out_qkv,
        out_w_out,
        out_gains,
        out_qk,
        grad_gate_up,
        grad_down,
    )


def solution(mesh):
    placed = (
        P("fsdp", "ctx", None),
        P("fsdp", "ctx", None),
        P("fsdp"),
        P("fsdp", "ctx", None),
        P("fsdp", "ctx", None),
        P(("fsdp", "ctx"), None, "tp"),
        P("tp", ("fsdp", "ctx")),
        P(None, ("fsdp", "ctx")),
        P(None, ("fsdp", "ctx")),
        P(("fsdp", "ctx"), None, None, "tp"),
        P(("fsdp", "ctx"), "tp", None),
    )
    return jax.shard_map(
        per_device,
        mesh=mesh,
        in_specs=placed,
        out_specs=(
            P("fsdp", "ctx", None),
            P(),
            P(),
            P("fsdp", "ctx", None),
            P(("fsdp", "ctx"), None, "tp"),
            P("tp", ("fsdp", "ctx")),
            P(None, ("fsdp", "ctx")),
            P(None, ("fsdp", "ctx")),
            P(("fsdp", "ctx"), None, None, "tp"),
            P(("fsdp", "ctx"), "tp", None),
        ),
        check_vma=False,
    )
```

```python
import functools

import jax
import jax.numpy as jnp
from jax import lax
from jax.experimental.layout import Layout, with_layout_constraint
from jax.experimental import pallas as pl
from jax.experimental.pallas import tpu as pltpu
from jax.sharding import PartitionSpec as P

norm_eps = 1e-05
rope_base = 10000.0
loss_scale = 4096.0
masked_score = -1e30
plane = ("fsdp", "ctx")
everywhere = ("fsdp", "ctx", "tp")
low = jnp.bfloat16
wide = jnp.float32


def rms_norm(values, gain_vec):
    return (
        values * lax.rsqrt(jnp.mean(values * values, axis=-1, keepdims=True) + norm_eps) * gain_vec
    )


def norm_back(grad_normed, values, gain_vec):
    inverse = lax.rsqrt(jnp.mean(values * values, axis=-1, keepdims=True) + norm_eps)
    scaled = values * inverse
    grad_scaled = grad_normed * gain_vec
    grad_values = inverse * (
        grad_scaled - scaled * jnp.mean(grad_scaled * scaled, axis=-1, keepdims=True)
    )
    return (grad_values, jnp.sum(grad_normed * scaled, axis=0))


def rotate(values, position):
    half_dim = values.shape[-1] // 2
    frequency = rope_base ** (-2.0 * jnp.arange(half_dim, dtype=wide) / values.shape[-1])
    angles = position.astype(wide)[:, None] * frequency[None, :]
    cosine = jnp.cos(angles)[:, None, :]
    sine_part = jnp.sin(angles)[:, None, :]
    first_half = values[..., :half_dim]
    second_half = values[..., half_dim:]
    return jnp.concatenate(
        [
            first_half * cosine - second_half * sine_part,
            second_half * cosine + first_half * sine_part,
        ],
        axis=-1,
    )


def prepare(projected, qk_float, position):
    queries = rotate(rms_norm(projected[:, 0], qk_float[0]), position)
    key_states = rotate(rms_norm(projected[:, 1], qk_float[1]), position)
    return (queries, key_states, projected[:, 2])


def attend_sequence(query_seq, key_seq, value_seq, valid_seq, score_scale):
    scores = (
        jnp.einsum("qhd,khd->hqk", query_seq, key_seq, preferred_element_type=wide)
        * score_scale
    )
    scores = jnp.where(valid_seq[None, None, :], scores, masked_score)
    peak_score = jnp.max(scores, axis=-1, keepdims=True)
    exponent = jnp.exp(scores - peak_score)
    row_total = jnp.sum(exponent, axis=-1, keepdims=True)
    probability = (exponent / row_total).astype(low)
    output = jnp.einsum("hqk,khd->qhd", probability, value_seq, preferred_element_type=wide)
    return (output, (peak_score + jnp.log(row_total))[..., 0])


def back_sequence(query_seq, key_seq, value_seq, valid_seq, log_seq, grad_seq, score_scale):
    scores = (
        jnp.einsum("qhd,khd->hqk", query_seq, key_seq, preferred_element_type=wide)
        * score_scale
    )
    scores = jnp.where(valid_seq[None, None, :], scores, masked_score)
    probability = jnp.exp(scores - log_seq[..., None])
    grad_prob = jnp.einsum("qhd,khd->hqk", grad_seq, value_seq, preferred_element_type=wide)
    grad_scores = (
        probability * (grad_prob - jnp.sum(probability * grad_prob, axis=-1, keepdims=True))
    ).astype(low)
    grad_query = (
        jnp.einsum("hqk,khd->qhd", grad_scores, key_seq, preferred_element_type=wide)
        * score_scale
    )
    grad_key = (
        jnp.einsum("hqk,qhd->khd", grad_scores, query_seq, preferred_element_type=wide)
        * score_scale
    )
    grad_value = jnp.einsum(
        "hqk,qhd->khd", probability.astype(low), grad_seq, preferred_element_type=wide
    )
    return (grad_query, grad_key, grad_value)


def route_tables(route_rows, gate_rows, experts):
    slots = route_rows.shape[0]
    hit = route_rows[None, :, :] == jnp.arange(experts, dtype=jnp.int32)[:, None, None]
    named = jnp.sum(hit.astype(wide), axis=-1)
    gates = jnp.sum(jnp.where(hit, gate_rows[None, :, :], 0.0), axis=-1)
    order = jnp.arange(slots, dtype=jnp.int32)
    before = (order[:, None] < order[None, :]).astype(low)
    rank = jnp.dot(named.astype(low), before, preferred_element_type=wide)
    return jnp.stack([jnp.where(named > 0.0, rank, -1.0), gates], axis=1)


def pick_rows(table_ref, block, capacity, slots):
    rank = table_ref[block, 0, 0:1, :].astype(jnp.int32)
    gate = table_ref[block, 0, 1:2, :]
    match = lax.broadcasted_iota(jnp.int32, (capacity, slots), 0) == rank
    chosen = jnp.where(match, 1.0, 0.0).astype(low)
    weight = jnp.sum(jnp.where(match, gate, 0.0), axis=1, keepdims=True)
    return (chosen, weight)


def spread_rows(place_ref, block, experts, capacity, slots):
    column = lax.broadcasted_iota(jnp.int32, (slots, experts * capacity), 1)
    match = column == place_ref[block, :, 0:1]
    for expert in range(1, experts):
        match = match | (column == place_ref[block, :, expert : expert + 1])
    return jnp.where(match, 1.0, 0.0).astype(low)


def nt_dot(left, right):
    return lax.dot_general(left, right, (((1,), (1,)), ((), ())), preferred_element_type=wide)


def tiles_of(width, most=512):
    step = min(width, most)
    return [slice(begin, begin + step) for begin in range(0, width, step)]


def take_rows(x_refs, table_ref, rows_ref):
    blocks, capacity, width = rows_ref.shape[1:]
    slots = table_ref.shape[3]
    weights, place = [], 0
    for block in range(blocks):
        chosen, weight = pick_rows(table_ref, block, capacity, slots)
        weights.append(weight)
        done = 0
        while done < width:
            x_ref = x_refs[place]
            for cut in tiles_of(x_ref.shape[1]):
                rows_ref[0, block, :, done + cut.start : done + cut.stop] = jnp.dot(
                    chosen, x_ref[:, cut], preferred_element_type=wide
                ).astype(low)
            done, place = done + x_ref.shape[1], place + 1
    return (rows_ref[0].reshape(blocks * capacity, width), jnp.concatenate(weights, axis=0))


def fill_spread(place_ref, spread_ref, capacity):
    blocks, slots, total = spread_ref.shape
    for block in range(blocks):
        spread_ref[block] = spread_rows(place_ref, block, total // capacity, capacity, slots)


def combine_blocks(spread_ref, y_ref, out_refs):
    for block, out_ref in enumerate(out_refs):
        for cut in tiles_of(y_ref.shape[2]):
            out_ref[:, cut] = jnp.dot(
                spread_ref[block], y_ref[block, :, cut], preferred_element_type=wide
            ).astype(low)


def forward_body(n_x, n_out, n_keep, *refs):
    x_refs, refs = refs[:n_x], refs[n_x:]
    (table_ref, place_ref, up_ref, down_ref), refs = refs[:4], refs[4 + n_keep :]
    out_refs, (rows_ref, gate_up_ref, hidden_ref, y_ref, spread_ref) = refs[:n_out], refs[n_out:]
    expert = pl.program_id(0)
    blocks, capacity, width = rows_ref.shape[1:]
    experts = y_ref.shape[1] // capacity

    @pl.when(expert == 0)
    def _():
        fill_spread(place_ref, spread_ref, capacity)

    half = down_ref.shape[1]
    rows, weight = take_rows(x_refs, table_ref, rows_ref)
    gate_up = jnp.dot(rows, up_ref[expert], preferred_element_type=wide)
    gate_up_ref[0] = gate_up.astype(low).reshape(blocks, capacity, 2 * half)
    gate_part = gate_up[:, :half]
    up_part = gate_up[:, half:]
    hidden = (gate_part * jax.nn.sigmoid(gate_part) * up_part * weight).astype(low)
    hidden_ref[0] = hidden.reshape(blocks, capacity, half)
    begin = pl.multiple_of(expert * capacity, 16)
    for cut in tiles_of(width):
        y_ref[:, pl.ds(begin, capacity), cut] = (
            jnp.dot(hidden, down_ref[expert, :, cut], preferred_element_type=wide)
            .astype(low)
            .reshape(blocks, capacity, -1)
        )

    @pl.when(expert == experts - 1)
    def _():
        combine_blocks(spread_ref, y_ref, out_refs)


def backward_body(n_x, n_out, n_keep, *refs):
    x_refs, refs = refs[:n_x], refs[n_x:]
    (table_ref, place_ref, up_ref, down_ref, gate_up_ref), refs = refs[:5], refs[5 + n_keep :]
    out_refs, (rows_ref, grad_ref, y_ref, spread_ref) = refs[:n_out], refs[n_out:]
    expert = pl.program_id(0)
    blocks, capacity, width = rows_ref.shape[1:]
    experts = y_ref.shape[1] // capacity

    @pl.when(expert == 0)
    def _():
        fill_spread(place_ref, spread_ref, capacity)

    half = down_ref.shape[1]
    rows, weight = take_rows(x_refs, table_ref, rows_ref)
    grad_hidden = nt_dot(rows, down_ref[expert]) * weight
    gate_up = gate_up_ref[0].astype(wide).reshape(blocks * capacity, 2 * half)
    gate_part = gate_up[:, :half]
    up_part = gate_up[:, half:]
    sigmoid = jax.nn.sigmoid(gate_part)
    grad_gate = grad_hidden * up_part * sigmoid * (1.0 + gate_part * (1.0 - sigmoid))
    grad_up = grad_hidden * gate_part * sigmoid
    grad_rows = jnp.concatenate([grad_gate, grad_up], axis=1).astype(low)
    grad_ref[0] = grad_rows.reshape(blocks, capacity, 2 * half)
    begin = pl.multiple_of(expert * capacity, 16)
    for cut in tiles_of(width):
        y_ref[:, pl.ds(begin, capacity), cut] = (
            nt_dot(grad_rows, up_ref[expert, cut, :]).astype(low).reshape(blocks, capacity, -1)
        )

    @pl.when(expert == experts - 1)
    def _():
        combine_blocks(spread_ref, y_ref, out_refs)


def expert_call(begin, pieces, table, place, w_up, w_down, gate_up, kept, capacity, total):
    blocks, experts, _, slots = table.shape
    width = w_up.shape[1]
    double, half = w_up.shape[2], w_down.shape[1]
    backward = gate_up is not None
    once = pl.Buffered(1)
    row_spec = lambda last: pl.BlockSpec(
        (1, blocks, capacity, last), lambda e: (e, begin // blocks, 0, 0)
    )
    row_shape = lambda last, kind: pltpu.HBM((experts, total, capacity, last), kind)
    whole = lambda shape: pl.BlockSpec(shape, lambda e: (0,) * len(shape), pipeline_mode=once)
    in_specs = [pl.BlockSpec(memory_space=pltpu.VMEM)] * len(pieces) + [
        pl.BlockSpec((blocks, 1, 2, slots), lambda e: (0, e, 0, 0)),
        whole((blocks, slots, experts)),
        pl.BlockSpec(memory_space=pltpu.VMEM),
        pl.BlockSpec(memory_space=pltpu.VMEM),
    ]
    held = [pltpu.with_memory_space_constraint(p, pltpu.VMEM) for p in pieces]
    operands = [*held, table, place, w_up, w_down]
    n_out = blocks
    out_specs = [pl.BlockSpec(memory_space=pltpu.VMEM)] * n_out + [row_spec(width), row_spec(double)]
    out_shape = [pltpu.VMEM((slots, width), low)] * n_out + [row_shape(width, low)]
    if backward:
        in_specs.append(row_spec(double))
        operands.append(pltpu.with_memory_space_constraint(gate_up, pltpu.HBM))
        out_shape.append(row_shape(double, low))
    else:
        out_specs.append(row_spec(half))
        out_shape += [row_shape(double, low), row_shape(half, low)]
    aliases = {len(operands) + i: n_out + i for i in range(len(kept))}
    rows = experts * blocks * capacity
    body = functools.partial(
        backward_body if backward else forward_body, len(pieces), n_out, len(kept)
    )
    made = pl.pallas_call(
        body,
        grid=(experts,),
        in_specs=in_specs + [pl.BlockSpec(memory_space=pl.ANY)] * len(kept),
        out_specs=out_specs,
        out_shape=out_shape,
        input_output_aliases=aliases,
        scratch_shapes=[
            pltpu.VMEM((blocks, experts * capacity, width), low),
            pltpu.VMEM((blocks, slots, experts * capacity), low),
        ],
        compiler_params=pltpu.CompilerParams(
            dimension_semantics=("arbitrary",), vmem_limit_bytes=20 << 20
        ),
        cost_estimate=pl.CostEstimate(
            flops=2 * rows * width * (2 * slots + double + half),
            bytes_accessed=4 * blocks * slots * width + rows * (2 * width + 6 * double),
            transcendentals=rows * half,
        ),
    )(*operands, *kept)
    return (made[:n_out], made[n_out:])


def on_chip(*arrays):
    count = len(arrays)

    def body(*refs):
        sources, targets, sems = refs[:count], refs[count : 2 * count], refs[-1]
        copies = [
            pltpu.make_async_copy(sources[i], targets[i], sems.at[i]) for i in range(count)
        ]
        for copy in copies:
            copy.start()
        for copy in copies:
            copy.wait()

    return pl.pallas_call(
        body,
        in_specs=[pl.BlockSpec(memory_space=pltpu.HBM)] * count,
        out_specs=[pl.BlockSpec(memory_space=pltpu.VMEM)] * count,
        out_shape=[pltpu.VMEM(a.shape, a.dtype) for a in arrays],
        scratch_shapes=[pltpu.SemaphoreType.DMA((count,))],
        compiler_params=pltpu.CompilerParams(vmem_limit_bytes=24 << 20),
    )(*[pltpu.with_memory_space_constraint(a, pltpu.HBM) for a in arrays])


def added(left, right):
    return left.astype(wide) + right.astype(wide)


def tie(values, *anchors):
    return lax.optimization_barrier((values, anchors))[0]


def sum_everywhere(values):
    values = values[None]
    for axis in everywhere:
        size, step = lax.axis_size(axis), 1
        while step < size:
            pairs = [(i, i ^ step) for i in range(size)]
            values = values + lax.ppermute(values, axis, pairs)
            step *= 2
    return values[0]


def line_gather(shard):
    size = lax.axis_size("tp")
    if size > 4:
        return lax.all_gather(shard, "tp", axis=0, tiled=True)
    move = lambda d: lax.ppermute(
        shard, "tp", [(i, i + d) for i in range(size) if 0 <= i + d < size]
    )
    near = [move(d) for d in range(size - 1, 0, -1)] + [shard] + [move(-d) for d in range(1, size)]
    rows = shard.shape[0]
    begin = (size - 1 - lax.axis_index("tp")) * rows
    return lax.dynamic_slice_in_dim(jnp.concatenate(near, axis=0), begin, size * rows, 0)


class Plane:
    def __init__(self):
        self.fsdp, self.ctx = lax.axis_size("fsdp"), lax.axis_size("ctx")
        self.tree = self.fsdp == 4 and self.ctx == 2
        self.shards = self.fsdp * self.ctx

    def core(self, a):
        return lax.ppermute(a, "fsdp", [(i, i ^ 1) for i in range(self.fsdp)])

    def along_x(self, a):
        return lax.ppermute(a, "fsdp", [(i, i ^ 2) for i in range(self.fsdp)])

    def along_y(self, a):
        return lax.ppermute(a, "ctx", [(i, i ^ 1) for i in range(self.ctx)])

    def order(self):
        if not self.tree:
            return list(range(self.shards))
        fsdp, ctx = lax.axis_index("fsdp"), lax.axis_index("ctx")
        chips = ((0, 0), (1, 0), (0, 1), (1, 1))
        return [(fsdp ^ (2 * x) ^ core) * 2 + (ctx ^ y) for x, y in chips for core in (0, 1)]

    def gather_whole(self, shard):
        rows = shard.shape[0]
        if not self.tree:
            return lax.all_gather(shard, plane, axis=0, tiled=True)
        halves = (shard[: rows // 2], shard[rows // 2 :]) if rows > 1 else (shard,)
        x = [self.along_x(h) for h in halves]
        y = [self.along_y(h) for h in halves]
        far = [self.along_y(x[0])] + [self.along_x(h) for h in y[1:]]
        whole = jnp.zeros((self.shards * rows, *shard.shape[1:]), shard.dtype)
        order = self.order()
        for c, pieces in enumerate((halves, x, y, far)):
            for core in (0, 1):
                begin = order[2 * c + core] * rows
                for piece in pieces:
                    found = self.core(piece) if core else piece
                    whole = lax.dynamic_update_slice_in_dim(whole, found, begin, 0)
                    begin = begin + piece.shape[0]
        return whole

    def reduce_whole(self, partial):
        rows = partial.shape[0] // self.shards
        if not self.tree:
            return lax.psum_scatter(partial, plane, scatter_dimension=0, tiled=True).astype(wide)
        blocks = [lax.dynamic_slice_in_dim(partial, i * rows, rows, 0) for i in self.order()]
        pre = [added(blocks[2 * c], self.core(blocks[2 * c + 1])) for c in range(4)]
        cuts = tiles_of(partial.shape[1], partial.shape[1] // 2)
        return jnp.concatenate(
            [self.total(k, *[p[:, cut] for p in pre]) for k, cut in enumerate(cuts)], axis=1
        )

    def total(self, k, own, near_x, near_y, far):
        if k % 2 == 0:
            near_y = near_y + self.along_x(far.astype(low)).astype(wide)
        else:
            near_x = near_x + self.along_y(far.astype(low)).astype(wide)
        from_x, from_y = self.along_x(near_x.astype(low)), self.along_y(near_y.astype(low))
        return own + from_x.astype(wide) + from_y.astype(wide)

    def experts(self, first, second, call, filler):
        if not self.tree:
            split = lambda a: jnp.split(lax.all_gather(a, plane, axis=0, tiled=True), self.shards)
            halves, made = list(zip(split(first), split(second), strict=True)), []
            for i in range(0, self.shards, 2):
                made += call(i, [*halves[i], *halves[i + 1]])
            return lax.psum_scatter(
                jnp.concatenate(made, axis=0), plane, scatter_dimension=0, tiled=True
            )
        step = first.shape[1]
        pre = lambda made, other: [
            added(made[:, k * step : (k + 1) * step], other[:, k * step : (k + 1) * step])
            for k in range(2)
        ]
        narrow = lambda a: a.astype(low)
        x_first, y_first = self.along_x(first), self.along_y(first)
        second = tie(second, x_first, y_first)
        own_pieces = [first, second, self.core(first), self.core(second)]
        x_second, y_second = self.along_x(second), self.along_y(second)
        over_x, over_y = self.core(x_first), self.core(y_first)
        own = call(0, tie(own_pieces, over_x, over_y))
        x_second, y_second = tie((x_second, y_second), own[0])
        far = [self.along_y(x_first), self.along_x(y_second)]
        over_y = [over_y, self.core(y_second)]
        near_x = call(2, [x_first, x_second, over_x, self.core(x_second)])
        near_x = tie(near_x, over_y)
        other_own, other_x = self.core(own[1]), self.core(near_x[1])
        far += [self.core(piece) for piece in far]
        near_y = tie(call(4, [y_first, y_second, *over_y]), other_own, other_x, far)
        other_y = self.core(near_y[1])
        sum_x, sum_y = pre(near_x[0], other_x), pre(near_y[0], other_y)
        early_x, early_y = narrow(sum_x[0]), narrow(sum_y[1])
        last = call(6, tie(far, early_x, early_y))
        sent = [self.along_x(early_x), self.along_y(early_y)]
        last = tie(last, sent)
        sum_far = pre(last[0], self.core(last[1]))
        sum_own = pre(own[0], other_own)
        fillers = iter(filler())
        far = [self.along_x(narrow(sum_far[0])), self.along_y(narrow(sum_far[1]))]
        far = tie(far, next(fillers))
        near = [
            self.along_y(narrow(added(sum_y[0], far[0]))),
            self.along_x(narrow(added(sum_x[1], far[1]))),
        ]
        near = tie(near, next(fillers))
        return jnp.concatenate(
            [added(sum_own[k], sent[k]) + near[k].astype(wide) for k in range(2)], axis=1
        ).astype(low)


def per_device(
    states,
    teacher,
    lengths,
    routes,
    gate_weights,
    w_qkv,
    w_out,
    norm_gains,
    qk_gains,
    w_gate_up,
    w_down,
):
    seq_count, slot_count, width = states.shape
    top_count = routes.shape[-1]
    ctx_size = lax.axis_size("ctx")
    tp_size = lax.axis_size("tp")
    shards = lax.axis_size(plane)
    ctx_index = lax.axis_index("ctx")
    tp_index = lax.axis_index("tp")
    plane_index = lax.axis_index(plane)
    tokens = seq_count * slot_count
    part = tokens // tp_size
    shard_experts = w_gate_up.shape[0]
    hidden_local = w_gate_up.shape[3]
    experts = shard_experts * shards
    capacity = 5 * tokens * top_count // (4 * experts)
    own_slots = jnp.arange(slot_count, dtype=jnp.int32)
    position = ctx_index * slot_count + own_slots
    tok_position = jnp.tile(position, seq_count)
    row_valid = (position[None, :] < lengths[:, None]).reshape(tokens).astype(wide)
    mirror = [(i, (i + 1) % ctx_size) for i in range(ctx_size)]

    gain_cols, head_cols = norm_gains.shape[1], qk_gains.shape[1]
    small = jnp.concatenate(
        [
            norm_gains.astype(wide).reshape(-1),
            qk_gains.astype(wide).reshape(-1),
            jnp.sum(lengths).astype(wide)[None],
        ]
    )
    places = Plane()
    small_all = places.gather_whole(small[None])
    gain_rows = small_all[:, : 2 * gain_cols].reshape(shards, 2, gain_cols)
    full_gains = jnp.swapaxes(gain_rows, 0, 1).reshape(2, shards * gain_cols)
    head_rows = small_all[:, 2 * gain_cols : 2 * (gain_cols + head_cols)]
    qk_float = jnp.swapaxes(head_rows.reshape(shards, 2, head_cols), 0, 1).reshape(
        2, shards * head_cols
    )
    valid_count = jnp.sum(small_all[:, -1]) / ctx_size
    gain_attn, gain_ffn = full_gains[0], full_gains[1]
    head_dim = qk_float.shape[1]
    heads_local = w_qkv.shape[2] // head_dim
    score_scale = head_dim ** (-0.5)

    tables = route_tables(
        routes.reshape(tokens, top_count), gate_weights.reshape(tokens, top_count), experts
    )
    table = lax.all_to_all(tables, plane, split_axis=0, concat_axis=0, tiled=True).reshape(
        shards, shard_experts, 2, tokens
    )
    rank = table[:, :, 0].astype(jnp.int32)
    offset = (jnp.arange(shard_experts, dtype=jnp.int32) * capacity)[None, :, None]
    place = jnp.swapaxes(jnp.where(rank >= 0, rank + offset, -1), 1, 2)
    w_up = w_gate_up.reshape(shard_experts, width, 2 * hidden_local)
    order = places.order()
    sort = lambda a: jnp.concatenate(
        [lax.dynamic_slice_in_dim(a, block, 1, 0) for block in order], axis=0
    )
    table, place = sort(table), sort(place)
    some = lambda a, begin, pieces: a[begin : begin + blocks_in(pieces)]

    def blocks_in(pieces):
        return sum(piece.shape[1] for piece in pieces) // width

    full_qkv = lax.all_gather(
        w_qkv.reshape(w_qkv.shape[0], -1), plane, axis=0, tiled=True
    )
    rows_out = tie(line_gather(w_out), full_qkv[:1])
    full_out = lax.all_gather(rows_out, plane, axis=1, tiled=True)
    flat_states = states.astype(wide).reshape(tokens, width)
    normed = rms_norm(flat_states, gain_attn).astype(low)
    projected = jnp.dot(normed, full_qkv, preferred_element_type=wide).reshape(
        tokens, 3, heads_local, head_dim
    )

    def prepare_query(projected_in, gain):
        return rotate(rms_norm(projected_in, gain), tok_position)

    queries, query_back = jax.vjp(prepare_query, projected[:, 0], qk_float[0])
    key_states, key_back = jax.vjp(prepare_query, projected[:, 1], qk_float[1])
    query_low = queries.astype(low).reshape(seq_count, slot_count, heads_local, head_dim)
    by_head = lambda a: a.astype(low).reshape(seq_count, slot_count, heads_local, head_dim)
    value_low, key_low = by_head(projected[:, 2]), by_head(key_states)
    other_value = lax.ppermute(value_low, "ctx", mirror)
    other_key = lax.ppermute(key_low, "ctx", mirror)
    gathered_value = jnp.concatenate([value_low, other_value], axis=1)
    gathered_key = jnp.concatenate([key_low, other_key], axis=1)
    other_position = (1 - ctx_index) * slot_count + own_slots
    key_position = jnp.concatenate([position, other_position])
    key_valid = key_position[None, :] < lengths[:, None]
    pieces = [
        attend_sequence(
            query_low[i], gathered_key[i], gathered_value[i], key_valid[i], score_scale
        )
        for i in range(seq_count)
    ]
    attended_low = (
        jnp.stack([p[0] for p in pieces]).astype(low).reshape(tokens, heads_local * head_dim)
    )
    begin = tp_index * part
    own = lambda a: lax.dynamic_slice_in_dim(a, begin, part, 0)
    attended_low, table, place = lax.optimization_barrier((attended_low, table, place))
    attended_own = lax.all_to_all(
        attended_low, "tp", split_axis=0, concat_axis=1, tiled=True
    )
    states_own = own(flat_states)
    middle_own = states_own + jnp.dot(attended_own, full_out, preferred_element_type=wide)
    normed_own = rms_norm(middle_own, gain_ffn).astype(low)

    middle_col = width // 2
    cols = (slice(0, middle_col), slice(middle_col, width))

    def spread(*halves):
        return [lax.all_gather(half.astype(low), "tp", axis=0, tiled=True) for half in halves]

    saved = [()]

    def forward(begin, pieces):
        made, saved[0] = expert_call(
            begin, pieces, some(table, begin, pieces), some(place, begin, pieces), *near_weights,
            None, saved[0], capacity, shards,
        )
        return made

    def finish(half):
        return lax.psum_scatter(half, "tp", scatter_dimension=0, tiled=True).astype(wide)

    teacher_own = own(teacher.reshape(tokens, width)).astype(wide)
    valid_own = own(row_valid)
    grad_scale = (2.0 * loss_scale / valid_count * valid_own)[:, None]
    second_own = normed_own[:, cols[1]]
    first_block, second_block = spread(normed_own[:, cols[0]], second_own)
    second_block, w_up = lax.optimization_barrier((second_block, w_up))
    near_weights = on_chip(w_up, w_down)
    mixture = places.experts(
        first_block,
        second_block,
        forward,
        lambda: ((), ()),
    )
    rows_in, gate_up, hidden = saved[0]
    final_own = middle_own + finish(mixture)
    difference = final_own - teacher_own
    local_loss = jnp.sum(valid_own * jnp.sum(difference * difference, axis=-1))
    grad_final = grad_scale * difference
    spread_halves = spread(grad_final[:, cols[0]], grad_final[:, cols[1]])
    activations = lax.all_gather(final_own.astype(low), "tp", axis=0, tiled=True).reshape(
        seq_count, slot_count, width
    )

    saved[0] = ()

    def backward(begin, pieces):
        made, saved[0] = expert_call(
            begin, pieces, some(table, begin, pieces), some(place, begin, pieces), *back_weights,
            gate_up, saved[0], capacity, shards,
        )
        return made

    def weight_grads():
        rows_back, grad_rows = saved[0]
        grad_up = jnp.einsum("ebcd,ebcf->edf", rows_in, grad_rows, preferred_element_type=wide)
        made.append(grad_up)
        yield [grad_up]
        made.append(
            jnp.einsum("ebcf,ebcd->efd", hidden, rows_back, preferred_element_type=wide)
        )
        yield [made[1], activations]

    made = []
    first_block, second_block = spread_halves
    second_block, w_up = lax.optimization_barrier((second_block, w_up))
    back_weights = on_chip(w_up, w_down)
    total_in = places.experts(first_block, second_block, backward, weight_grads)
    if not made:
        for _ in weight_grads():
            pass
    grad_up, grad_down = made
    grad_gate_up = with_layout_constraint(
        grad_up.reshape(shard_experts, width, 2, hidden_local),
        Layout(major_to_minor=(0, 1, 2, 3)),
    )
    grad_ffn = tie(finish(total_in), grad_gate_up, grad_down)

    grad_middle_norm, grad_gain_ffn = norm_back(grad_ffn, middle_own, gain_ffn)
    grad_middle = grad_final + grad_middle_norm
    grad_branch = grad_middle.astype(low)

    grad_attended = lax.all_to_all(
        nt_dot(grad_branch, full_out).astype(low), "tp", split_axis=1, concat_axis=0, tiled=True
    )
    grad_heads = grad_attended.reshape(seq_count, slot_count, heads_local, head_dim)
    backs = [
        back_sequence(
            query_low[i],
            gathered_key[i],
            gathered_value[i],
            key_valid[i],
            pieces[i][1],
            grad_heads[i],
            score_scale,
        )
        for i in range(seq_count)
    ]
    grad_query, grad_key, grad_value = [jnp.stack(parts) for parts in zip(*backs, strict=True)]

    def returned(grad):
        coming = lax.ppermute(grad[:, slot_count:].astype(low), "ctx", mirror)
        return added(grad[:, :slot_count], coming).reshape(tokens, heads_local, head_dim)

    branch_block = lax.all_gather(grad_branch, "tp", axis=0, tiled=True)
    grad_v, own_key = returned(grad_value), returned(grad_key)
    grad_v, branch_block = lax.optimization_barrier((grad_v, branch_block))
    grad_w_out = jnp.einsum("nd,nf->df", branch_block, attended_low, preferred_element_type=wide)
    grad_q, grad_q_gain = query_back(grad_query.reshape(tokens, heads_local, head_dim))
    grad_k, grad_k_gain = key_back(own_key)
    flat = lambda a: a.astype(low).reshape(tokens, -1)
    grad_proj_low = jnp.concatenate([flat(grad_q), flat(grad_k), flat(grad_v)], axis=1)
    grad_qk = jnp.stack([grad_q_gain, grad_k_gain])
    grad_normed = lax.psum_scatter(
        nt_dot(grad_proj_low, full_qkv).astype(low),
        "tp",
        scatter_dimension=0,
        tiled=True,
    ).astype(wide)
    grad_w_qkv = jnp.einsum("nd,nk->dk", normed, grad_proj_low, preferred_element_type=wide)
    grad_states_norm, grad_gain_attn = norm_back(grad_normed, states_own, gain_attn)
    grad_states = (
        lax.all_gather((grad_middle + grad_states_norm).astype(low), "tp", axis=0, tiled=True)
        .astype(wide)
        .reshape(seq_count, slot_count, width)
    )
    sums = sum_everywhere(
        jnp.concatenate([grad_gain_attn, grad_gain_ffn, grad_qk.reshape(-1), local_loss[None]])
    )
    out_gains = lax.dynamic_slice_in_dim(
        sums[: 2 * width].reshape(2, width), plane_index * gain_cols, gain_cols, 1
    )
    out_qk = lax.dynamic_slice_in_dim(
        sums[2 * width : 2 * (width + head_dim)].reshape(2, head_dim),
        plane_index * head_cols,
        head_cols,
        1,
    )
    loss_value = sums[-1] / valid_count
    weights_own = places.reduce_whole(
        jnp.concatenate([grad_w_qkv.astype(low), grad_w_out.astype(low)], axis=1)
    )
    qkv_cols = grad_w_qkv.shape[1]
    out_qkv = weights_own[:, :qkv_cols].reshape(w_qkv.shape)
    out_w_out = weights_own[:, qkv_cols:].T
    return (
        activations,
        loss_value,
        valid_count,
        grad_states,
        out_qkv,
        out_w_out,
        out_gains,
        out_qk,
        grad_gate_up,
        grad_down,
    )


def solution(mesh):
    placed = (
        P("fsdp", "ctx", None),
        P("fsdp", "ctx", None),
        P("fsdp"),
        P("fsdp", "ctx", None),
        P("fsdp", "ctx", None),
        P(("fsdp", "ctx"), None, "tp"),
        P("tp", ("fsdp", "ctx")),
        P(None, ("fsdp", "ctx")),
        P(None, ("fsdp", "ctx")),
        P(("fsdp", "ctx"), None, None, "tp"),
        P(("fsdp", "ctx"), "tp", None),
    )
    return jax.shard_map(
        per_device,
        mesh=mesh,
        in_specs=placed,
        out_specs=(
            P("fsdp", "ctx", None),
            P(),
            P(),
            P("fsdp", "ctx", None),
            P(("fsdp", "ctx"), None, "tp"),
            P("tp", ("fsdp", "ctx")),
            P(None, ("fsdp", "ctx")),
            P(None, ("fsdp", "ctx")),
            P(("fsdp", "ctx"), None, None, "tp"),
            P(("fsdp", "ctx"), "tp", None),
        ),
        check_vma=False,
    )
```
